32 devices in a mesh: wide: 16 (over z, y, x), narrow: 2 (over core).
Axes of the slice: x: 2, y: 2, z: 4, core: 2. Of those that a mesh axis runs over, the one named last changes fastest.
Arguments:
- patches: bfloat16 [192, 256, 768], P(('wide', 'narrow')), may hold values from -6 to 6
- timeloc: bfloat16 [192, 768], P(('wide', 'narrow')), may hold values from -6 to 6
- visible: int32 [192, 64], P(('wide', 'narrow')), may hold values from 0 to 255, as said below
- masked: int32 [192, 192], P(('wide', 'narrow')), may hold values from 0 to 255, as said below
- flags: int32 [192], P(('wide', 'narrow')), may hold values 0 or 1
- cotangent: bfloat16 [192, 256, 512], P(('wide', 'narrow')), may hold values from -6 to 6
- params: float32 [79104, 128], P('narrow')
- moment1: float32 [79104, 128], P('narrow'), may hold values from -1.5 to 1.5
- moment2: float32 [79104, 128], P('narrow'), may hold values from 0.01 to 10
Outputs:
- dec_out: bfloat16 [192, 256, 512], P(('wide', 'narrow'))
- patch_grad: bfloat16 [192, 256, 768], P(('wide', 'narrow'))
- grads: float32 [79104, 128], P('narrow')
- update: float32 [79104, 128], P('narrow')
- new_moment1: float32 [79104, 128], P('narrow')
- new_moment2: float32 [79104, 128], P('narrow')
The draws below stay inside these ranges and needn't reach their ends.
Inputs may be any that keep to these rules, and one draw needn't show every extreme that they name: For every chip, its 64 visible and 192 masked indices are distinct and together name each patch 0 to 255 once. `masked`: the complement of the same chip's visible indices.
All inputs are finite; a program needn't handle non-finite values. No bound on the sum of `flags` on one device may be relied on, other than what follows from the above.
Results may differ from the reference program's by a relative error of at most 0.018.
Values may be sent and summed in bfloat16 or wider, within the bound.
No kernel may reach another device: no remote copies, remote signals or barrier semaphores. Data moves between devices by JAX's collectives and lax.ppermute only.
A program may use at most 384 MiB of HBM per device.

```python
import math
import jax
import jax.numpy as jnp
from jax import lax

DE = 768
HE = 12
HD = 64
FE = 3072
DD = 512
HDEC = 4
FD = 2048
PATCH = 256
CHIPS_DEV = 6
VIS = 64
TE = 66
CHIPS = 192
PR = 79104


def segment_list_drawn():
    enc_inner = HE * HD
    dec_inner = HDEC * HD
    return [('enc_cls', (DE,)), ('enc_norm1_gain', (DE,)), ('enc_norm1_bias', (DE,)), ('enc_qkv', (DE, 3 * enc_inner)), ('enc_out', (enc_inner, DE)), ('enc_out_bias', (DE,)), ('enc_norm2_gain', (DE,)), ('enc_norm2_bias', (DE,)), ('enc_fc1', (DE, FE)), ('enc_fc1_bias', (FE,)), ('enc_fc2', (FE, DE)), ('enc_fc2_bias', (DE,)), ('enc_final_gain', (DE,)), ('enc_final_bias', (DE,)), ('proj', (DE, DD)), ('proj_bias', (DD,)), ('mask_token', (DD,)), ('dec_norm1_gain', (DD,)), ('dec_norm1_bias', (DD,)), ('dec_qkv', (DD, 3 * dec_inner)), ('dec_out', (dec_inner, DD)), ('dec_out_bias', (DD,)), ('dec_norm2_gain', (DD,)), ('dec_norm2_bias', (DD,)), ('dec_fc1', (DD, FD)), ('dec_fc1_bias', (FD,)), ('dec_fc2', (FD, DD)), ('dec_fc2_bias', (DD,))]


def segment_law(label):
    if label[-5:] == '_gain':
        return (0.1, 1.0)
    if label[-5:] == '_bias':
        return (0.2, 0.0)
    if label == 'enc_qkv' or label == 'enc_fc1' or label == 'proj':
        return (DE ** (-0.5), 0.0)
    if label == 'dec_qkv' or label == 'dec_fc1':
        return (DD ** (-0.5), 0.0)
    if label == 'enc_out':
        return (0.6 * math.sqrt(TE) / math.sqrt(HE * HD), 0.0)
    if label == 'dec_out':
        return (0.6 * math.sqrt(PATCH) / math.sqrt(HDEC * HD), 0.0)
    if label == 'enc_fc2':
        return (math.sqrt(2.0) / math.sqrt(FE), 0.0)
    if label == 'dec_fc2':
        return (math.sqrt(2.0) / math.sqrt(FD), 0.0)
    return (1.0, 0.0)


def draw_params(key, part):
    scale_parts = []
    center_parts = []
    filled = 0
    for label, dims_of in segment_list_drawn():
        length = math.prod(dims_of)
        scaling, center = segment_law(label)
        scale_parts.append(jnp.full((length,), scaling, jnp.float32))
        center_parts.append(jnp.full((length,), center, jnp.float32))
        filled = filled + length
    scale_parts.append(jnp.full((PR * 128 - filled,), 0.02, jnp.float32))
    center_parts.append(jnp.zeros((PR * 128 - filled,), jnp.float32))
    scaling_all = jnp.concatenate(scale_parts)
    center_all = jnp.concatenate(center_parts)
    noise = jax.random.normal(jax.random.fold_in(key, 3), (PR * 128,), jnp.float32)
    return (center_all + scaling_all * noise).reshape(PR, 128)


def choose_patches(key):
    chip_keys = jax.random.split(jax.random.fold_in(key, 11), CHIPS)
    return jax.vmap(lambda chip_key: jax.random.permutation(chip_key, PATCH))(chip_keys).astype(jnp.int32)


def draw_visible(key, part):
    return choose_patches(key)[:, :VIS]


def draw_masked(key, part):
    return choose_patches(key)[:, VIS:]


def plant(entries, stream_key, low, largest):
    longest = entries.shape.index(max(entries.shape))
    spots = []
    for shift in (0, 1):
        where = [jax.random.randint(jax.random.fold_in(stream_key, axis), (), 0, length) for axis, length in enumerate(entries.shape)]
        where[longest] = (where[longest] + shift) % entries.shape[longest]
        spots.append(tuple(where))
    return entries.at[spots[0]].set(low).at[spots[1]].set(largest)


def shard_levels(own_key, extent, cuts, smallest, high):
    def one(dim, parts):
        steps = jax.random.uniform(jax.random.fold_in(jax.random.fold_in(own_key, 6), dim), (parts,), jnp.float32, smallest / len(cuts), high / len(cuts))
        return jnp.repeat(jnp.exp(steps), extent[dim] // parts).reshape((-1,) + (1,) * (len(extent) - dim - 1))

    factor_of = one(*cuts[0])
    for cut in cuts[1:]:
        factor_of = factor_of * one(*cut)
    return factor_of


def normal_values(own_key, shape, scale, reach, cuts=(), kind=jnp.bfloat16):
    values = jax.random.normal(own_key, shape, jnp.float32) * scale
    if len(cuts) > 0:
        values = shard_levels(own_key, shape, cuts, -0.22, 0.18) * values
    return jnp.clip(values, min=-reach, max=reach).astype(kind)


def setup_inputs(seed: int = 0) -> dict:
    arg_keys = jax.random.split(jax.random.key(seed), 10)
    return {
        "patches": normal_values(arg_keys[0], (CHIPS, PATCH, DE), 1.0, 6.0, ((0, 32),)),
        "timeloc": normal_values(arg_keys[1], (CHIPS, DE), 1.0, 6.0, ((0, 32),)),
        "visible": draw_visible(jax.random.fold_in(arg_keys[9], 71), 0),
        "masked": draw_masked(jax.random.fold_in(arg_keys[9], 71), 0),
        "flags": plant((jax.random.randint(arg_keys[4], (CHIPS,), 0, 4) < 1).astype(jnp.int32), jax.random.fold_in(arg_keys[4], 1), 0, 1),
        "cotangent": normal_values(arg_keys[5], (CHIPS, PATCH, DD), 1.0, 6.0, ((0, 32),)),
        "params": draw_params(jax.random.fold_in(arg_keys[9], 71), 0),
        "moment1": normal_values(arg_keys[7], (PR, 128), 0.1, 1.5, ((0, 2),), jnp.float32),
        "moment2": jnp.clip(jnp.exp(math.log(10.0) - 6.9077553 * jax.random.uniform(arg_keys[8], (PR, 128), jnp.float32) ** shard_levels(arg_keys[8], (PR, 128), ((0, 2),), -0.2, 0.2)), 0.01, 10.0),
    }


@jax.custom_vjp
def low(v):
    return lax.optimization_barrier(v.astype(jnp.bfloat16)).astype(jnp.float32)

@jax.custom_vjp
def low_back(v):
    return v

def low_keep(v):
    return (low(v), None)

def low_pass(kept, grad):
    return (grad,)

def back_keep(v):
    return (v, None)

def back_low(kept, grad):
    return (low(grad),)
low.defvjp(low_keep, low_pass)
low_back.defvjp(back_keep, back_low)
highest = lax.Precision.HIGHEST
first_bias_fix = 0.9999734386011124
second_bias_fix = 0.994079470779666

def segment_list():
    enc_inner = HE * HD
    dec_inner = HDEC * HD
    return [('enc_cls', (DE,)), ('enc_norm1_gain', (DE,)), ('enc_norm1_bias', (DE,)), ('enc_qkv', (DE, 3 * enc_inner)), ('enc_out', (enc_inner, DE)), ('enc_out_bias', (DE,)), ('enc_norm2_gain', (DE,)), ('enc_norm2_bias', (DE,)), ('enc_fc1', (DE, FE)), ('enc_fc1_bias', (FE,)), ('enc_fc2', (FE, DE)), ('enc_fc2_bias', (DE,)), ('enc_final_gain', (DE,)), ('enc_final_bias', (DE,)), ('proj', (DE, DD)), ('proj_bias', (DD,)), ('mask_token', (DD,)), ('dec_norm1_gain', (DD,)), ('dec_norm1_bias', (DD,)), ('dec_qkv', (DD, 3 * dec_inner)), ('dec_out', (dec_inner, DD)), ('dec_out_bias', (DD,)), ('dec_norm2_gain', (DD,)), ('dec_norm2_bias', (DD,)), ('dec_fc1', (DD, FD)), ('dec_fc1_bias', (FD,)), ('dec_fc2', (FD, DD)), ('dec_fc2_bias', (DD,))]

def unpack(flat_vec):
    pieces = {}
    offset = 0
    for label, dims_of in segment_list():
        length = math.prod(dims_of)
        pieces[label] = flat_vec[offset:offset + length].reshape(dims_of)
        offset = offset + length
    return pieces

def position_table():
    half_width = DD // 2
    places = jnp.arange(PATCH, dtype=jnp.float32)[:, None]
    rates = jnp.exp(jnp.arange(half_width, dtype=jnp.float32) * (-math.log(10000.0) / half_width))
    angles = places * rates[None, :]
    return jnp.concatenate([jnp.sin(angles), jnp.cos(angles)], 1)

def layer_norm(stream, gain_vec, bias_vec):
    average = lax.optimization_barrier(jnp.mean(stream, -1, keepdims=True))
    centred = stream - average
    spread = lax.optimization_barrier(jnp.mean(centred * centred, -1, keepdims=True))
    return centred * lax.rsqrt(spread + 1e-05) * gain_vec + bias_vec

def both_ways(value):
    return low(low_back(value))

def attention_branch(normed, wmap, prefix, heads):
    chips, tokens, width = normed.shape
    inner = heads * HD
    triple = both_ways(jnp.einsum('ctd,de->cte', normed, wmap[prefix + '_qkv'], precision=highest))
    query_rows = triple[:, :, :inner].reshape(chips, tokens, heads, HD)
    key_rows = triple[:, :, inner:2 * inner].reshape(chips, tokens, heads, HD)
    value_rows = triple[:, :, 2 * inner:].reshape(chips, tokens, heads, HD)
    scores = low_back(jnp.einsum('cqhe,ckhe->chqk', query_rows, key_rows, precision=highest) * HD ** (-0.5))
    probs = jax.nn.softmax(scores, -1)
    mixed = jnp.einsum('chqk,ckhe->cqhe', low(probs), value_rows, precision=highest)
    mixed = both_ways(mixed.reshape(chips, tokens, inner))
    return low_back(jnp.einsum('cti,id->ctd', mixed, wmap[prefix + '_out'], precision=highest) + wmap[prefix + '_out_bias'])

def block(stream, wmap, prefix, heads):
    normed1 = low(layer_norm(stream, wmap[prefix + '_norm1_gain'], wmap[prefix + '_norm1_bias']))
    middle = stream + attention_branch(normed1, wmap, prefix, heads)
    normed2 = low(layer_norm(middle, wmap[prefix + '_norm2_gain'], wmap[prefix + '_norm2_bias']))
    hidden_pre = low_back(jnp.einsum('ctd,df->ctf', normed2, wmap[prefix + '_fc1'], precision=highest) + wmap[prefix + '_fc1_bias'])
    activ = low(jax.nn.gelu(hidden_pre, approximate=False))
    return middle + low_back(jnp.einsum('ctf,fd->ctd', activ, wmap[prefix + '_fc2'], precision=highest) + wmap[prefix + '_fc2_bias'])

def forward(flat_vec, patch_vals, meta_vals, visible_ids, masked_ids, flag_vals):
    wmap = unpack(low(flat_vec))
    chips = patch_vals.shape[0]
    patch_ids = jnp.arange(PATCH, dtype=jnp.int32)
    chooser = (visible_ids[:, :, None] == patch_ids[None, None, :]).astype(jnp.float32)
    picked = jnp.einsum('cvp,cpd->cvd', chooser, patch_vals, precision=highest)
    keep_meta = (1 - flag_vals).astype(jnp.float32)
    meta_row = meta_vals * keep_meta[:, None]
    class_row = jnp.broadcast_to(wmap['enc_cls'][None, None, :], (chips, 1, DE))
    enc_in = jnp.concatenate([class_row, meta_row[:, None, :], picked], 1)
    enc_out = block(enc_in, wmap, 'enc', HE)
    encoded = low(layer_norm(enc_out[:, 2:, :], wmap['enc_final_gain'], wmap['enc_final_bias']))
    projected = low_back(jnp.einsum('cvd,de->cve', encoded, wmap['proj'], precision=highest) + wmap['proj_bias'])
    filled = jnp.einsum('cvp,cve->cpe', chooser, projected, precision=highest)
    mask_rows = lax.optimization_barrier(jnp.sum((masked_ids[:, :, None] == patch_ids[None, None, :]).astype(jnp.float32), 1))
    dec_in = filled + mask_rows[:, :, None] * wmap['mask_token'][None, None, :] + position_table()[None]
    return block(dec_in, wmap, 'dec', HDEC)

def adam_step(grads, moment1, moment2):
    new_first = 0.9 * moment1 + (1.0 - 0.9) * grads
    new_second = 0.95 * moment2 + (1.0 - 0.95) * grads * grads
    update = new_first / first_bias_fix / (jnp.sqrt(new_second / second_bias_fix) + 1e-08)
    return (update, new_first, new_second)

def reference(patches, timeloc, visible, masked, flags, cotangent, params, moment1, moment2):
    flat = params.reshape(-1)
    groups = CHIPS // CHIPS_DEV

    def split_groups(array):
        return array.reshape((groups, CHIPS_DEV) + array.shape[1:])
    items = tuple((split_groups(array) for array in (patches, timeloc, visible, masked, flags, cotangent)))

    def step(totals, item):
        patch_grp, meta_grp, visible_grp, masked_grp, flag_grp, cot_grp = item

        def run(flat_vec, patch_vals):
            return forward(flat_vec, patch_vals, meta_grp.astype(jnp.float32), visible_grp, masked_grp, flag_grp)
        result, pull = jax.vjp(run, flat, patch_grp.astype(jnp.float32))
        d_flat, d_patch = pull(cot_grp.astype(jnp.float32))
        return (totals + d_flat, (result.astype(jnp.bfloat16), d_patch.astype(jnp.bfloat16)))
    totals, (outputs, patch_grads) = lax.scan(step, jnp.zeros(flat.shape, jnp.float32), items)
    grads = (totals / CHIPS).reshape(PR, 128)
    update, new_moment1, new_moment2 = adam_step(grads, moment1, moment2)
    dec_out = outputs.reshape(CHIPS, PATCH, DD)
    patch_grad = patch_grads.reshape(CHIPS, PATCH, DE)
    return (dec_out, patch_grad, grads, update, new_moment1, new_moment2)
```

```python
import math

import jax
import jax.numpy as jnp
from jax import lax
from jax.experimental import pallas as pl
from jax.experimental.pallas import tpu as pltpu
from jax.sharding import PartitionSpec as P

DE = 768
HE = 12
HD = 64
FE = 3072
DD = 512
HDEC = 4
FD = 2048
PATCH = 256


highest = lax.Precision.HIGHEST
first_bias_fix = 0.9999734386011124
second_bias_fix = 0.994079470779666


def block_segments(prefix, width, inner, hidden):
    names = ("g1", "b1", "qkv", "o", "ob", "g2", "b2", "u", "ub", "v", "vb")
    dims = ((width,), (width,), (width, 3 * inner), (inner, width), (width,), (width,), (width,))
    dims = (*dims, (width, hidden), (hidden,), (hidden, width), (width,))
    return [(prefix + name, size) for name, size in zip(names, dims)]


def segment_list():
    ends = (("fg", (DE,)), ("fb", (DE,)), ("proj", (DE, DD)), ("pb", (DD,)), ("mask", (DD,)))
    return [
        ("cls", (DE,)),
        *block_segments("e", DE, HE * HD, FE),
        *ends,
        *block_segments("d", DD, HDEC * HD, FD),
    ]


MARGIN = 256


def flat_rows():
    table = {}
    offset = 0
    for label, dims_of in segment_list():
        rows = math.prod(dims_of) // 128
        table[label] = (offset, rows)
        offset = offset + rows
    return table, offset


def round_up(value, unit):
    return -(-value // unit) * unit


def group_list():
    firsts = ("cls", "eo", "eu", "ev", "proj", "dqkv", "du", "dv")
    groups = []
    for label, dims in segment_list():
        if label in firsts:
            groups.append([])
        if label == "dg1" or label == "db1" or groups:
            groups[-1].append(label)
    return groups


def unpack(sources, total):
    table, used = flat_rows()
    shapes = dict(segment_list())
    groups = group_list()
    spans = [(table[g[0]][0], sum(table[g[-1]])) for g in groups]
    edges = [0, *[min(round_up(high, 16), total) for low, high in spans]]
    half = total // 2
    copies = []
    for k, (low, high) in enumerate(zip(edges, edges[1:])):
        parts = [(low, high)]
        if len(sources) == 2 and low < half < high:
            parts = [(low, half), (half, high)]
        copies.append(parts)
    slots = [(k, p) for k, parts in enumerate(copies) for p in range(len(parts))]
    labels = [label for label, dims in segment_list()]
    deepest = max(round_up(high, 16) - low // 16 * 16 for low, high in spans)

    def kernel(*refs):
        ins, rest = refs[: len(sources)], refs[len(sources) :]
        outs = dict(zip(labels, rest))
        staged, wide_rows, sems = rest[len(labels) :]

        def copy(slot, source, shift):
            k, p = slot
            low, high = copies[k][p]
            return pltpu.make_async_copy(
                source.at[pl.ds(low - shift, high - low)],
                staged.at[pl.ds(low, high - low)],
                sems.at[slots.index(slot)],
            )

        if len(sources) == 2:
            mine = lax.axis_index("narrow")
            for slot in slots:
                place = 0 if copies[slot[0]][slot[1]][0] < half else 1

                @pl.when(mine == place)
                def own_part(slot=slot, place=place):
                    copy(slot, ins[0], place * half).start()

                @pl.when(mine != place)
                def other_part(slot=slot, place=place):
                    copy(slot, ins[1], place * half).start()
        else:
            for slot in slots:
                copy(slot, ins[0], 0).start()
        for k, group in enumerate(groups):
            for p in range(len(copies[k])):
                copy((k, p), ins[0], copies[k][p][0]).wait()
            low, high = spans[k]
            origin = low // 16 * 16
            length = round_up(high, 16) - origin

            def widen(i, carry, origin=origin):
                spot = pl.multiple_of(i * 128, 128)
                wide_rows[pl.ds(spot, 128), :] = staged[
                    pl.ds(pl.multiple_of(origin + spot, 16), 128), :
                ].astype(jnp.float32)
                return carry

            lax.fori_loop(0, length // 128, widen, 0)
            done = length // 128 * 128
            if done < length:
                wide_rows[done:length, :] = staged[origin + done : origin + length, :].astype(
                    jnp.float32
                )
            for label in group:
                base = table[label][0] - origin
                dims, ref = shapes[label], outs[label]
                tiles = dims[-1] // 128
                if len(dims) == 1:
                    for c in range(tiles):
                        ref[:, c * 128 : (c + 1) * 128] = wide_rows[base + c : base + c + 1, :]
                    continue

                def step(i, carry, base=base, tiles=tiles, ref=ref):
                    for c in range(tiles):
                        rows = wide_rows[pl.ds(base + i * 16 * tiles + c, 16, stride=tiles), :]
                        ref[pl.ds(pl.multiple_of(i * 16, 16), 16), c * 128 : (c + 1) * 128] = (
                            rows.astype(jnp.bfloat16)
                        )
                    return carry

                lax.fori_loop(0, dims[0] // 16, step, 0)

    out_shape = [
        jax.ShapeDtypeStruct(dims, jnp.bfloat16)
        if len(dims) == 2
        else jax.ShapeDtypeStruct((1, dims[0]), jnp.float32)
        for label, dims in segment_list()
    ]
    outs = pl.pallas_call(
        kernel,
        out_shape=out_shape,
        in_specs=[pl.BlockSpec(memory_space=pl.ANY)] * len(sources),
        scratch_shapes=[
            pltpu.VMEM((total, 128), jnp.bfloat16),
            pltpu.VMEM((deepest, 128), jnp.float32),
            pltpu.SemaphoreType.DMA((len(slots),)),
        ],
        compiler_params=pltpu.CompilerParams(vmem_limit_bytes=61 << 20),
        name="unpack",
    )(*sources)
    return dict(zip(labels, outs))


def cut_points(total, unit):
    table, used = flat_rows()
    inner = [round_up(table[label][0], unit) for label in ("eu", "ev", "proj")]
    return [0, *inner, round_up(total, unit)]


def pack_segment(pieces, low, high, first, last, held):
    table, used = flat_rows()
    labels = [k for k, (off, rows) in table.items() if off < high and off + rows > low]
    arrays = [
        pieces[k] if pieces[k].ndim == 2 else pieces[k].reshape(1, -1) for k in labels
    ]
    length = high - low
    middle = (first + last) // 2
    runs = [
        (max(low, start), min(high, end), place, start)
        for place, (start, end) in enumerate(((first, middle), (middle, last)))
        if max(low, start) < min(high, end)
    ]
    taken = len(held)

    def kernel(*refs):
        ins, rest = refs[: len(labels)], refs[len(labels) + taken :]
        kept, sent, flat, out, sems = rest
        if used < high:
            start = max(used, low) - low + MARGIN
            flat[start : MARGIN + length, :] = jnp.zeros((MARGIN + length - start, 128), jnp.float32)
        for k, ref in zip(labels, ins):
            off, rows = table[k]
            tiles = ref.shape[1] // 128
            base = off - low + MARGIN
            if ref.shape[0] == 1:
                for c in range(tiles):
                    spot = base + c
                    if 0 <= spot < length + 2 * MARGIN:
                        flat[spot : spot + 1, :] = ref[:, c * 128 : (c + 1) * 128]
                continue
            block = 8 * tiles
            begin = max(0, low - off) // block
            end = -(-min(rows, high - off) // block)

            def step(i, carry, ref=ref, tiles=tiles, base=base, block=block):
                for c in range(tiles):
                    flat[pl.ds(base + i * block + c, 8, stride=tiles), :] = ref[
                        pl.ds(pl.multiple_of(i * 8, 8), 8), c * 128 : (c + 1) * 128
                    ]
                return carry

            lax.fori_loop(begin, end, step, 0)

        def narrow_down(i, carry):
            spot = pl.multiple_of(i * 128, 128)
            out[pl.ds(spot, 128), :] = flat[pl.ds(MARGIN + spot, 128), :].astype(jnp.bfloat16)
            return carry

        lax.fori_loop(0, length // 128, narrow_down, 0)
        mine = lax.axis_index("narrow")

        def copy(n, target):
            start, end, place, origin = runs[n]
            return pltpu.make_async_copy(
                out.at[pl.ds(start - low, end - start)],
                target.at[pl.ds(start - origin, end - start)],
                sems.at[n],
            )

        for n, (start, end, place, origin) in enumerate(runs):

            @pl.when(mine == place)
            def keep(n=n):
                copy(n, kept).start()

            @pl.when(mine != place)
            def send(n=n):
                copy(n, sent).start()

        for n in range(len(runs)):
            copy(n, kept).wait()

    anywhere = pl.BlockSpec(memory_space=pl.ANY)
    whole = pl.BlockSpec(memory_space=pltpu.VMEM)
    return pl.pallas_call(
        kernel,
        out_shape=[jax.ShapeDtypeStruct((middle - first, 128), jnp.bfloat16)] * 2,
        in_specs=[whole] * len(arrays) + [anywhere] * taken,
        out_specs=[anywhere] * 2,
        input_output_aliases={len(arrays) + n: n for n in range(taken)},
        scratch_shapes=[
            pltpu.VMEM((length + 2 * MARGIN, 128), jnp.float32),
            pltpu.VMEM((length, 128), jnp.bfloat16),
            pltpu.SemaphoreType.DMA((len(runs),)),
        ],
        compiler_params=pltpu.CompilerParams(vmem_limit_bytes=61 << 20),
        name=f"pack{low}",
    )(*arrays, *held)


def pack_halves(pieces, cuts):
    if lax.axis_size("narrow") == 2:
        held = ()
        for low, high in zip(cuts, cuts[1:]):
            held = pack_segment(pieces, low, high, cuts[0], cuts[-1], held)
        return held
    flat = jnp.concatenate([pieces[k].reshape(-1) for k, dims in segment_list()])
    flat = jnp.concatenate([flat, jnp.zeros((cuts[-1] * 128 - flat.shape[0],), jnp.float32)])
    return (flat.reshape(-1, 128)[cuts[0] :].astype(jnp.bfloat16),)


def added(first, second):
    return (first.astype(jnp.float32) + second.astype(jnp.float32)).astype(jnp.bfloat16)


def piece(value, index, rows):
    return lax.dynamic_slice_in_dim(value, index * rows, rows, 0)


class Line:
    def __init__(self, stride, size):
        self.stride, self.size, self.wide = stride, size, lax.axis_size("wide")
        self.me = (lax.axis_index("wide") // stride) % size
        self.groups = [
            [i + k * stride for k in range(size)]
            for i in range(self.wide)
            if (i // stride) % size == 0
        ]

    def swap(self, value):
        pairs = [pair for a, b in self.groups for pair in ((a, b), (b, a))]
        return lax.ppermute(value, "wide", pairs)

    def exchange(self, value):
        return lax.all_to_all(value, "wide", 0, 0, axis_index_groups=self.groups)

    def scatter(self, value):
        rows = value.shape[0] // self.size
        if self.size == 2:
            got = self.swap(piece(value, 1 - self.me, rows))
            return added(piece(value, self.me, rows), got)
        got = self.exchange(value.reshape(self.size, -1, 128)).astype(jnp.float32)
        return jnp.sum(got, 0).astype(jnp.bfloat16).reshape(rows, -1, 128)

    def gather(self, value):
        if self.size == 2:
            got = self.swap(value)
            low = self.me == 0
            return jnp.concatenate([jnp.where(low, value, got), jnp.where(low, got, value)], 0)
        copies = jnp.broadcast_to(value[None], (self.size, *value.shape))
        return self.exchange(copies).reshape(-1, *value.shape[1:])


def narrow_swap(value, step):
    count = lax.axis_size("narrow")
    return lax.ppermute(value, "narrow", [(i, (i + step) % count) for i in range(count)])


def sum_everywhere(halves):
    count, wide = lax.axis_size("narrow"), lax.axis_size("wide")
    if len(halves) == 2:
        total = added(halves[0], narrow_swap(halves[1], 1))
    else:
        (value,) = halves
        mine = lax.axis_index("narrow")
        rows = value.shape[0] // count
        total = piece(value, mine, rows)
        for step in range(1, count):
            total = added(total, narrow_swap(piece(value, (mine + step) % count, rows), step))
    rows = total.shape[0]
    depth = wide // 4
    x, y, z = Line(1, 2), Line(2, 2), Line(4, depth)
    unit = wide * 8
    units = rows // unit
    most = units * 4 // 11
    first, second = most * unit, 2 * most * unit
    a = total[:first].reshape(2, 2, depth, -1, 128)
    b = total[first:second].reshape(2, 2, depth, -1, 128)
    c = total[second:].reshape(depth, 2, 2, -1, 128)
    flat3 = lambda v, n: v.reshape(n, -1, 128)
    c = z.scatter(flat3(c, depth))
    a = x.scatter(flat3(a, 2))
    b = y.scatter(flat3(b, 2))
    a = y.scatter(flat3(a, 2))
    b = x.scatter(flat3(b, 2))
    a, b, c = lax.optimization_barrier((a, b, c))
    ab = z.scatter(jnp.concatenate([flat3(a, depth), flat3(b, depth)], 1))
    c = x.scatter(flat3(c, 2))
    c = y.scatter(flat3(c, 2))
    ab, c = lax.optimization_barrier((ab, c))
    ab = z.gather(flat3(ab, 1))
    c = x.gather(y.gather(flat3(c, 1)))
    ab, c = lax.optimization_barrier((ab, c))
    half = ab.shape[1] // 2
    a, b = ab[:, :half], ab[:, half:]
    c = z.gather(flat3(c, 1))
    a = y.gather(flat3(a, 1))
    b = x.gather(flat3(b, 1))
    a = x.gather(flat3(a, 1))
    b = y.gather(flat3(b, 1))
    return jnp.concatenate([v.reshape(-1, 128) for v in (a, b, c)], 0)


def whole_params(params):
    low_params = params.astype(jnp.bfloat16)
    if lax.axis_size("narrow") == 2:
        return (low_params, narrow_swap(low_params, 1))
    return (lax.all_gather(low_params, "narrow", axis=0, tiled=True),)


def position_table():
    half_width = DD // 2
    places = jnp.arange(PATCH, dtype=jnp.float32)[:, None]
    rates = jnp.exp(jnp.arange(half_width, dtype=jnp.float32) * (-math.log(10000.0) / half_width))
    angles = places * rates[None, :]
    return jnp.concatenate([jnp.sin(angles), jnp.cos(angles)], 1)


def layer_norm(stream, gain_vec, bias_vec):
    average = jnp.mean(stream, -1, keepdims=True)
    centred = stream - average
    spread = jnp.mean(centred * centred, -1, keepdims=True)
    return centred * lax.rsqrt(spread + 1e-05) * gain_vec + bias_vec


def vector(weights_map, label):
    return weights_map[label].reshape(-1)


def adam_step(grads, moment1, moment2):
    new_first = 0.9 * moment1 + (1.0 - 0.9) * grads
    new_second = 0.95 * moment2 + (1.0 - 0.95) * grads * grads
    update = new_first / first_bias_fix / (jnp.sqrt(new_second / second_bias_fix) + 1e-08)
    return (update, new_first, new_second)


def gelu_and_slope(u):
    t = 1.0 / (1.0 + (0.3275911 * math.sqrt(0.5)) * jnp.abs(u))
    bell = jnp.exp(-0.5 * u * u)
    tail = 0.5 * 1.061405429
    for term in (-1.453152027, 1.421413741, -0.284496736, 0.254829592):
        tail = tail * t + 0.5 * term
    tail = tail * t * bell
    below = jnp.where(u < 0, tail, 1.0 - tail)
    slope = below + u * bell * (1.0 / math.sqrt(2.0 * math.pi))
    return (u * below).astype(jnp.bfloat16), slope.astype(jnp.bfloat16)


def block_forward(stream, weights_map, prefix, heads):
    chips, tokens, width = stream.shape
    inner = heads * HD
    normed1 = layer_norm(
        stream,
        vector(weights_map, prefix + "g1"),
        vector(weights_map, prefix + "b1"),
    )
    first_in = normed1.astype(jnp.bfloat16)
    triple = jnp.einsum(
        "ctd,de->cte", first_in, weights_map[prefix + "qkv"], preferred_element_type=jnp.float32
    ).astype(jnp.bfloat16)
    query_rows = triple[:, :, :inner].reshape(chips, tokens, heads, HD)
    key_rows = triple[:, :, inner : 2 * inner].reshape(chips, tokens, heads, HD)
    value_rows = triple[:, :, 2 * inner :].reshape(chips, tokens, heads, HD)
    scores = jnp.einsum(
        "cqhe,ckhe->chqk", query_rows, key_rows, preferred_element_type=jnp.float32
    ) * HD ** (-0.5)
    topmost = jnp.max(scores, -1, keepdims=True)
    expos = jnp.exp(scores - topmost)
    totals = jnp.sum(expos, -1, keepdims=True)
    logsum = topmost + jnp.log(totals)
    probs = (expos / totals).astype(jnp.bfloat16)
    mixed = jnp.einsum("chqk,ckhe->cqhe", probs, value_rows, preferred_element_type=jnp.float32)
    mixed = mixed.reshape(chips, tokens, inner).astype(jnp.bfloat16)
    middle = (
        stream
        + jnp.einsum(
            "cti,id->ctd", mixed, weights_map[prefix + "o"], preferred_element_type=jnp.float32
        )
        + vector(weights_map, prefix + "ob")
    )
    normed2 = layer_norm(
        middle,
        vector(weights_map, prefix + "g2"),
        vector(weights_map, prefix + "b2"),
    )
    second_in = normed2.astype(jnp.bfloat16)
    hidden_pre = jnp.einsum(
        "ctd,df->ctf", second_in, weights_map[prefix + "u"], preferred_element_type=jnp.float32
    ) + vector(weights_map, prefix + "ub")
    activ, slope = gelu_and_slope(hidden_pre)
    result = (
        middle
        + jnp.einsum(
            "ctf,fd->ctd", activ, weights_map[prefix + "v"], preferred_element_type=jnp.float32
        )
        + vector(weights_map, prefix + "vb")
    )
    kept = (
        stream,
        middle,
        first_in,
        query_rows,
        key_rows,
        value_rows,
        logsum,
        mixed,
        second_in,
        slope,
        activ,
    )
    return (result, kept)


def block_backward(upstream, kept, weights_map, prefix, heads):
    (
        stream,
        middle,
        first_in,
        query_rows,
        key_rows,
        value_rows,
        logsum,
        mixed,
        second_in,
        slope,
        activ,
    ) = kept
    chips, tokens, width = stream.shape
    inner = heads * HD
    grads = {}
    branch_two = upstream.astype(jnp.bfloat16)
    grads[prefix + "vb"] = jnp.sum(branch_two.astype(jnp.float32), (0, 1))
    grads[prefix + "v"] = jnp.einsum(
        "ctf,ctd->fd", activ, branch_two, preferred_element_type=jnp.float32
    )
    d_activ = jnp.einsum(
        "ctd,fd->ctf", branch_two, weights_map[prefix + "v"], preferred_element_type=jnp.float32
    )
    d_hidden = (d_activ * slope.astype(jnp.float32)).astype(jnp.bfloat16)
    grads[prefix + "ub"] = jnp.sum(d_hidden.astype(jnp.float32), (0, 1))
    grads[prefix + "u"] = jnp.einsum(
        "ctd,ctf->df", second_in, d_hidden, preferred_element_type=jnp.float32
    )
    d_second = jnp.einsum(
        "ctf,df->ctd", d_hidden, weights_map[prefix + "u"], preferred_element_type=jnp.float32
    )
    norm_pull = jax.vjp(
        layer_norm,
        middle,
        vector(weights_map, prefix + "g2"),
        vector(weights_map, prefix + "b2"),
    )[1]
    d_middle_part, grads[prefix + "g2"], grads[prefix + "b2"] = norm_pull(
        d_second
    )
    d_middle = upstream + d_middle_part
    branch_one = d_middle.astype(jnp.bfloat16)
    grads[prefix + "ob"] = jnp.sum(branch_one.astype(jnp.float32), (0, 1))
    grads[prefix + "o"] = jnp.einsum(
        "cti,ctd->id", mixed, branch_one, preferred_element_type=jnp.float32
    )
    d_mixed = jnp.einsum(
        "ctd,id->cti", branch_one, weights_map[prefix + "o"], preferred_element_type=jnp.float32
    )
    d_mixed = d_mixed.astype(jnp.bfloat16).reshape(chips, tokens, heads, HD)
    scores = jnp.einsum(
        "cqhe,ckhe->chqk", query_rows, key_rows, preferred_element_type=jnp.float32
    ) * HD ** (-0.5)
    probs_full = jnp.exp(scores - logsum)
    probs_low = probs_full.astype(jnp.bfloat16)
    d_value = jnp.einsum("chqk,cqhe->ckhe", probs_low, d_mixed, preferred_element_type=jnp.float32)
    d_probs = jnp.einsum("cqhe,ckhe->chqk", d_mixed, value_rows, preferred_element_type=jnp.float32)
    row_shift = jnp.sum(d_probs * probs_full, -1, keepdims=True)
    d_scores = (probs_full * (d_probs - row_shift)).astype(jnp.bfloat16)
    d_query = jnp.einsum(
        "chqk,ckhe->cqhe", d_scores, key_rows, preferred_element_type=jnp.float32
    ) * HD ** (-0.5)
    d_key = jnp.einsum(
        "chqk,cqhe->ckhe", d_scores, query_rows, preferred_element_type=jnp.float32
    ) * HD ** (-0.5)
    d_triple = jnp.concatenate(
        [
            d_query.reshape(chips, tokens, inner),
            d_key.reshape(chips, tokens, inner),
            d_value.reshape(chips, tokens, inner),
        ],
        -1,
    ).astype(jnp.bfloat16)
    grads[prefix + "qkv"] = jnp.einsum(
        "ctd,cte->de", first_in, d_triple, preferred_element_type=jnp.float32
    )
    d_first = jnp.einsum(
        "cte,de->ctd", d_triple, weights_map[prefix + "qkv"], preferred_element_type=jnp.float32
    )
    first_pull = jax.vjp(
        layer_norm,
        stream,
        vector(weights_map, prefix + "g1"),
        vector(weights_map, prefix + "b1"),
    )[1]
    d_stream_part, grads[prefix + "g1"], grads[prefix + "b1"] = first_pull(
        d_first
    )
    return (d_middle + d_stream_part, grads)


def per_device(patches, timeloc, visible, masked, flags, cotangent, params, moment1, moment2):
    total_rows = params.shape[0] * lax.axis_size("narrow")
    weights_map = unpack(whole_params(params), total_rows)
    chips = patches.shape[0]
    patch_ids = jnp.arange(PATCH, dtype=jnp.int32)
    chooser = visible[:, :, None] == patch_ids[None, None, :]
    choose_low = chooser.astype(jnp.bfloat16)
    choose_full = chooser.astype(jnp.float32)
    picked = jnp.einsum("cvp,cpd->cvd", choose_low, patches, preferred_element_type=jnp.float32)
    keep_meta = (1 - flags).astype(jnp.float32)
    meta_row = timeloc.astype(jnp.float32) * keep_meta[:, None]
    class_row = jnp.broadcast_to(vector(weights_map, "cls")[None, None, :], (chips, 1, DE))
    enc_in = jnp.concatenate([class_row, meta_row[:, None, :], picked], 1)
    enc_out, enc_kept = block_forward(enc_in, weights_map, "e", HE)
    patch_rows = enc_out[:, 2:, :]
    final_gain = vector(weights_map, "fg")
    final_bias = vector(weights_map, "fb")
    encoded_low = layer_norm(patch_rows, final_gain, final_bias).astype(jnp.bfloat16)
    projected = jnp.einsum(
        "cvd,de->cve", encoded_low, weights_map["proj"], preferred_element_type=jnp.float32
    ) + vector(weights_map, "pb")
    filled = jnp.einsum("cvp,cve->cpe", choose_full, projected, precision=highest)
    mask_rows = jnp.sum((masked[:, :, None] == patch_ids[None, None, :]).astype(jnp.float32), 1)
    dec_in = (
        filled
        + mask_rows[:, :, None] * vector(weights_map, "mask")[None, None, :]
        + position_table()[None]
    )
    dec_out, dec_kept = block_forward(dec_in, weights_map, "d", HDEC)
    d_dec_in, grads = block_backward(
        cotangent.astype(jnp.float32), dec_kept, weights_map, "d", HDEC
    )
    grads["mask"] = jnp.sum(mask_rows[:, :, None] * d_dec_in, (0, 1))
    d_projected = jnp.einsum("cvp,cpe->cve", choose_full, d_dec_in, precision=highest).astype(
        jnp.bfloat16
    )
    grads["pb"] = jnp.sum(d_projected.astype(jnp.float32), (0, 1))
    grads["proj"] = jnp.einsum(
        "cvd,cve->de", encoded_low, d_projected, preferred_element_type=jnp.float32
    )
    d_encoded = jnp.einsum(
        "cve,de->cvd", d_projected, weights_map["proj"], preferred_element_type=jnp.float32
    )
    final_pull = jax.vjp(layer_norm, patch_rows, final_gain, final_bias)[1]
    d_patch_rows, grads["fg"], grads["fb"] = final_pull(d_encoded)
    d_enc_out = jnp.concatenate([jnp.zeros((chips, 2, DE), jnp.float32), d_patch_rows], 1)
    d_enc_in, enc_grads = block_backward(d_enc_out, enc_kept, weights_map, "e", HE)
    grads.update(enc_grads)
    grads["cls"] = jnp.sum(d_enc_in[:, 0, :], 0)
    patch_grad = jnp.einsum(
        "cvp,cvd->cpd", choose_full, d_enc_in[:, 2:, :], precision=highest
    ).astype(jnp.bfloat16)
    narrow_count, wide_count = lax.axis_size("narrow"), lax.axis_size("wide")
    chips_all = float(chips * wide_count * narrow_count)
    cuts = cut_points(total_rows, narrow_count * wide_count * 8)
    mine = sum_everywhere(pack_halves(grads, cuts))[: params.shape[0]]
    grad_out = mine.astype(jnp.float32) / chips_all
    update, new_moment1, new_moment2 = adam_step(grad_out, moment1, moment2)
    return (dec_out.astype(jnp.bfloat16), patch_grad, grad_out, update, new_moment1, new_moment2)


def solution(mesh):
    placed = (
        P(("wide", "narrow"), None, None),
        P(("wide", "narrow"), None),
        P(("wide", "narrow"), None),
        P(("wide", "narrow"), None),
        P(("wide", "narrow")),
        P(("wide", "narrow"), None, None),
        P("narrow", None),
        P("narrow", None),
        P("narrow", None),
    )
    return jax.shard_map(
        per_device,
        mesh=mesh,
        in_specs=placed,
        out_specs=(
            P(("wide", "narrow"), None, None),
            P(("wide", "narrow"), None, None),
            P("narrow", None),
            P("narrow", None),
            P("narrow", None),
            P("narrow", None),
        ),
        check_vma=False,
    )
```

```python
import math

import jax
import jax.numpy as jnp
from jax import lax
from jax.experimental import pallas as pl
from jax.experimental.pallas import tpu as pltpu
from jax.sharding import PartitionSpec as P

DE = 768
HE = 12
HD = 64
FE = 3072
DD = 512
HDEC = 4
FD = 2048
PATCH = 256


highest = lax.Precision.HIGHEST
first_bias_fix = 0.9999734386011124
second_bias_fix = 0.994079470779666


def block_segments(prefix, width, inner, hidden):
    names = ("g1", "b1", "qkv", "o", "ob", "g2", "b2", "u", "ub", "v", "vb")
    dims = ((width,), (width,), (width, 3 * inner), (inner, width), (width,), (width,), (width,))
    dims = (*dims, (width, hidden), (hidden,), (hidden, width), (width,))
    return [(prefix + name, size) for name, size in zip(names, dims)]


def segment_list():
    ends = (("fg", (DE,)), ("fb", (DE,)), ("proj", (DE, DD)), ("pb", (DD,)), ("mask", (DD,)))
    return [
        ("cls", (DE,)),
        *block_segments("e", DE, HE * HD, FE),
        *ends,
        *block_segments("d", DD, HDEC * HD, FD),
    ]


MARGIN = 256


def flat_rows():
    table = {}
    offset = 0
    for label, dims_of in segment_list():
        rows = math.prod(dims_of) // 128
        table[label] = (offset, rows)
        offset = offset + rows
    return table, offset


def round_up(value, unit):
    return -(-value // unit) * unit


def group_list():
    firsts = ("cls", "eo", "eu", "ev", "proj", "dqkv", "du", "dv")
    groups = []
    for label, dims in segment_list():
        if label in firsts:
            groups.append([])
        if label == "dg1" or label == "db1" or groups:
            groups[-1].append(label)
    return groups


def unpack(sources, total):
    table, used = flat_rows()
    shapes = dict(segment_list())
    groups = group_list()
    spans = [(table[g[0]][0], sum(table[g[-1]])) for g in groups]
    edges = [0, *[min(round_up(high, 16), total) for low, high in spans]]
    half = total // 2
    copies = []
    for k, (low, high) in enumerate(zip(edges, edges[1:])):
        parts = [(low, high)]
        if len(sources) == 2 and low < half < high:
            parts = [(low, half), (half, high)]
        copies.append(parts)
    slots = [(k, p) for k, parts in enumerate(copies) for p in range(len(parts))]
    labels = [label for label, dims in segment_list()]
    deepest = max(round_up(high, 16) - low // 16 * 16 for low, high in spans)

    def kernel(*refs):
        ins, rest = refs[: len(sources)], refs[len(sources) :]
        outs = dict(zip(labels, rest))
        staged, wide_rows, sems = rest[len(labels) :]

        def copy(slot, source, shift):
            k, p = slot
            low, high = copies[k][p]
            return pltpu.make_async_copy(
                source.at[pl.ds(low - shift, high - low)],
                staged.at[pl.ds(low, high - low)],
                sems.at[slots.index(slot)],
            )

        if len(sources) == 2:
            mine = lax.axis_index("narrow")
            for slot in slots:
                place = 0 if copies[slot[0]][slot[1]][0] < half else 1

                @pl.when(mine == place)
                def own_part(slot=slot, place=place):
                    copy(slot, ins[0], place * half).start()

                @pl.when(mine != place)
                def other_part(slot=slot, place=place):
                    copy(slot, ins[1], place * half).start()
        else:
            for slot in slots:
                copy(slot, ins[0], 0).start()
        for k, group in enumerate(groups):
            for p in range(len(copies[k])):
                copy((k, p), ins[0], copies[k][p][0]).wait()
            low, high = spans[k]
            origin = low // 16 * 16
            length = round_up(high, 16) - origin

            def widen(i, carry, origin=origin):
                spot = pl.multiple_of(i * 128, 128)
                wide_rows[pl.ds(spot, 128), :] = staged[
                    pl.ds(pl.multiple_of(origin + spot, 16), 128), :
                ].astype(jnp.float32)
                return carry

            lax.fori_loop(0, length // 128, widen, 0)
            done = length // 128 * 128
            if done < length:
                wide_rows[done:length, :] = staged[origin + done : origin + length, :].astype(
                    jnp.float32
                )
            for label in group:
                base = table[label][0] - origin
                dims, ref = shapes[label], outs[label]
                tiles = dims[-1] // 128
                if len(dims) == 1:
                    for c in range(tiles):
                        ref[:, c * 128 : (c + 1) * 128] = wide_rows[base + c : base + c + 1, :]
                    continue

                def step(i, carry, base=base, tiles=tiles, ref=ref):
                    for c in range(tiles):
                        rows = wide_rows[pl.ds(base + i * 16 * tiles + c, 16, stride=tiles), :]
                        ref[pl.ds(pl.multiple_of(i * 16, 16), 16), c * 128 : (c + 1) * 128] = (
                            rows.astype(jnp.bfloat16)
                        )
                    return carry

                lax.fori_loop(0, dims[0] // 16, step, 0)

    out_shape = [
        jax.ShapeDtypeStruct(dims, jnp.bfloat16)
        if len(dims) == 2
        else jax.ShapeDtypeStruct((1, dims[0]), jnp.float32)
        for label, dims in segment_list()
    ]
    outs = pl.pallas_call(
        kernel,
        out_shape=out_shape,
        in_specs=[pl.BlockSpec(memory_space=pl.ANY)] * len(sources),
        scratch_shapes=[
            pltpu.VMEM((total, 128), jnp.bfloat16),
            pltpu.VMEM((deepest, 128), jnp.float32),
            pltpu.SemaphoreType.DMA((len(slots),)),
        ],
        compiler_params=pltpu.CompilerParams(vmem_limit_bytes=61 << 20),
        name="unpack",
    )(*sources)
    return dict(zip(labels, outs))


def pack_chunk(pieces, low, high):
    table, used = flat_rows()
    labels = [k for k, (off, rows) in table.items() if off < high and off + rows > low]
    arrays, places = [], []
    for k in labels:
        value = pieces[k] if pieces[k].ndim == 2 else pieces[k].reshape(1, -1)
        off, rows = table[k]
        tiles = value.shape[1] // 128
        begin, end = 0, 1
        if value.shape[0] > 1:
            begin = max(0, low - off) // (8 * tiles)
            end = -(-min(rows, high - off) // (8 * tiles))
            if 3 * (end - begin) * 8 < value.shape[0]:
                value = value[begin * 8 : end * 8]
                off, end, begin = off + begin * 8 * tiles, end - begin, 0
        arrays.append(value)
        places.append((off, begin, end))
    length = high - low
    middle = length // 2

    def kernel(*refs):
        ins, rest = refs[: len(labels)], refs[len(labels) :]
        kept, sent, flat, out, sems = rest
        if used < high:
            start = max(used, low) - low + MARGIN
            flat[start : MARGIN + length, :] = jnp.zeros((MARGIN + length - start, 128), jnp.float32)
        for (off, begin, end), ref in zip(places, ins):
            tiles = ref.shape[1] // 128
            base = off - low + MARGIN
            if ref.shape[0] == 1:
                for c in range(tiles):
                    spot = base + c
                    if 0 <= spot < length + 2 * MARGIN:
                        flat[spot : spot + 1, :] = ref[:, c * 128 : (c + 1) * 128]
                continue
            block = 8 * tiles

            def step(i, carry, ref=ref, tiles=tiles, base=base, block=block):
                for c in range(tiles):
                    flat[pl.ds(base + i * block + c, 8, stride=tiles), :] = ref[
                        pl.ds(pl.multiple_of(i * 8, 8), 8), c * 128 : (c + 1) * 128
                    ]
                return carry

            lax.fori_loop(begin, end, step, 0)

        def narrow_down(i, carry):
            spot = pl.multiple_of(i * 128, 128)
            out[pl.ds(spot, 128), :] = flat[pl.ds(MARGIN + spot, 128), :].astype(jnp.bfloat16)
            return carry

        lax.fori_loop(0, length // 128, narrow_down, 0)
        mine = lax.axis_index("narrow")

        def copy(place, target):
            return pltpu.make_async_copy(out.at[pl.ds(place * middle, middle)], target, sems.at[place])

        for place in range(2):

            @pl.when(mine == place)
            def keep(place=place):
                copy(place, kept).start()

            @pl.when(mine != place)
            def send(place=place):
                copy(place, sent).start()

        for place in range(2):
            copy(place, kept).wait()

    anywhere = pl.BlockSpec(memory_space=pl.ANY)
    whole = pl.BlockSpec(memory_space=pltpu.VMEM)
    return pl.pallas_call(
        kernel,
        out_shape=[jax.ShapeDtypeStruct((middle, 128), jnp.bfloat16)] * 2,
        in_specs=[whole] * len(arrays),
        out_specs=[anywhere] * 2,
        scratch_shapes=[
            pltpu.VMEM((length + 2 * MARGIN, 128), jnp.float32),
            pltpu.VMEM((length, 128), jnp.bfloat16),
            pltpu.SemaphoreType.DMA((2,)),
        ],
        compiler_params=pltpu.CompilerParams(vmem_limit_bytes=61 << 20),
        name=f"pack{low}",
    )(*arrays)


def flat_gradient(grads, unit):
    table, used = flat_rows()
    flat = jnp.concatenate([grads[k].reshape(-1) for k, dims in segment_list()])
    padding = (round_up(used, unit) - used) * 128
    flat = jnp.concatenate([flat, jnp.zeros((padding,), jnp.float32)])
    return flat.reshape(-1, 128).astype(jnp.bfloat16)


def added(first, second):
    return (first.astype(jnp.float32) + second.astype(jnp.float32)).astype(jnp.bfloat16)


def piece(value, index, rows):
    return lax.dynamic_slice_in_dim(value, index * rows, rows, 0)


class Line:
    def __init__(self, stride, size):
        self.stride, self.size, self.wide = stride, size, lax.axis_size("wide")
        self.me = (lax.axis_index("wide") // stride) % size
        self.groups = [
            [i + k * stride for k in range(size)]
            for i in range(self.wide)
            if (i // stride) % size == 0
        ]

    def swap(self, value):
        pairs = [pair for a, b in self.groups for pair in ((a, b), (b, a))]
        return lax.ppermute(value, "wide", pairs)

    def exchange(self, value):
        return lax.all_to_all(value, "wide", 0, 0, axis_index_groups=self.groups)

    def scatter(self, value):
        rows = value.shape[0] // self.size
        if self.size == 2:
            got = self.swap(piece(value, 1 - self.me, rows))
            return added(piece(value, self.me, rows), got)
        got = self.exchange(value.reshape(self.size, -1, 128)).astype(jnp.float32)
        return jnp.sum(got, 0).astype(jnp.bfloat16).reshape(rows, -1, 128)

    def gather(self, value):
        if self.size == 2:
            got = self.swap(value)
            low = self.me == 0
            return jnp.concatenate([jnp.where(low, value, got), jnp.where(low, got, value)], 0)
        copies = jnp.broadcast_to(value[None], (self.size, *value.shape))
        return self.exchange(copies).reshape(-1, *value.shape[1:])


def narrow_swap(value, step):
    count = lax.axis_size("narrow")
    return lax.ppermute(value, "narrow", [(i, (i + step) % count) for i in range(count)])


def wide_lines():
    return Line(1, 2), Line(2, 2), Line(4, lax.axis_size("wide") // 4)


def scatter_first(value):
    x, y, z = wide_lines()
    half = value.shape[0] // 2
    a, b = value[:half].reshape(2, -1, 128), value[half:].reshape(2, -1, 128)
    return x.scatter(a), y.scatter(b)


def scatter_second(pair):
    x, y, z = wide_lines()
    return y.scatter(pair[0].reshape(2, -1, 128)), x.scatter(pair[1].reshape(2, -1, 128))


def scatter_last(pair):
    z = wide_lines()[2]
    return z.scatter(jnp.concatenate([v.reshape(z.size, -1, 128) for v in pair], 1))


def gather_first(value):
    z = wide_lines()[2]
    value = z.gather(value)
    half = value.shape[1] // 2
    return value[:, :half].reshape(1, -1, 128), value[:, half:].reshape(1, -1, 128)


def gather_second(pair):
    x, y, z = wide_lines()
    return y.gather(pair[0]).reshape(1, -1, 128), x.gather(pair[1]).reshape(1, -1, 128)


def gather_last(pair):
    x, y, z = wide_lines()
    a, b = x.gather(pair[0]), y.gather(pair[1])
    return jnp.concatenate([a.reshape(-1, 128), b.reshape(-1, 128)], 0)


def narrow_sum(halves):
    return added(halves[0], narrow_swap(halves[1], 1))


def sum_everywhere(value, rows):
    count = lax.axis_size("narrow")
    mine = lax.axis_index("narrow")
    total = lax.dynamic_slice_in_dim(value, mine * rows, rows, 0)
    for step in range(1, count):
        other = lax.dynamic_slice_in_dim(value, (mine + step) % count * rows, rows, 0)
        total = added(total, narrow_swap(other, step))
    unit = lax.axis_size("wide") * 16
    total = jnp.pad(total, ((0, round_up(rows, unit) - rows), (0, 0)))
    pair = scatter_second(scatter_first(total))
    return gather_last(gather_second(gather_first(scatter_last(pair))))[:rows]


BLOCK = 768


def adam_rows(parts, moment1, moment2, start, rows, held, chips_all):
    half = parts[0].shape[0] // BLOCK
    shift = start // BLOCK
    steps = -(-rows // BLOCK)

    def kernel(core, own_low, got_low, own_high, got_high, first, second, *rest):
        grad_out, update, new_first, new_second = rest[len(held) :]
        early = pl.program_id(0) < half
        low = jnp.where(early, own_low[...], got_low[...])
        high = jnp.where(early, got_high[...], own_high[...])
        grad = jnp.where(core[0] == 0, low, high).astype(jnp.float32) / chips_all
        grad_out[...] = grad
        update[...], new_first[...], new_second[...] = adam_step(grad, first[...], second[...])

    def early_rows(place):
        return lambda i, core: (jnp.where(core[0] == place, jnp.minimum(i, half - 1), 0), 0)

    def late_rows(place):
        return lambda i, core: (jnp.where(core[0] == place, jnp.maximum(i - half, 0), 0), 0)

    def spec(index_map):
        return pl.BlockSpec((BLOCK, 128), index_map)

    here = spec(lambda i, core: (i + shift, 0))
    maps = (early_rows(0), late_rows(0), late_rows(1), early_rows(1))
    core = lax.axis_index("narrow").astype(jnp.int32).reshape(1)
    return pl.pallas_call(
        kernel,
        out_shape=[jax.ShapeDtypeStruct(moment1.shape, jnp.float32)] * 4,
        grid_spec=pltpu.PrefetchScalarGridSpec(
            num_scalar_prefetch=1,
            grid=(steps,),
            in_specs=[*[spec(m) for m in maps], here, here]
            + [pl.BlockSpec(memory_space=pl.ANY)] * len(held),
            out_specs=[here] * 4,
        ),
        input_output_aliases={7 + n: n for n in range(len(held))},
        name=f"adam{start}",
    )(core, *parts, moment1, moment2, *held)


def to_owner(value, source):
    return lax.ppermute(value, "narrow", [(source, 1 - source)])


def whole_params(params):
    low_params = params.astype(jnp.bfloat16)
    if lax.axis_size("narrow") == 2:
        return (low_params, narrow_swap(low_params, 1))
    return (lax.all_gather(low_params, "narrow", axis=0, tiled=True),)


def position_table():
    half_width = DD // 2
    places = jnp.arange(PATCH, dtype=jnp.float32)[:, None]
    rates = jnp.exp(jnp.arange(half_width, dtype=jnp.float32) * (-math.log(10000.0) / half_width))
    angles = places * rates[None, :]
    return jnp.concatenate([jnp.sin(angles), jnp.cos(angles)], 1)


def layer_norm(stream, gain_vec, bias_vec):
    average = jnp.mean(stream, -1, keepdims=True)
    centred = stream - average
    spread = jnp.mean(centred * centred, -1, keepdims=True)
    return centred * lax.rsqrt(spread + 1e-05) * gain_vec + bias_vec


def vector(weights_map, label):
    return weights_map[label].reshape(-1)


def adam_step(grads, moment1, moment2):
    new_first = 0.9 * moment1 + (1.0 - 0.9) * grads
    new_second = 0.95 * moment2 + (1.0 - 0.95) * grads * grads
    update = new_first / first_bias_fix / (jnp.sqrt(new_second / second_bias_fix) + 1e-08)
    return (update, new_first, new_second)


tail_terms = (
    0.05025708328,
    -0.1828833063,
    0.1690591746,
    -0.005588040603,
    0.141423544,
    0.1685436795,
    0.2078425222,
    0.2256696051,
    0.2256758619,
)


def gelu_and_slope(u):
    t = 1.0 / (1.0 + (0.4 * math.sqrt(0.5)) * jnp.abs(u))
    bell = jnp.exp(-0.5 * u * u)
    tail = 0.5 * tail_terms[0]
    for term in tail_terms[1:]:
        tail = tail * t + 0.5 * term
    tail = tail * t * bell
    below = jnp.where(u < 0, tail, 1.0 - tail)
    slope = below + u * bell * (1.0 / math.sqrt(2.0 * math.pi))
    return (u * below).astype(jnp.bfloat16), slope.astype(jnp.bfloat16)


def block_forward(stream, weights_map, prefix, heads):
    chips, tokens, width = stream.shape
    inner = heads * HD
    normed1 = layer_norm(
        stream,
        vector(weights_map, prefix + "g1"),
        vector(weights_map, prefix + "b1"),
    )
    first_in = normed1.astype(jnp.bfloat16)
    triple = jnp.einsum(
        "ctd,de->cte", first_in, weights_map[prefix + "qkv"], preferred_element_type=jnp.float32
    ).astype(jnp.bfloat16)
    query_rows = triple[:, :, :inner].reshape(chips, tokens, heads, HD)
    key_rows = triple[:, :, inner : 2 * inner].reshape(chips, tokens, heads, HD)
    value_rows = triple[:, :, 2 * inner :].reshape(chips, tokens, heads, HD)
    scores = jnp.einsum(
        "cqhe,ckhe->chqk", query_rows, key_rows, preferred_element_type=jnp.float32
    ) * HD ** (-0.5)
    topmost = jnp.max(scores, -1, keepdims=True)
    expos = jnp.exp(scores - topmost)
    totals = jnp.sum(expos, -1, keepdims=True)
    logsum = topmost + jnp.log(totals)
    probs = (expos / totals).astype(jnp.bfloat16)
    mixed = jnp.einsum("chqk,ckhe->cqhe", probs, value_rows, preferred_element_type=jnp.float32)
    mixed = mixed.reshape(chips, tokens, inner).astype(jnp.bfloat16)
    middle = (
        stream
        + jnp.einsum(
            "cti,id->ctd", mixed, weights_map[prefix + "o"], preferred_element_type=jnp.float32
        )
        + vector(weights_map, prefix + "ob")
    )
    normed2 = layer_norm(
        middle,
        vector(weights_map, prefix + "g2"),
        vector(weights_map, prefix + "b2"),
    )
    second_in = normed2.astype(jnp.bfloat16)
    hidden_pre = jnp.einsum(
        "ctd,df->ctf", second_in, weights_map[prefix + "u"], preferred_element_type=jnp.float32
    ) + vector(weights_map, prefix + "ub")
    activ, slope = gelu_and_slope(hidden_pre)
    result = (
        middle
        + jnp.einsum(
            "ctf,fd->ctd", activ, weights_map[prefix + "v"], preferred_element_type=jnp.float32
        )
        + vector(weights_map, prefix + "vb")
    )
    kept = (
        stream,
        middle,
        first_in,
        query_rows,
        key_rows,
        value_rows,
        logsum,
        mixed,
        second_in,
        slope,
        activ,
    )
    return (result, kept)


def norm_backward(stream, weights_map, gain_label, bias_label, upstream):
    pull = jax.vjp(
        layer_norm, stream, vector(weights_map, gain_label), vector(weights_map, bias_label)
    )[1]
    return pull(upstream)


def mlp_backward(upstream, kept, weights_map, prefix):
    middle, second_in, slope = kept[1], kept[8], kept[9]
    grads = {}
    branch_two = upstream.astype(jnp.bfloat16)
    grads[prefix + "vb"] = jnp.sum(branch_two.astype(jnp.float32), (0, 1))
    d_activ = jnp.einsum(
        "ctd,fd->ctf", branch_two, weights_map[prefix + "v"], preferred_element_type=jnp.float32
    )
    d_hidden = (d_activ * slope.astype(jnp.float32)).astype(jnp.bfloat16)
    grads[prefix + "ub"] = jnp.sum(d_hidden.astype(jnp.float32), (0, 1))
    d_second = jnp.einsum(
        "ctf,df->ctd", d_hidden, weights_map[prefix + "u"], preferred_element_type=jnp.float32
    )
    d_middle_part, grads[prefix + "g2"], grads[prefix + "b2"] = norm_backward(
        middle, weights_map, prefix + "g2", prefix + "b2", d_second
    )
    return upstream + d_middle_part, d_hidden, grads


def hidden_gradient(kept, d_hidden):
    return jnp.einsum("ctd,ctf->df", kept[8], d_hidden, preferred_element_type=jnp.float32)


def output_gradient(kept, upstream):
    return jnp.einsum(
        "ctf,ctd->fd", kept[10], upstream.astype(jnp.bfloat16), preferred_element_type=jnp.float32
    )


def scores_backward(d_middle, kept, weights_map, prefix, heads):
    query_rows, key_rows, value_rows, logsum = kept[3:7]
    chips, tokens, width = d_middle.shape
    branch_one = d_middle.astype(jnp.bfloat16)
    d_mixed = jnp.einsum(
        "ctd,id->cti", branch_one, weights_map[prefix + "o"], preferred_element_type=jnp.float32
    )
    d_mixed = d_mixed.astype(jnp.bfloat16).reshape(chips, tokens, heads, HD)
    scores = jnp.einsum(
        "cqhe,ckhe->chqk", query_rows, key_rows, preferred_element_type=jnp.float32
    ) * HD ** (-0.5)
    probs_full = jnp.exp(scores - logsum)
    probs_low = probs_full.astype(jnp.bfloat16)
    d_value = jnp.einsum("chqk,cqhe->ckhe", probs_low, d_mixed, preferred_element_type=jnp.float32)
    d_probs = jnp.einsum("cqhe,ckhe->chqk", d_mixed, value_rows, preferred_element_type=jnp.float32)
    row_shift = jnp.sum(d_probs * probs_full, -1, keepdims=True)
    d_scores = (probs_full * (d_probs - row_shift)).astype(jnp.bfloat16)
    return d_scores, d_value.astype(jnp.bfloat16)


def stream_backward(d_middle, d_scores, d_value, kept, weights_map, prefix, heads):
    stream, first_in, query_rows, key_rows, mixed = kept[0], kept[2], kept[3], kept[4], kept[7]
    chips, tokens, width = stream.shape
    inner = heads * HD
    grads = {}
    branch_one = d_middle.astype(jnp.bfloat16)
    grads[prefix + "ob"] = jnp.sum(branch_one.astype(jnp.float32), (0, 1))
    grads[prefix + "o"] = jnp.einsum(
        "cti,ctd->id", mixed, branch_one, preferred_element_type=jnp.float32
    )
    d_query = jnp.einsum(
        "chqk,ckhe->cqhe", d_scores, key_rows, preferred_element_type=jnp.float32
    ) * HD ** (-0.5)
    d_key = jnp.einsum(
        "chqk,cqhe->ckhe", d_scores, query_rows, preferred_element_type=jnp.float32
    ) * HD ** (-0.5)
    d_triple = jnp.concatenate(
        [
            d_query.reshape(chips, tokens, inner).astype(jnp.bfloat16),
            d_key.reshape(chips, tokens, inner).astype(jnp.bfloat16),
            d_value.reshape(chips, tokens, inner),
        ],
        -1,
    )
    grads[prefix + "qkv"] = jnp.einsum(
        "ctd,cte->de", first_in, d_triple, preferred_element_type=jnp.float32
    )
    d_first = jnp.einsum(
        "cte,de->ctd", d_triple, weights_map[prefix + "qkv"], preferred_element_type=jnp.float32
    )
    d_stream_part, grads[prefix + "g1"], grads[prefix + "b1"] = norm_backward(
        stream, weights_map, prefix + "g1", prefix + "b1", d_first
    )
    return (d_middle + d_stream_part, grads)


def per_device(patches, timeloc, visible, masked, flags, cotangent, params, moment1, moment2):
    total_rows = params.shape[0] * lax.axis_size("narrow")
    weights_map = unpack(whole_params(params), total_rows)
    chips = patches.shape[0]
    patch_ids = jnp.arange(PATCH, dtype=jnp.int32)
    chooser = visible[:, :, None] == patch_ids[None, None, :]
    choose_low = chooser.astype(jnp.bfloat16)
    choose_full = chooser.astype(jnp.float32)
    picked = jnp.einsum("cvp,cpd->cvd", choose_low, patches, preferred_element_type=jnp.float32)
    keep_meta = (1 - flags).astype(jnp.float32)
    meta_row = timeloc.astype(jnp.float32) * keep_meta[:, None]
    class_row = jnp.broadcast_to(vector(weights_map, "cls")[None, None, :], (chips, 1, DE))
    enc_in = jnp.concatenate([class_row, meta_row[:, None, :], picked], 1)
    enc_out, enc_kept = block_forward(enc_in, weights_map, "e", HE)
    patch_rows = enc_out[:, 2:, :]
    final_gain = vector(weights_map, "fg")
    final_bias = vector(weights_map, "fb")
    encoded_low = layer_norm(patch_rows, final_gain, final_bias).astype(jnp.bfloat16)
    projected = jnp.einsum(
        "cvd,de->cve", encoded_low, weights_map["proj"], preferred_element_type=jnp.float32
    ) + vector(weights_map, "pb")
    filled = jnp.einsum("cvp,cve->cpe", choose_full, projected, precision=highest)
    mask_rows = jnp.sum((masked[:, :, None] == patch_ids[None, None, :]).astype(jnp.float32), 1)
    dec_in = (
        filled
        + mask_rows[:, :, None] * vector(weights_map, "mask")[None, None, :]
        + position_table()[None]
    )
    dec_out, dec_kept = block_forward(dec_in, weights_map, "d", HDEC)
    tie = lax.optimization_barrier
    chunked = lax.axis_size("narrow") == 2 and lax.axis_size("wide") == 16
    half_rows = params.shape[0]
    cut = round_up(flat_rows()[0]["du"][0] - half_rows, 2 * BLOCK)
    top = round_up(half_rows - cut, 2 * BLOCK)
    upstream = cotangent.astype(jnp.float32)
    d_mid, d_hidden, grads = mlp_backward(upstream, dec_kept, weights_map, "d")
    grads["du"] = hidden_gradient(dec_kept, d_hidden)
    grads["dv"] = output_gradient(dec_kept, upstream)
    if chunked:
        packed = pack_chunk(grads, half_rows + cut, half_rows + cut + top)
        d_mid, e1 = tie((d_mid, packed))
        e1 = scatter_first(narrow_sum(e1))
    attention = scores_backward(d_mid, dec_kept, weights_map, "d", HDEC)
    if chunked:
        attention, d_mid, e1 = tie((attention, d_mid, e1))
        e1 = scatter_last(scatter_second(e1))
    d_dec_in, more = stream_backward(d_mid, *attention, dec_kept, weights_map, "d", HDEC)
    grads.update(more)
    grads["mask"] = jnp.sum(mask_rows[:, :, None] * d_dec_in, (0, 1))
    d_projected = jnp.einsum("cvp,cpe->cve", choose_full, d_dec_in, precision=highest).astype(
        jnp.bfloat16
    )
    grads["pb"] = jnp.sum(d_projected.astype(jnp.float32), (0, 1))
    grads["proj"] = jnp.einsum(
        "cvd,cve->de", encoded_low, d_projected, preferred_element_type=jnp.float32
    )
    d_encoded = jnp.einsum(
        "cve,de->cvd", d_projected, weights_map["proj"], preferred_element_type=jnp.float32
    )
    final_pull = jax.vjp(layer_norm, patch_rows, final_gain, final_bias)[1]
    d_patch_rows, grads["fg"], grads["fb"] = final_pull(d_encoded)
    d_enc_out = jnp.concatenate([jnp.zeros((chips, 2, DE), jnp.float32), d_patch_rows], 1)
    if chunked:
        d_enc_out, e1 = tie((d_enc_out, e1))
    grads["ev"] = output_gradient(enc_kept, d_enc_out)
    grads["evb"] = jnp.sum(d_enc_out.astype(jnp.bfloat16).astype(jnp.float32), (0, 1))
    if chunked:
        e2 = pack_chunk(grads, half_rows, half_rows + cut)
        e1 = gather_second(gather_first(e1))
        d_enc_out, e1, e2 = tie((d_enc_out, e1, e2))
        e1 = gather_last(e1)
        e2 = narrow_sum(e2)
    d_mid, d_hidden, more = mlp_backward(d_enc_out, enc_kept, weights_map, "e")
    grads.update(more)
    grads["eu"] = hidden_gradient(enc_kept, d_hidden)
    if chunked:
        d_mid, grads["eu"], e1, e2 = tie((d_mid, grads["eu"], e1, e2))
        l1 = pack_chunk(grads, cut, cut + top)
        e1 = (e1, to_owner(e1, 0))
        e2 = scatter_first(e2)
        d_mid, e1, e2, l1 = tie((d_mid, e1, e2, l1))
        e2 = scatter_last(scatter_second(e2))
        l1 = scatter_first(narrow_sum(l1))
    attention = scores_backward(d_mid, enc_kept, weights_map, "e", HE)
    if chunked:
        attention, d_mid, e2, l1 = tie((attention, d_mid, e2, l1))
        e2 = gather_first(e2)
        l1 = scatter_last(scatter_second(l1))
    d_enc_in, more = stream_backward(d_mid, *attention, enc_kept, weights_map, "e", HE)
    grads.update(more)
    grads["cls"] = jnp.sum(d_enc_in[:, 0, :], 0)
    chips_all = float(chips * lax.axis_size("wide") * lax.axis_size("narrow"))
    if chunked:
        d_enc_in, e2, l1 = tie((d_enc_in, e2, l1))
        l2 = pack_chunk(grads, 0, cut)
        e2 = gather_second(e2)
        l1 = gather_first(l1)
        d_enc_in, e2, l1, l2 = tie((d_enc_in, e2, l1, l2))
        e2 = gather_last(e2)
        l1 = gather_second(l1)
        l2 = scatter_first(narrow_sum(l2))
    patch_grad = jnp.einsum(
        "cvp,cvd->cpd", choose_full, d_enc_in[:, 2:, :], precision=highest
    ).astype(jnp.bfloat16)
    if chunked:
        patch_grad, e2, l1, l2 = tie((patch_grad, e2, l1, l2))
        e2 = (e2, to_owner(e2, 0))
        l1 = gather_last(l1)
        l2 = scatter_last(scatter_second(l2))
        e2, l1, l2 = tie((e2, l1, l2))
        l1 = (l1, to_owner(l1, 1))
        l2 = gather_first(l2)
        l1, l2 = tie((l1, l2))
        results = adam_rows((*l1, *e1), moment1, moment2, cut, half_rows - cut, (), chips_all)
        l2 = gather_last(gather_second(l2))
        l2 = (l2, to_owner(l2, 1))
        grad_out, update, new_moment1, new_moment2 = adam_rows(
            (*l2, *e2), moment1, moment2, 0, cut, results, chips_all
        )
    else:
        every = flat_gradient(grads, half_rows * lax.axis_size("narrow"))
        grad_out = sum_everywhere(every, half_rows).astype(jnp.float32) / chips_all
        update, new_moment1, new_moment2 = adam_step(grad_out, moment1, moment2)
    return (dec_out.astype(jnp.bfloat16), patch_grad, grad_out, update, new_moment1, new_moment2)


def solution(mesh):
    placed = (
        P(("wide", "narrow"), None, None),
        P(("wide", "narrow"), None),
        P(("wide", "narrow"), None),
        P(("wide", "narrow"), None),
        P(("wide", "narrow")),
        P(("wide", "narrow"), None, None),
        P("narrow", None),
        P("narrow", None),
        P("narrow", None),
    )
    return jax.shard_map(
        per_device,
        mesh=mesh,
        in_specs=placed,
        out_specs=(
            P(("wide", "narrow"), None, None),
            P(("wide", "narrow"), None, None),
            P("narrow", None),
            P("narrow", None),
            P("narrow", None),
            P("narrow", None),
        ),
        check_vma=False,
    )
```

```python
import math

import jax
import jax.numpy as jnp
from jax import lax
from jax.experimental import pallas as pl
from jax.experimental.pallas import tpu as pltpu
from jax.sharding import PartitionSpec as P

DE = 768
HE = 12
HD = 64
FE = 3072
DD = 512
HDEC = 4
FD = 2048
PATCH = 256


highest = lax.Precision.HIGHEST
first_bias_fix = 0.9999734386011124
second_bias_fix = 0.994079470779666


def block_segments(prefix, width, inner, hidden):
    names = ("g1", "b1", "qkv", "o", "ob", "g2", "b2", "u", "ub", "v", "vb")
    dims = ((width,), (width,), (width, 3 * inner), (inner, width), (width,), (width,), (width,))
    dims = (*dims, (width, hidden), (hidden,), (hidden, width), (width,))
    return [(prefix + name, size) for name, size in zip(names, dims)]


def segment_list():
    ends = (("fg", (DE,)), ("fb", (DE,)), ("proj", (DE, DD)), ("pb", (DD,)), ("mask", (DD,)))
    return [
        ("cls", (DE,)),
        *block_segments("e", DE, HE * HD, FE),
        *ends,
        *block_segments("d", DD, HDEC * HD, FD),
    ]


MARGIN = 256


def flat_rows():
    table = {}
    offset = 0
    for label, dims_of in segment_list():
        rows = math.prod(dims_of) // 128
        table[label] = (offset, rows)
        offset = offset + rows
    return table, offset


def round_up(value, unit):
    return -(-value // unit) * unit


def group_list():
    firsts = ("cls", "eo", "eu", "ev", "proj", "dqkv", "du", "dv")
    groups = []
    for label, dims in segment_list():
        if label in firsts:
            groups.append([])
        if label == "dg1" or label == "db1" or groups:
            groups[-1].append(label)
    return groups


def unpack(sources, total):
    table, used = flat_rows()
    shapes = dict(segment_list())
    groups = group_list()
    spans = [(table[g[0]][0], sum(table[g[-1]])) for g in groups]
    edges = [0, *[min(round_up(high, 16), total) for low, high in spans]]
    half = total // 2
    copies = []
    for k, (low, high) in enumerate(zip(edges, edges[1:])):
        parts = [(low, high)]
        if len(sources) == 2 and low < half < high:
            parts = [(low, half), (half, high)]
        copies.append(parts)
    slots = [(k, p) for k, parts in enumerate(copies) for p in range(len(parts))]
    labels = [label for label, dims in segment_list()]
    deepest = max(round_up(high, 16) - low // 16 * 16 for low, high in spans)

    def kernel(*refs):
        ins, rest = refs[: len(sources)], refs[len(sources) :]
        outs = dict(zip(labels, rest))
        staged, wide_rows, sems = rest[len(labels) :]

        def copy(slot, source, shift):
            k, p = slot
            low, high = copies[k][p]
            return pltpu.make_async_copy(
                source.at[pl.ds(low - shift, high - low)],
                staged.at[pl.ds(low, high - low)],
                sems.at[slots.index(slot)],
            )

        if len(sources) == 2:
            mine = lax.axis_index("narrow")
            for slot in slots:
                place = 0 if copies[slot[0]][slot[1]][0] < half else 1

                @pl.when(mine == place)
                def own_part(slot=slot, place=place):
                    copy(slot, ins[0], place * half).start()

                @pl.when(mine != place)
                def other_part(slot=slot, place=place):
                    copy(slot, ins[1], place * half).start()
        else:
            for slot in slots:
                copy(slot, ins[0], 0).start()
        for k, group in enumerate(groups):
            for p in range(len(copies[k])):
                copy((k, p), ins[0], copies[k][p][0]).wait()
            low, high = spans[k]
            origin = low // 16 * 16
            length = round_up(high, 16) - origin

            def widen(i, carry, origin=origin):
                spot = pl.multiple_of(i * 128, 128)
                wide_rows[pl.ds(spot, 128), :] = staged[
                    pl.ds(pl.multiple_of(origin + spot, 16), 128), :
                ].astype(jnp.float32)
                return carry

            lax.fori_loop(0, length // 128, widen, 0)
            done = length // 128 * 128
            if done < length:
                wide_rows[done:length, :] = staged[origin + done : origin + length, :].astype(
                    jnp.float32
                )
            for label in group:
                base = table[label][0] - origin
                dims, ref = shapes[label], outs[label]
                tiles = dims[-1] // 128
                if len(dims) == 1:
                    for c in range(tiles):
                        ref[:, c * 128 : (c + 1) * 128] = wide_rows[base + c : base + c + 1, :]
                    continue

                def step(i, carry, base=base, tiles=tiles, ref=ref):
                    for c in range(tiles):
                        rows = wide_rows[pl.ds(base + i * 16 * tiles + c, 16, stride=tiles), :]
                        ref[pl.ds(pl.multiple_of(i * 16, 16), 16), c * 128 : (c + 1) * 128] = (
                            rows.astype(jnp.bfloat16)
                        )
                    return carry

                lax.fori_loop(0, dims[0] // 16, step, 0)

    out_shape = [
        jax.ShapeDtypeStruct(dims, jnp.bfloat16)
        if len(dims) == 2
        else jax.ShapeDtypeStruct((1, dims[0]), jnp.float32)
        for label, dims in segment_list()
    ]
    outs = pl.pallas_call(
        kernel,
        out_shape=out_shape,
        in_specs=[pl.BlockSpec(memory_space=pl.ANY)] * len(sources),
        scratch_shapes=[
            pltpu.VMEM((total, 128), jnp.bfloat16),
            pltpu.VMEM((deepest, 128), jnp.float32),
            pltpu.SemaphoreType.DMA((len(slots),)),
        ],
        compiler_params=pltpu.CompilerParams(vmem_limit_bytes=61 << 20),
        name="unpack",
    )(*sources)
    return dict(zip(labels, outs))


def pack_part(pieces, low, high, first, last, held=()):
    table, used = flat_rows()
    labels = [k for k, (off, rows) in table.items() if off < high and off + rows > low]
    arrays, places = [], []
    for k in labels:
        value = pieces[k] if pieces[k].ndim == 2 else pieces[k].reshape(1, -1)
        off, rows = table[k]
        tiles = value.shape[1] // 128
        begin, end = 0, 1
        if value.shape[0] > 1:
            begin = max(0, low - off) // (8 * tiles)
            end = -(-min(rows, high - off) // (8 * tiles))
            if 3 * (end - begin) * 8 < value.shape[0]:
                value = value[begin * 8 : end * 8]
                off, end, begin = off + begin * 8 * tiles, end - begin, 0
        arrays.append(value)
        places.append((off, begin, end))
    length = high - low
    middle = (first + last) // 2
    runs = [
        (max(low, start), min(high, end), place, start)
        for place, (start, end) in enumerate(((first, middle), (middle, last)))
        if max(low, start) < min(high, end)
    ]

    def kernel(*refs):
        ins, rest = refs[: len(labels)], refs[len(labels) + len(held) :]
        kept, sent, flat, out, sems = rest
        if used < high:
            start = max(used, low) - low + MARGIN
            flat[start : MARGIN + length, :] = jnp.zeros((MARGIN + length - start, 128), jnp.float32)
        for (off, begin, end), ref in zip(places, ins):
            tiles = ref.shape[1] // 128
            base = off - low + MARGIN
            if ref.shape[0] == 1:
                for c in range(tiles):
                    spot = base + c
                    if 0 <= spot < length + 2 * MARGIN:
                        flat[spot : spot + 1, :] = ref[:, c * 128 : (c + 1) * 128]
                continue
            block = 8 * tiles

            def step(i, carry, ref=ref, tiles=tiles, base=base, block=block):
                for c in range(tiles):
                    flat[pl.ds(base + i * block + c, 8, stride=tiles), :] = ref[
                        pl.ds(pl.multiple_of(i * 8, 8), 8), c * 128 : (c + 1) * 128
                    ]
                return carry

            lax.fori_loop(begin, end, step, 0)

        def narrow_down(i, carry):
            spot = pl.multiple_of(i * 128, 128)
            out[pl.ds(spot, 128), :] = flat[pl.ds(MARGIN + spot, 128), :].astype(jnp.bfloat16)
            return carry

        lax.fori_loop(0, length // 128, narrow_down, 0)
        mine = lax.axis_index("narrow")

        def copy(n, target):
            start, end, place, origin = runs[n]
            return pltpu.make_async_copy(
                out.at[pl.ds(start - low, end - start)],
                target.at[pl.ds(start - origin, end - start)],
                sems.at[n],
            )

        for n, (start, end, place, origin) in enumerate(runs):

            @pl.when(mine == place)
            def keep(n=n):
                copy(n, kept).start()

            @pl.when(mine != place)
            def send(n=n):
                copy(n, sent).start()

        for n in range(len(runs)):
            copy(n, kept).wait()

    anywhere = pl.BlockSpec(memory_space=pl.ANY)
    whole = pl.BlockSpec(memory_space=pltpu.VMEM)
    return pl.pallas_call(
        kernel,
        out_shape=[jax.ShapeDtypeStruct((middle - first, 128), jnp.bfloat16)] * 2,
        in_specs=[whole] * len(arrays) + [anywhere] * len(held),
        out_specs=[anywhere] * 2,
        input_output_aliases={len(arrays) + n: n for n in range(len(held))},
        scratch_shapes=[
            pltpu.VMEM((length + 2 * MARGIN, 128), jnp.float32),
            pltpu.VMEM((length, 128), jnp.bfloat16),
            pltpu.SemaphoreType.DMA((len(runs),)),
        ],
        compiler_params=pltpu.CompilerParams(vmem_limit_bytes=61 << 20),
        name=f"pack{low}",
    )(*arrays, *held)


def flat_gradient(grads, unit):
    table, used = flat_rows()
    flat = jnp.concatenate([grads[k].reshape(-1) for k, dims in segment_list()])
    padding = (round_up(used, unit) - used) * 128
    flat = jnp.concatenate([flat, jnp.zeros((padding,), jnp.float32)])
    return flat.reshape(-1, 128).astype(jnp.bfloat16)


def added(first, second):
    return (first.astype(jnp.float32) + second.astype(jnp.float32)).astype(jnp.bfloat16)


def piece(value, index, rows):
    return lax.dynamic_slice_in_dim(value, index * rows, rows, 0)


class Line:
    def __init__(self, stride, size):
        self.stride, self.size, self.wide = stride, size, lax.axis_size("wide")
        self.me = (lax.axis_index("wide") // stride) % size
        self.groups = [
            [i + k * stride for k in range(size)]
            for i in range(self.wide)
            if (i // stride) % size == 0
        ]

    def swap(self, value):
        pairs = [pair for a, b in self.groups for pair in ((a, b), (b, a))]
        return lax.ppermute(value, "wide", pairs)

    def exchange(self, value):
        return lax.all_to_all(value, "wide", 0, 0, axis_index_groups=self.groups)

    def scatter(self, value):
        rows = value.shape[0] // self.size
        if self.size == 2:
            got = self.swap(piece(value, 1 - self.me, rows))
            return added(piece(value, self.me, rows), got)
        got = self.exchange(value.reshape(self.size, -1, 128)).astype(jnp.float32)
        return jnp.sum(got, 0).astype(jnp.bfloat16).reshape(rows, -1, 128)

    def gather(self, value):
        if self.size == 2:
            got = self.swap(value)
            low = self.me == 0
            return jnp.concatenate([jnp.where(low, value, got), jnp.where(low, got, value)], 0)
        copies = jnp.broadcast_to(value[None], (self.size, *value.shape))
        return self.exchange(copies).reshape(-1, *value.shape[1:])


def narrow_swap(value, step):
    count = lax.axis_size("narrow")
    return lax.ppermute(value, "narrow", [(i, (i + step) % count) for i in range(count)])


def flat3(value, places):
    return value.reshape(places, -1, 128)


def wide_lines():
    return Line(1, 2), Line(2, 2), Line(4, lax.axis_size("wide") // 4)


def staged_scatter(total):
    x, y, z = wide_lines()
    unit = lax.axis_size("wide") * 8
    most = total.shape[0] // unit * 4 // 11
    first, second = most * unit, 2 * most * unit
    a = total[:first].reshape(2, 2, z.size, -1, 128)
    b = total[first:second].reshape(2, 2, z.size, -1, 128)
    c = total[second:].reshape(z.size, 2, 2, -1, 128)
    c = z.scatter(flat3(c, z.size))
    a = x.scatter(flat3(a, 2))
    b = y.scatter(flat3(b, 2))
    a = y.scatter(flat3(a, 2))
    b = x.scatter(flat3(b, 2))
    a, b, c = lax.optimization_barrier((a, b, c))
    ab = z.scatter(jnp.concatenate([flat3(a, z.size), flat3(b, z.size)], 1))
    c = x.scatter(flat3(c, 2))
    c = y.scatter(flat3(c, 2))
    return lax.optimization_barrier((ab, c))


def staged_gather(ab, c):
    x, y, z = wide_lines()
    ab = z.gather(flat3(ab, 1))
    c = x.gather(y.gather(flat3(c, 1)))
    ab, c = lax.optimization_barrier((ab, c))
    half = ab.shape[1] // 2
    a, b = ab[:, :half], ab[:, half:]
    c = z.gather(flat3(c, 1))
    a = y.gather(flat3(a, 1))
    b = x.gather(flat3(b, 1))
    a = x.gather(flat3(a, 1))
    b = y.gather(flat3(b, 1))
    return jnp.concatenate([v.reshape(-1, 128) for v in (a, b, c)], 0)


def narrow_sum(halves):
    return added(halves[0], narrow_swap(halves[1], 1))


def sum_everywhere(value, rows):
    count = lax.axis_size("narrow")
    mine = lax.axis_index("narrow")
    total = lax.dynamic_slice_in_dim(value, mine * rows, rows, 0)
    for step in range(1, count):
        other = lax.dynamic_slice_in_dim(value, (mine + step) % count * rows, rows, 0)
        total = added(total, narrow_swap(other, step))
    unit = lax.axis_size("wide") * 16
    total = jnp.pad(total, ((0, round_up(rows, unit) - rows), (0, 0)))
    return staged_gather(*staged_scatter(total))[:rows]


BLOCK = 2496


def adam_rows(parts, moment1, moment2, start, rows, held, chips_all):
    half = parts[0].shape[0] // BLOCK
    shift = start // BLOCK
    steps = -(-rows // BLOCK)

    def kernel(core, own_low, got_low, own_high, got_high, first, second, *rest):
        grad_out, update, new_first, new_second = rest[len(held) :]
        early = pl.program_id(0) < half
        low = jnp.where(early, own_low[...], got_low[...])
        high = jnp.where(early, got_high[...], own_high[...])
        grad = jnp.where(core[0] == 0, low, high).astype(jnp.float32) / chips_all
        grad_out[...] = grad
        update[...], new_first[...], new_second[...] = adam_step(grad, first[...], second[...])

    def early_rows(place):
        return lambda i, core: (jnp.where(core[0] == place, jnp.minimum(i, half - 1), 0), 0)

    def late_rows(place):
        return lambda i, core: (jnp.where(core[0] == place, jnp.maximum(i - half, 0), 0), 0)

    def spec(index_map):
        return pl.BlockSpec((BLOCK, 128), index_map)

    here = spec(lambda i, core: (i + shift, 0))
    maps = (early_rows(0), late_rows(0), late_rows(1), early_rows(1))
    core = lax.axis_index("narrow").astype(jnp.int32).reshape(1)
    return pl.pallas_call(
        kernel,
        out_shape=[jax.ShapeDtypeStruct(moment1.shape, jnp.float32)] * 4,
        grid_spec=pltpu.PrefetchScalarGridSpec(
            num_scalar_prefetch=1,
            grid=(steps,),
            in_specs=[*[spec(m) for m in maps], here, here]
            + [pl.BlockSpec(memory_space=pl.ANY)] * len(held),
            out_specs=[here] * 4,
        ),
        input_output_aliases={7 + n: n for n in range(len(held))},
        name=f"adam{start}",
    )(core, *parts, moment1, moment2, *held)


def to_owner(value, source):
    return lax.ppermute(value, "narrow", [(source, 1 - source)])


def whole_params(params):
    low_params = params.astype(jnp.bfloat16)
    if lax.axis_size("narrow") == 2:
        return (low_params, narrow_swap(low_params, 1))
    return (lax.all_gather(low_params, "narrow", axis=0, tiled=True),)


def position_table():
    half_width = DD // 2
    places = jnp.arange(PATCH, dtype=jnp.float32)[:, None]
    rates = jnp.exp(jnp.arange(half_width, dtype=jnp.float32) * (-math.log(10000.0) / half_width))
    angles = places * rates[None, :]
    return jnp.concatenate([jnp.sin(angles), jnp.cos(angles)], 1)


def layer_norm(stream, gain_vec, bias_vec):
    average = jnp.mean(stream, -1, keepdims=True)
    centred = stream - average
    spread = jnp.mean(centred * centred, -1, keepdims=True)
    return centred * lax.rsqrt(spread + 1e-05) * gain_vec + bias_vec


def vector(weights_map, label):
    return weights_map[label].reshape(-1)


def adam_step(grads, moment1, moment2):
    new_first = 0.9 * moment1 + (1.0 - 0.9) * grads
    new_second = 0.95 * moment2 + (1.0 - 0.95) * grads * grads
    update = new_first / first_bias_fix / (jnp.sqrt(new_second / second_bias_fix) + 1e-08)
    return (update, new_first, new_second)


tail_terms = (
    0.05025708328,
    -0.1828833063,
    0.1690591746,
    -0.005588040603,
    0.141423544,
    0.1685436795,
    0.2078425222,
    0.2256696051,
    0.2256758619,
)


def gelu_and_slope(u):
    t = 1.0 / (1.0 + (0.4 * math.sqrt(0.5)) * jnp.abs(u))
    bell = jnp.exp(-0.5 * u * u)
    tail = 0.5 * tail_terms[0]
    for term in tail_terms[1:]:
        tail = tail * t + 0.5 * term
    tail = tail * t * bell
    below = jnp.where(u < 0, tail, 1.0 - tail)
    slope = below + u * bell * (1.0 / math.sqrt(2.0 * math.pi))
    return (u * below).astype(jnp.bfloat16), slope.astype(jnp.bfloat16)


def block_forward(stream, weights_map, prefix, heads):
    chips, tokens, width = stream.shape
    inner = heads * HD
    normed1 = layer_norm(
        stream,
        vector(weights_map, prefix + "g1"),
        vector(weights_map, prefix + "b1"),
    )
    first_in = normed1.astype(jnp.bfloat16)
    triple = jnp.einsum(
        "ctd,de->cte", first_in, weights_map[prefix + "qkv"], preferred_element_type=jnp.float32
    ).astype(jnp.bfloat16)
    query_rows = triple[:, :, :inner].reshape(chips, tokens, heads, HD)
    key_rows = triple[:, :, inner : 2 * inner].reshape(chips, tokens, heads, HD)
    value_rows = triple[:, :, 2 * inner :].reshape(chips, tokens, heads, HD)
    scores = jnp.einsum(
        "cqhe,ckhe->chqk", query_rows, key_rows, preferred_element_type=jnp.float32
    ) * HD ** (-0.5)
    topmost = jnp.max(scores, -1, keepdims=True)
    expos = jnp.exp(scores - topmost)
    totals = jnp.sum(expos, -1, keepdims=True)
    logsum = topmost + jnp.log(totals)
    probs = (expos / totals).astype(jnp.bfloat16)
    mixed = jnp.einsum("chqk,ckhe->cqhe", probs, value_rows, preferred_element_type=jnp.float32)
    mixed = mixed.reshape(chips, tokens, inner).astype(jnp.bfloat16)
    middle = (
        stream
        + jnp.einsum(
            "cti,id->ctd", mixed, weights_map[prefix + "o"], preferred_element_type=jnp.float32
        )
        + vector(weights_map, prefix + "ob")
    )
    normed2 = layer_norm(
        middle,
        vector(weights_map, prefix + "g2"),
        vector(weights_map, prefix + "b2"),
    )
    second_in = normed2.astype(jnp.bfloat16)
    hidden_pre = jnp.einsum(
        "ctd,df->ctf", second_in, weights_map[prefix + "u"], preferred_element_type=jnp.float32
    ) + vector(weights_map, prefix + "ub")
    activ, slope = gelu_and_slope(hidden_pre)
    result = (
        middle
        + jnp.einsum(
            "ctf,fd->ctd", activ, weights_map[prefix + "v"], preferred_element_type=jnp.float32
        )
        + vector(weights_map, prefix + "vb")
    )
    kept = (
        stream,
        middle,
        first_in,
        query_rows,
        key_rows,
        value_rows,
        logsum,
        mixed,
        second_in,
        slope,
        activ,
    )
    return (result, kept)


def norm_backward(stream, weights_map, gain_label, bias_label, upstream):
    pull = jax.vjp(
        layer_norm, stream, vector(weights_map, gain_label), vector(weights_map, bias_label)
    )[1]
    return pull(upstream)


def mlp_backward(upstream, kept, weights_map, prefix):
    middle, second_in, slope = kept[1], kept[8], kept[9]
    grads = {}
    branch_two = upstream.astype(jnp.bfloat16)
    grads[prefix + "vb"] = jnp.sum(branch_two.astype(jnp.float32), (0, 1))
    d_activ = jnp.einsum(
        "ctd,fd->ctf", branch_two, weights_map[prefix + "v"], preferred_element_type=jnp.float32
    )
    d_hidden = (d_activ * slope.astype(jnp.float32)).astype(jnp.bfloat16)
    grads[prefix + "ub"] = jnp.sum(d_hidden.astype(jnp.float32), (0, 1))
    d_second = jnp.einsum(
        "ctf,df->ctd", d_hidden, weights_map[prefix + "u"], preferred_element_type=jnp.float32
    )
    d_middle_part, grads[prefix + "g2"], grads[prefix + "b2"] = norm_backward(
        middle, weights_map, prefix + "g2", prefix + "b2", d_second
    )
    return upstream + d_middle_part, d_hidden, grads


def hidden_gradient(kept, d_hidden):
    return jnp.einsum("ctd,ctf->df", kept[8], d_hidden, preferred_element_type=jnp.float32)


def output_gradient(kept, upstream):
    return jnp.einsum(
        "ctf,ctd->fd", kept[10], upstream.astype(jnp.bfloat16), preferred_element_type=jnp.float32
    )


def scores_backward(d_middle, kept, weights_map, prefix, heads):
    query_rows, key_rows, value_rows, logsum = kept[3:7]
    chips, tokens, width = d_middle.shape
    branch_one = d_middle.astype(jnp.bfloat16)
    d_mixed = jnp.einsum(
        "ctd,id->cti", branch_one, weights_map[prefix + "o"], preferred_element_type=jnp.float32
    )
    d_mixed = d_mixed.astype(jnp.bfloat16).reshape(chips, tokens, heads, HD)
    scores = jnp.einsum(
        "cqhe,ckhe->chqk", query_rows, key_rows, preferred_element_type=jnp.float32
    ) * HD ** (-0.5)
    probs_full = jnp.exp(scores - logsum)
    probs_low = probs_full.astype(jnp.bfloat16)
    d_value = jnp.einsum("chqk,cqhe->ckhe", probs_low, d_mixed, preferred_element_type=jnp.float32)
    d_probs = jnp.einsum("cqhe,ckhe->chqk", d_mixed, value_rows, preferred_element_type=jnp.float32)
    row_shift = jnp.sum(d_probs * probs_full, -1, keepdims=True)
    d_scores = (probs_full * (d_probs - row_shift)).astype(jnp.bfloat16)
    return d_scores, d_value.astype(jnp.bfloat16)


def stream_backward(d_middle, d_scores, d_value, kept, weights_map, prefix, heads):
    stream, first_in, query_rows, key_rows, mixed = kept[0], kept[2], kept[3], kept[4], kept[7]
    chips, tokens, width = stream.shape
    inner = heads * HD
    grads = {}
    branch_one = d_middle.astype(jnp.bfloat16)
    grads[prefix + "ob"] = jnp.sum(branch_one.astype(jnp.float32), (0, 1))
    grads[prefix + "o"] = jnp.einsum(
        "cti,ctd->id", mixed, branch_one, preferred_element_type=jnp.float32
    )
    d_query = jnp.einsum(
        "chqk,ckhe->cqhe", d_scores, key_rows, preferred_element_type=jnp.float32
    ) * HD ** (-0.5)
    d_key = jnp.einsum(
        "chqk,cqhe->ckhe", d_scores, query_rows, preferred_element_type=jnp.float32
    ) * HD ** (-0.5)
    d_triple = jnp.concatenate(
        [
            d_query.reshape(chips, tokens, inner).astype(jnp.bfloat16),
            d_key.reshape(chips, tokens, inner).astype(jnp.bfloat16),
            d_value.reshape(chips, tokens, inner),
        ],
        -1,
    )
    grads[prefix + "qkv"] = jnp.einsum(
        "ctd,cte->de", first_in, d_triple, preferred_element_type=jnp.float32
    )
    d_first = jnp.einsum(
        "cte,de->ctd", d_triple, weights_map[prefix + "qkv"], preferred_element_type=jnp.float32
    )
    d_stream_part, grads[prefix + "g1"], grads[prefix + "b1"] = norm_backward(
        stream, weights_map, prefix + "g1", prefix + "b1", d_first
    )
    return (d_middle + d_stream_part, grads)


def per_device(patches, timeloc, visible, masked, flags, cotangent, params, moment1, moment2):
    total_rows = params.shape[0] * lax.axis_size("narrow")
    weights_map = unpack(whole_params(params), total_rows)
    chips = patches.shape[0]
    patch_ids = jnp.arange(PATCH, dtype=jnp.int32)
    chooser = visible[:, :, None] == patch_ids[None, None, :]
    choose_low = chooser.astype(jnp.bfloat16)
    choose_full = chooser.astype(jnp.float32)
    picked = jnp.einsum("cvp,cpd->cvd", choose_low, patches, preferred_element_type=jnp.float32)
    keep_meta = (1 - flags).astype(jnp.float32)
    meta_row = timeloc.astype(jnp.float32) * keep_meta[:, None]
    class_row = jnp.broadcast_to(vector(weights_map, "cls")[None, None, :], (chips, 1, DE))
    enc_in = jnp.concatenate([class_row, meta_row[:, None, :], picked], 1)
    enc_out, enc_kept = block_forward(enc_in, weights_map, "e", HE)
    patch_rows = enc_out[:, 2:, :]
    final_gain = vector(weights_map, "fg")
    final_bias = vector(weights_map, "fb")
    encoded_low = layer_norm(patch_rows, final_gain, final_bias).astype(jnp.bfloat16)
    projected = jnp.einsum(
        "cvd,de->cve", encoded_low, weights_map["proj"], preferred_element_type=jnp.float32
    ) + vector(weights_map, "pb")
    filled = jnp.einsum("cvp,cve->cpe", choose_full, projected, precision=highest)
    mask_rows = 1.0 - jnp.sum(choose_full, 1)
    dec_in = (
        filled
        + mask_rows[:, :, None] * vector(weights_map, "mask")[None, None, :]
        + position_table()[None]
    )
    dec_out, dec_kept = block_forward(dec_in, weights_map, "d", HDEC)
    tie = lax.optimization_barrier
    chunked = lax.axis_size("narrow") == 2 and lax.axis_size("wide") == 16
    half_rows = params.shape[0]
    padded = round_up(half_rows, 512)
    upper = (half_rows, half_rows + padded)
    upstream = cotangent.astype(jnp.float32)
    d_mid, d_hidden, grads = mlp_backward(upstream, dec_kept, weights_map, "d")
    grads["du"] = hidden_gradient(dec_kept, d_hidden)
    grads["dv"] = output_gradient(dec_kept, upstream)
    if chunked:
        cut = round_up(flat_rows()[0]["du"][0], 128)
        held = pack_part(grads, cut, upper[1], *upper)
        d_mid, held = tie((d_mid, held))
    attention = scores_backward(d_mid, dec_kept, weights_map, "d", HDEC)
    d_dec_in, more = stream_backward(d_mid, *attention, dec_kept, weights_map, "d", HDEC)
    grads.update(more)
    grads["mask"] = jnp.sum(mask_rows[:, :, None] * d_dec_in, (0, 1))
    d_projected = jnp.einsum("cvp,cpe->cve", choose_full, d_dec_in, precision=highest).astype(
        jnp.bfloat16
    )
    grads["pb"] = jnp.sum(d_projected.astype(jnp.float32), (0, 1))
    grads["proj"] = jnp.einsum(
        "cvd,cve->de", encoded_low, d_projected, preferred_element_type=jnp.float32
    )
    d_encoded = jnp.einsum(
        "cve,de->cvd", d_projected, weights_map["proj"], preferred_element_type=jnp.float32
    )
    final_pull = jax.vjp(layer_norm, patch_rows, final_gain, final_bias)[1]
    d_patch_rows, grads["fg"], grads["fb"] = final_pull(d_encoded)
    d_enc_out = jnp.concatenate([jnp.zeros((chips, 2, DE), jnp.float32), d_patch_rows], 1)
    grads["ev"] = output_gradient(enc_kept, d_enc_out)
    grads["evb"] = jnp.sum(d_enc_out.astype(jnp.bfloat16).astype(jnp.float32), (0, 1))
    if chunked:
        high = pack_part(grads, half_rows, cut, *upper, held)
        d_enc_out, high = tie((d_enc_out, high))
        high = lax.psum_scatter(narrow_sum(high), "wide", scatter_dimension=0, tiled=True)
    d_mid, d_hidden, more = mlp_backward(d_enc_out, enc_kept, weights_map, "e")
    grads.update(more)
    grads["eu"] = hidden_gradient(enc_kept, d_hidden)
    if chunked:
        cut = round_up(flat_rows()[0]["eu"][0], 128)
        held = pack_part(grads, cut, padded, 0, padded)
        d_mid, held = tie((d_mid, held))
    attention = scores_backward(d_mid, enc_kept, weights_map, "e", HE)
    d_enc_in, more = stream_backward(d_mid, *attention, enc_kept, weights_map, "e", HE)
    grads.update(more)
    grads["cls"] = jnp.sum(d_enc_in[:, 0, :], 0)
    chips_all = float(chips * lax.axis_size("wide") * lax.axis_size("narrow"))
    if chunked:
        low = pack_part(grads, 0, cut, 0, padded, held)
        d_enc_in, high, low = tie((d_enc_in, high, low))
        high = lax.all_gather(high, "wide", axis=0, tiled=True)
    patch_grad = jnp.einsum(
        "cvp,cvd->cpd", choose_full, d_enc_in[:, 2:, :], precision=highest
    ).astype(jnp.bfloat16)
    if chunked:
        low = staged_gather(*staged_scatter(narrow_sum(low)))
        parts = (low, to_owner(low, 1), high, to_owner(high, 0))
        grad_out, update, new_moment1, new_moment2 = adam_rows(
            parts, moment1, moment2, 0, half_rows, (), chips_all
        )
    else:
        every = flat_gradient(grads, half_rows * lax.axis_size("narrow"))
        grad_out = sum_everywhere(every, half_rows).astype(jnp.float32) / chips_all
        update, new_moment1, new_moment2 = adam_step(grad_out, moment1, moment2)
    return (dec_out.astype(jnp.bfloat16), patch_grad, grad_out, update, new_moment1, new_moment2)


def solution(mesh):
    placed = (
        P(("wide", "narrow"), None, None),
        P(("wide", "narrow"), None),
        P(("wide", "narrow"), None),
        P(("wide", "narrow"), None),
        P(("wide", "narrow")),
        P(("wide", "narrow"), None, None),
        P("narrow", None),
        P("narrow", None),
        P("narrow", None),
    )
    return jax.shard_map(
        per_device,
        mesh=mesh,
        in_specs=placed,
        out_specs=(
            P(("wide", "narrow"), None, None),
            P(("wide", "narrow"), None, None),
            P("narrow", None),
            P("narrow", None),
            P("narrow", None),
            P("narrow", None),
        ),
        check_vma=False,
    )
```

```python
import math

import jax
import jax.numpy as jnp
from jax import lax
from jax.experimental import pallas as pl
from jax.experimental.pallas import tpu as pltpu
from jax.sharding import PartitionSpec as P

DE = 768
HE = 12
HD = 64
FE = 3072
DD = 512
HDEC = 4
FD = 2048
PATCH = 256


highest = lax.Precision.HIGHEST
first_bias_fix = 0.9999734386011124
second_bias_fix = 0.994079470779666


def block_segments(prefix, width, inner, hidden):
    names = ("g1", "b1", "qkv", "o", "ob", "g2", "b2", "u", "ub", "v", "vb")
    dims = ((width,), (width,), (width, 3 * inner), (inner, width), (width,), (width,), (width,))
    dims = (*dims, (width, hidden), (hidden,), (hidden, width), (width,))
    return [(prefix + name, size) for name, size in zip(names, dims)]


def segment_list():
    ends = (("fg", (DE,)), ("fb", (DE,)), ("proj", (DE, DD)), ("pb", (DD,)), ("mask", (DD,)))
    return [
        ("cls", (DE,)),
        *block_segments("e", DE, HE * HD, FE),
        *ends,
        *block_segments("d", DD, HDEC * HD, FD),
    ]


MARGIN = 512


def flat_rows():
    table = {}
    offset = 0
    for label, dims_of in segment_list():
        rows = math.prod(dims_of) // 128
        table[label] = (offset, rows)
        offset = offset + rows
    return table, offset


def round_up(value, unit):
    return -(-value // unit) * unit


def group_list():
    firsts = ("cls", "eo", "eu", "ev", "proj", "dqkv", "du", "dv")
    groups = []
    for label, dims in segment_list():
        if label in firsts:
            groups.append([])
        if label == "dg1" or label == "db1" or groups:
            groups[-1].append(label)
    return groups


def unpack(sources, total):
    table, used = flat_rows()
    shapes = dict(segment_list())
    groups = group_list()
    spans = [(table[g[0]][0], sum(table[g[-1]])) for g in groups]
    edges = [0, *[min(round_up(high, 16), total) for low, high in spans]]
    half = total // 2
    copies = []
    for k, (low, high) in enumerate(zip(edges, edges[1:])):
        parts = [(low, high)]
        if len(sources) == 2 and low < half < high:
            parts = [(low, half), (half, high)]
        copies.append(parts)
    slots = [(k, p) for k, parts in enumerate(copies) for p in range(len(parts))]
    labels = [label for label, dims in segment_list()]
    matrices = [label for label, dims in segment_list() if len(dims) == 2]
    deepest = max(round_up(high, 16) - low // 16 * 16 for low, high in spans)

    def kernel(*refs):
        ins, rest = refs[: len(sources)], refs[len(sources) :]
        finals = dict(zip(labels, rest))
        staged, wide_rows, sems, *own, out_sems = rest[len(labels) :]
        outs = {**finals, **dict(zip(matrices, own))}

        def leave(label):
            return pltpu.make_async_copy(
                outs[label], finals[label], out_sems.at[matrices.index(label)]
            )

        def copy(slot, source, shift):
            k, p = slot
            low, high = copies[k][p]
            return pltpu.make_async_copy(
                source.at[pl.ds(low - shift, high - low)],
                staged.at[pl.ds(low, high - low)],
                sems.at[slots.index(slot)],
            )

        if len(sources) == 2:
            mine = lax.axis_index("narrow")
            for slot in slots:
                place = 0 if copies[slot[0]][slot[1]][0] < half else 1

                @pl.when(mine == place)
                def own_part(slot=slot, place=place):
                    copy(slot, ins[0], place * half).start()

                @pl.when(mine != place)
                def other_part(slot=slot, place=place):
                    copy(slot, ins[1], place * half).start()
        else:
            for slot in slots:
                copy(slot, ins[0], 0).start()
        for k, group in enumerate(groups):
            for p in range(len(copies[k])):
                copy((k, p), ins[0], copies[k][p][0]).wait()
            low, high = spans[k]
            origin = low // 16 * 16
            length = round_up(high, 16) - origin

            def widen(i, carry, origin=origin):
                spot = pl.multiple_of(i * 128, 128)
                wide_rows[pl.ds(spot, 128), :] = staged[
                    pl.ds(pl.multiple_of(origin + spot, 16), 128), :
                ].astype(jnp.float32)
                return carry

            lax.fori_loop(0, length // 128, widen, 0)
            done = length // 128 * 128
            if done < length:
                wide_rows[done:length, :] = staged[origin + done : origin + length, :].astype(
                    jnp.float32
                )
            for label in group:
                base = table[label][0] - origin
                dims, ref = shapes[label], outs[label]
                tiles = dims[-1] // 128
                if len(dims) == 1:
                    for c in range(tiles):
                        ref[:, c * 128 : (c + 1) * 128] = wide_rows[base + c : base + c + 1, :]
                    continue

                def step(i, carry, base=base, tiles=tiles, ref=ref):
                    for c in range(tiles):
                        rows = wide_rows[pl.ds(base + i * 16 * tiles + c, 16, stride=tiles), :]
                        ref[pl.ds(pl.multiple_of(i * 16, 16), 16), c * 128 : (c + 1) * 128] = (
                            rows.astype(jnp.bfloat16)
                        )
                    return carry

                lax.fori_loop(0, dims[0] // 16, step, 0)
                leave(label).start()
        for label in matrices:
            leave(label).wait()

    out_shape = [
        jax.ShapeDtypeStruct(dims, jnp.bfloat16)
        if len(dims) == 2
        else jax.ShapeDtypeStruct((1, dims[0]), jnp.float32)
        for label, dims in segment_list()
    ]
    outs = pl.pallas_call(
        kernel,
        out_shape=out_shape,
        in_specs=[pl.BlockSpec(memory_space=pl.ANY)] * len(sources),
        out_specs=[
            pl.BlockSpec(memory_space=pl.ANY if label in matrices else pltpu.VMEM)
            for label in labels
        ],
        scratch_shapes=[
            pltpu.VMEM((total, 128), jnp.bfloat16),
            pltpu.VMEM((deepest, 128), jnp.float32),
            pltpu.SemaphoreType.DMA((len(slots),)),
            *[pltpu.VMEM(shapes[label], jnp.bfloat16) for label in matrices],
            pltpu.SemaphoreType.DMA((len(matrices),)),
        ],
        compiler_params=pltpu.CompilerParams(vmem_limit_bytes=61 << 20),
        name="unpack",
    )(*sources)
    return dict(zip(labels, outs))


def pack_part(pieces, low, high, first, last, held=()):
    table, used = flat_rows()
    labels = [k for k, (off, rows) in table.items() if off < high and off + rows > low]
    arrays, places = [], []
    for k in labels:
        value = pieces[k] if pieces[k].ndim == 2 else pieces[k].reshape(1, -1)
        off, rows = table[k]
        tiles = value.shape[1] // 128
        begin, end = 0, 1
        if value.shape[0] > 1:
            begin = max(0, low - off) // (16 * tiles)
            end = -(-min(rows, high - off) // (16 * tiles))
            if 3 * (end - begin) * 16 < value.shape[0]:
                value = value[begin * 16 : end * 16]
                off, end, begin = off + begin * 16 * tiles, end - begin, 0
        arrays.append(value)
        places.append((off, begin, end))
    length = high - low
    middle = (first + last) // 2
    runs = [
        (max(low, start), min(high, end), place, start)
        for place, (start, end) in enumerate(((first, middle), (middle, last)))
        if max(low, start) < min(high, end)
    ]

    def kernel(*refs):
        ins, rest = refs[: len(labels)], refs[len(labels) + len(held) :]
        kept, sent, flat, out, sems = rest
        if used < high:
            start = max(used, low) - low + MARGIN
            flat[start : MARGIN + length, :] = jnp.zeros((MARGIN + length - start, 128), jnp.float32)
        for (off, begin, end), ref in zip(places, ins):
            tiles = ref.shape[1] // 128
            base = off - low + MARGIN
            if ref.shape[0] == 1:
                for c in range(tiles):
                    spot = base + c
                    if 0 <= spot < length + 2 * MARGIN:
                        flat[spot : spot + 1, :] = ref[:, c * 128 : (c + 1) * 128]
                continue
            block = 16 * tiles

            def step(i, carry, ref=ref, tiles=tiles, base=base, block=block):
                for c in range(tiles):
                    rows = ref[pl.ds(pl.multiple_of(i * 16, 16), 16), c * 128 : (c + 1) * 128]
                    flat[pl.ds(base + i * block + c, 16, stride=tiles), :] = rows.astype(jnp.float32)
                return carry

            lax.fori_loop(begin, end, step, 0)

        def narrow_down(i, carry):
            spot = pl.multiple_of(i * 128, 128)
            out[pl.ds(spot, 128), :] = flat[pl.ds(MARGIN + spot, 128), :].astype(jnp.bfloat16)
            return carry

        lax.fori_loop(0, length // 128, narrow_down, 0)
        mine = lax.axis_index("narrow")

        def copy(n, target):
            start, end, place, origin = runs[n]
            return pltpu.make_async_copy(
                out.at[pl.ds(start - low, end - start)],
                target.at[pl.ds(start - origin, end - start)],
                sems.at[n],
            )

        for n, (start, end, place, origin) in enumerate(runs):

            @pl.when(mine == place)
            def keep(n=n):
                copy(n, kept).start()

            @pl.when(mine != place)
            def send(n=n):
                copy(n, sent).start()

        for n in range(len(runs)):
            copy(n, kept).wait()

    anywhere = pl.BlockSpec(memory_space=pl.ANY)
    whole = pl.BlockSpec(memory_space=pltpu.VMEM)
    return pl.pallas_call(
        kernel,
        out_shape=[jax.ShapeDtypeStruct((middle - first, 128), jnp.bfloat16)] * 2,
        in_specs=[whole] * len(arrays) + [anywhere] * len(held),
        out_specs=[anywhere] * 2,
        input_output_aliases={len(arrays) + n: n for n in range(len(held))},
        scratch_shapes=[
            pltpu.VMEM((length + 2 * MARGIN, 128), jnp.float32),
            pltpu.VMEM((length, 128), jnp.bfloat16),
            pltpu.SemaphoreType.DMA((len(runs),)),
        ],
        compiler_params=pltpu.CompilerParams(vmem_limit_bytes=61 << 20),
        name=f"pack{low}",
    )(*arrays, *held)


def flat_gradient(grads, unit):
    table, used = flat_rows()
    flat = jnp.concatenate([grads[k].astype(jnp.bfloat16).reshape(-1) for k, dims in segment_list()])
    padding = (round_up(used, unit) - used) * 128
    flat = jnp.concatenate([flat, jnp.zeros((padding,), jnp.bfloat16)])
    return flat.reshape(-1, 128)


def added(first, second):
    return (first.astype(jnp.float32) + second.astype(jnp.float32)).astype(jnp.bfloat16)


def piece(value, index, rows):
    return lax.dynamic_slice_in_dim(value, index * rows, rows, 0)


class Line:
    def __init__(self, stride, size):
        self.stride, self.size, self.wide = stride, size, lax.axis_size("wide")
        self.me = (lax.axis_index("wide") // stride) % size
        self.groups = [
            [i + k * stride for k in range(size)]
            for i in range(self.wide)
            if (i // stride) % size == 0
        ]

    def swap(self, value):
        pairs = [pair for a, b in self.groups for pair in ((a, b), (b, a))]
        return lax.ppermute(value, "wide", pairs)

    def exchange(self, value):
        return lax.all_to_all(value, "wide", 0, 0, axis_index_groups=self.groups)

    def scatter(self, value):
        rows = value.shape[0] // self.size
        if self.size == 2:
            got = self.swap(piece(value, 1 - self.me, rows))
            return added(piece(value, self.me, rows), got)
        got = self.exchange(value.reshape(self.size, -1, 128)).astype(jnp.float32)
        return jnp.sum(got, 0).astype(jnp.bfloat16).reshape(rows, -1, 128)

    def gather(self, value):
        if self.size == 2:
            got = self.swap(value)
            low = self.me == 0
            return jnp.concatenate([jnp.where(low, value, got), jnp.where(low, got, value)], 0)
        copies = jnp.broadcast_to(value[None], (self.size, *value.shape))
        return self.exchange(copies).reshape(-1, *value.shape[1:])


def narrow_swap(value, step):
    count = lax.axis_size("narrow")
    return lax.ppermute(value, "narrow", [(i, (i + step) % count) for i in range(count)])


def flat3(value, places):
    return value.reshape(places, -1, 128)


def wide_lines():
    return Line(1, 2), Line(2, 2), Line(4, lax.axis_size("wide") // 4)


def staged_scatter(total, beside=()):
    x, y, z = wide_lines()
    unit = lax.axis_size("wide") * 8
    most = total.shape[0] // unit * 4 // 11
    first, second = most * unit, 2 * most * unit
    a = total[:first].reshape(2, 2, z.size, -1, 128)
    b = total[first:second].reshape(2, 2, z.size, -1, 128)
    c = total[second:].reshape(z.size, 2, 2, -1, 128)
    c = z.scatter(flat3(c, z.size))
    a = x.scatter(flat3(a, 2))
    b = y.scatter(flat3(b, 2))
    a = y.scatter(flat3(a, 2))
    b = x.scatter(flat3(b, 2))
    a, b, c, beside = lax.optimization_barrier((a, b, c, beside))
    ab = z.scatter(jnp.concatenate([flat3(a, z.size), flat3(b, z.size)], 1))
    c = x.scatter(flat3(c, 2))
    c = y.scatter(flat3(c, 2))
    return lax.optimization_barrier((ab, c)), beside


def staged_gather(ab, c):
    x, y, z = wide_lines()
    ab = z.gather(flat3(ab, 1))
    c = x.gather(y.gather(flat3(c, 1)))
    ab, c = lax.optimization_barrier((ab, c))
    half = ab.shape[1] // 2
    a, b = ab[:, :half], ab[:, half:]
    c = z.gather(flat3(c, 1))
    a = y.gather(flat3(a, 1)).reshape(-1, 128)
    b = x.gather(flat3(b, 1)).reshape(-1, 128)
    return join_pieces((x, a, x.swap(a)), (y, b, y.swap(b)), c.reshape(-1, 128))


def join_pieces(first, second, third):
    pairs = (first, second)
    sizes = [2 * own.shape[0] for line, own, other in pairs]

    def kernel(own1, other1, own2, other2, last, out, sems):
        copies = []
        start = 0
        for (line, own, other), refs in zip(pairs, ((own1, other1), (own2, other2))):
            rows = own.shape[0]
            me = (lax.axis_index("wide") // line.stride) % 2
            for ref, place in zip(refs, (me, 1 - me)):
                copies.append((ref, pl.multiple_of(start + place * rows, 8), rows))
            start += 2 * rows
        copies.append((last, start, third.shape[0]))
        copies = [
            pltpu.make_async_copy(ref, out.at[pl.ds(spot, rows)], sems.at[n])
            for n, (ref, spot, rows) in enumerate(copies)
        ]
        for copy in copies:
            copy.start()
        for copy in copies:
            copy.wait()

    anywhere = pl.BlockSpec(memory_space=pl.ANY)
    return pl.pallas_call(
        kernel,
        out_shape=jax.ShapeDtypeStruct((sum(sizes) + third.shape[0], 128), third.dtype),
        in_specs=[anywhere] * 5,
        out_specs=anywhere,
        scratch_shapes=[pltpu.SemaphoreType.DMA((5,))],
        name="join",
    )(first[1], first[2], second[1], second[2], third)


def narrow_sum(halves):
    return added(halves[0], narrow_swap(halves[1], 1))


def sum_everywhere(value, rows):
    count = lax.axis_size("narrow")
    mine = lax.axis_index("narrow")
    total = lax.dynamic_slice_in_dim(value, mine * rows, rows, 0)
    for step in range(1, count):
        other = lax.dynamic_slice_in_dim(value, (mine + step) % count * rows, rows, 0)
        total = added(total, narrow_swap(other, step))
    unit = lax.axis_size("wide") * 16
    total = jnp.pad(total, ((0, round_up(rows, unit) - rows), (0, 0)))
    return staged_gather(*staged_scatter(total)[0])[:rows]


BLOCK = 2496


def adam_rows(low, high, moment1, moment2, start, held, chips_all):
    shift = start // BLOCK
    steps = -(-min(low.shape[0], moment1.shape[0] - start) // BLOCK)

    def kernel(core, low_rows, high_rows, first, second, *rest):
        grad_out, update, new_first, new_second = rest[len(held) :]
        grad = jnp.where(core[0] == 0, low_rows[...], high_rows[...].reshape(BLOCK, 128))
        grad = grad.astype(jnp.float32) / chips_all
        grad_out[...] = grad
        update[...], new_first[...], new_second[...] = adam_step(grad, first[...], second[...])

    def spec(index_map):
        return pl.BlockSpec((BLOCK, 128), index_map)

    here = spec(lambda i, core: (i + shift, 0))
    group = BLOCK // high.shape[2]
    count = high.shape[0] // group

    def high_place(i, core):
        turn = jnp.where(core[0] == 1, i, 0)
        return turn % count, turn // count, 0, 0

    parts = (
        spec(lambda i, core: (jnp.where(core[0] == 0, i, 0), 0)),
        pl.BlockSpec((group, 1, high.shape[2], 128), high_place),
    )
    core = lax.axis_index("narrow").astype(jnp.int32).reshape(1)
    return pl.pallas_call(
        kernel,
        out_shape=[jax.ShapeDtypeStruct(moment1.shape, jnp.float32)] * 4,
        grid_spec=pltpu.PrefetchScalarGridSpec(
            num_scalar_prefetch=1,
            grid=(steps,),
            in_specs=[*parts, here, here] + [pl.BlockSpec(memory_space=pl.ANY)] * len(held),
            out_specs=[here] * 4,
        ),
        input_output_aliases={5 + n: n for n in range(len(held))},
        compiler_params=pltpu.CompilerParams(vmem_limit_bytes=40 << 20),
        name=f"adam{start}",
    )(core, low, high, moment1, moment2, *held)


def scatter_wide(value):
    return lax.psum_scatter(value, "wide", scatter_dimension=0, tiled=True)


def to_owner(value, source):
    return lax.ppermute(value, "narrow", [(source, 1 - source)])


def whole_params(params):
    low_params = params.astype(jnp.bfloat16)
    if lax.axis_size("narrow") == 2:
        return (low_params, narrow_swap(low_params, 1))
    return (lax.all_gather(low_params, "narrow", axis=0, tiled=True),)


def position_table():
    half_width = DD // 2
    places = jnp.arange(PATCH, dtype=jnp.float32)[:, None]
    rates = jnp.exp(jnp.arange(half_width, dtype=jnp.float32) * (-math.log(10000.0) / half_width))
    angles = places * rates[None, :]
    return jnp.concatenate([jnp.sin(angles), jnp.cos(angles)], 1)


def layer_norm(stream, gain_vec, bias_vec):
    average = jnp.mean(stream, -1, keepdims=True)
    centred = stream - average
    spread = jnp.mean(centred * centred, -1, keepdims=True)
    return centred * lax.rsqrt(spread + 1e-05) * gain_vec + bias_vec


def vector(weights_map, label):
    return weights_map[label].reshape(-1)


def adam_step(grads, moment1, moment2):
    new_first = 0.9 * moment1 + (1.0 - 0.9) * grads
    new_second = 0.95 * moment2 + (1.0 - 0.95) * grads * grads
    update = new_first / first_bias_fix / (jnp.sqrt(new_second / second_bias_fix) + 1e-08)
    return (update, new_first, new_second)


tail_terms = (
    0.05025708328,
    -0.1828833063,
    0.1690591746,
    -0.005588040603,
    0.141423544,
    0.1685436795,
    0.2078425222,
    0.2256696051,
    0.2256758619,
)


def gelu_and_slope(u):
    t = 1.0 / (1.0 + (0.4 * math.sqrt(0.5)) * jnp.abs(u))
    bell = jnp.exp(-0.5 * u * u)
    tail = 0.5 * tail_terms[0]
    for term in tail_terms[1:]:
        tail = tail * t + 0.5 * term
    tail = tail * t * bell
    below = jnp.where(u < 0, tail, 1.0 - tail)
    slope = below + u * bell * (1.0 / math.sqrt(2.0 * math.pi))
    return (u * below).astype(jnp.bfloat16), slope.astype(jnp.bfloat16)


def block_forward(stream, weights_map, prefix, heads):
    chips, tokens, width = stream.shape
    inner = heads * HD
    normed1 = layer_norm(
        stream,
        vector(weights_map, prefix + "g1"),
        vector(weights_map, prefix + "b1"),
    )
    first_in = normed1.astype(jnp.bfloat16)
    triple = jnp.einsum(
        "ctd,de->cte", first_in, weights_map[prefix + "qkv"], preferred_element_type=jnp.float32
    ).astype(jnp.bfloat16)
    query_rows = triple[:, :, :inner].reshape(chips, tokens, heads, HD)
    key_rows = triple[:, :, inner : 2 * inner].reshape(chips, tokens, heads, HD)
    value_rows = triple[:, :, 2 * inner :].reshape(chips, tokens, heads, HD)
    scores = jnp.einsum(
        "cqhe,ckhe->chqk", query_rows, key_rows, preferred_element_type=jnp.float32
    ) * HD ** (-0.5)
    topmost = jnp.max(scores, -1, keepdims=True)
    expos = jnp.exp(scores - topmost)
    totals = jnp.sum(expos, -1, keepdims=True)
    logsum = topmost + jnp.log(totals)
    probs = (expos / totals).astype(jnp.bfloat16)
    mixed = jnp.einsum("chqk,ckhe->cqhe", probs, value_rows, preferred_element_type=jnp.float32)
    mixed = mixed.reshape(chips, tokens, inner).astype(jnp.bfloat16)
    middle = (
        stream
        + jnp.einsum(
            "cti,id->ctd", mixed, weights_map[prefix + "o"], preferred_element_type=jnp.float32
        )
        + vector(weights_map, prefix + "ob")
    )
    normed2 = layer_norm(
        middle,
        vector(weights_map, prefix + "g2"),
        vector(weights_map, prefix + "b2"),
    )
    second_in = normed2.astype(jnp.bfloat16)
    hidden_pre = jnp.einsum(
        "ctd,df->ctf", second_in, weights_map[prefix + "u"], preferred_element_type=jnp.float32
    ) + vector(weights_map, prefix + "ub")
    activ, slope = lax.optimization_barrier(gelu_and_slope(hidden_pre))
    result = (
        middle
        + jnp.einsum(
            "ctf,fd->ctd", activ, weights_map[prefix + "v"], preferred_element_type=jnp.float32
        )
        + vector(weights_map, prefix + "vb")
    )
    kept = (
        stream,
        middle,
        first_in,
        query_rows,
        key_rows,
        value_rows,
        logsum,
        mixed,
        second_in,
        slope,
        activ,
    )
    return (result, kept)


def norm_backward(stream, weights_map, gain_label, bias_label, upstream):
    pull = jax.vjp(
        layer_norm, stream, vector(weights_map, gain_label), vector(weights_map, bias_label)
    )[1]
    return pull(upstream)


def mlp_backward(upstream, kept, weights_map, prefix):
    middle, second_in, slope = kept[1], kept[8], kept[9]
    grads = {}
    branch_two = upstream.astype(jnp.bfloat16)
    grads[prefix + "vb"] = jnp.sum(branch_two.astype(jnp.float32), (0, 1))
    d_activ = jnp.einsum(
        "ctd,fd->ctf", branch_two, weights_map[prefix + "v"], preferred_element_type=jnp.float32
    )
    d_hidden = (d_activ * slope.astype(jnp.float32)).astype(jnp.bfloat16)
    grads[prefix + "ub"] = jnp.sum(d_hidden.astype(jnp.float32), (0, 1))
    d_second = jnp.einsum(
        "ctf,df->ctd", d_hidden, weights_map[prefix + "u"], preferred_element_type=jnp.float32
    )
    d_middle_part, grads[prefix + "g2"], grads[prefix + "b2"] = norm_backward(
        middle, weights_map, prefix + "g2", prefix + "b2", d_second
    )
    return upstream + d_middle_part, d_hidden, grads


def hidden_gradient(kept, d_hidden):
    return jnp.einsum(
        "ctd,ctf->df", kept[8], d_hidden, preferred_element_type=jnp.float32
    ).astype(jnp.bfloat16)


def output_gradient(kept, upstream):
    return jnp.einsum(
        "ctf,ctd->fd", kept[10], upstream.astype(jnp.bfloat16), preferred_element_type=jnp.float32
    ).astype(jnp.bfloat16)


def scores_backward(d_middle, kept, weights_map, prefix, heads):
    query_rows, key_rows, value_rows, logsum = kept[3:7]
    chips, tokens, width = d_middle.shape
    branch_one = d_middle.astype(jnp.bfloat16)
    d_mixed = jnp.einsum(
        "ctd,id->cti", branch_one, weights_map[prefix + "o"], preferred_element_type=jnp.float32
    )
    d_mixed = d_mixed.astype(jnp.bfloat16).reshape(chips, tokens, heads, HD)
    scores = jnp.einsum(
        "cqhe,ckhe->chqk", query_rows, key_rows, preferred_element_type=jnp.float32
    ) * HD ** (-0.5)
    probs_full = jnp.exp(scores - logsum)
    probs_low = probs_full.astype(jnp.bfloat16)
    d_value = jnp.einsum("chqk,cqhe->ckhe", probs_low, d_mixed, preferred_element_type=jnp.float32)
    d_probs = jnp.einsum("cqhe,ckhe->chqk", d_mixed, value_rows, preferred_element_type=jnp.float32)
    row_shift = jnp.sum(d_probs * probs_full, -1, keepdims=True)
    d_scores = (probs_full * (d_probs - row_shift)).astype(jnp.bfloat16)
    return d_scores, d_value.astype(jnp.bfloat16)


def stream_backward(d_middle, d_scores, d_value, kept, weights_map, prefix, heads):
    stream, first_in, query_rows, key_rows, mixed = kept[0], kept[2], kept[3], kept[4], kept[7]
    chips, tokens, width = stream.shape
    inner = heads * HD
    grads = {}
    branch_one = d_middle.astype(jnp.bfloat16)
    grads[prefix + "ob"] = jnp.sum(branch_one.astype(jnp.float32), (0, 1))
    grads[prefix + "o"] = jnp.einsum(
        "cti,ctd->id", mixed, branch_one, preferred_element_type=jnp.float32
    ).astype(jnp.bfloat16)
    d_query = jnp.einsum(
        "chqk,ckhe->cqhe", d_scores, key_rows, preferred_element_type=jnp.float32
    ) * HD ** (-0.5)
    d_key = jnp.einsum(
        "chqk,cqhe->ckhe", d_scores, query_rows, preferred_element_type=jnp.float32
    ) * HD ** (-0.5)
    d_triple = jnp.concatenate(
        [
            d_query.reshape(chips, tokens, inner).astype(jnp.bfloat16),
            d_key.reshape(chips, tokens, inner).astype(jnp.bfloat16),
            d_value.reshape(chips, tokens, inner),
        ],
        -1,
    )
    grads[prefix + "qkv"] = jnp.einsum(
        "ctd,cte->de", first_in, d_triple, preferred_element_type=jnp.float32
    ).astype(jnp.bfloat16)
    d_first = jnp.einsum(
        "cte,de->ctd", d_triple, weights_map[prefix + "qkv"], preferred_element_type=jnp.float32
    )
    d_stream_part, grads[prefix + "g1"], grads[prefix + "b1"] = norm_backward(
        stream, weights_map, prefix + "g1", prefix + "b1", d_first
    )
    return (d_middle + d_stream_part, grads)


def per_device(patches, timeloc, visible, masked, flags, cotangent, params, moment1, moment2):
    total_rows = params.shape[0] * lax.axis_size("narrow")
    weights_map = unpack(whole_params(params), total_rows)
    chips = patches.shape[0]
    patch_ids = jnp.arange(PATCH, dtype=jnp.int32)
    chooser = visible[:, :, None] == patch_ids[None, None, :]
    choose_low = chooser.astype(jnp.bfloat16)
    choose_full = chooser.astype(jnp.float32)
    picked = jnp.einsum("cvp,cpd->cvd", choose_low, patches, preferred_element_type=jnp.float32)
    keep_meta = (1 - flags).astype(jnp.float32)
    meta_row = timeloc.astype(jnp.float32) * keep_meta[:, None]
    class_row = jnp.broadcast_to(vector(weights_map, "cls")[None, None, :], (chips, 1, DE))
    enc_in = jnp.concatenate([class_row, meta_row[:, None, :], picked], 1)
    enc_out, enc_kept = block_forward(enc_in, weights_map, "e", HE)
    patch_rows = enc_out[:, 2:, :]
    final_gain = vector(weights_map, "fg")
    final_bias = vector(weights_map, "fb")
    encoded_low = layer_norm(patch_rows, final_gain, final_bias).astype(jnp.bfloat16)
    projected = jnp.einsum(
        "cvd,de->cve", encoded_low, weights_map["proj"], preferred_element_type=jnp.float32
    ) + vector(weights_map, "pb")
    filled = jnp.einsum("cvp,cve->cpe", choose_full, projected, precision=highest)
    mask_rows = 1.0 - jnp.sum(choose_full, 1)
    dec_in = (
        filled
        + mask_rows[:, :, None] * vector(weights_map, "mask")[None, None, :]
        + position_table()[None]
    )
    dec_out, dec_kept = block_forward(dec_in, weights_map, "d", HDEC)
    tie = lax.optimization_barrier
    chunked = lax.axis_size("narrow") == 2 and lax.axis_size("wide") == 16
    half_rows = params.shape[0]
    padded = round_up(half_rows, 512)
    upper = (half_rows, half_rows + padded)
    upstream = cotangent.astype(jnp.float32)
    d_mid, d_hidden, grads = mlp_backward(upstream, dec_kept, weights_map, "d")
    grads["du"] = hidden_gradient(dec_kept, d_hidden)
    grads["dv"] = output_gradient(dec_kept, upstream)
    if chunked:
        cut = round_up(flat_rows()[0]["du"][0], 128)
        held = pack_part(grads, cut, upper[1], *upper)
        d_mid, held = tie((d_mid, held))
    attention = scores_backward(d_mid, dec_kept, weights_map, "d", HDEC)
    d_dec_in, more = stream_backward(d_mid, *attention, dec_kept, weights_map, "d", HDEC)
    grads.update(more)
    grads["mask"] = jnp.sum(mask_rows[:, :, None] * d_dec_in, (0, 1))
    d_projected = jnp.einsum("cvp,cpe->cve", choose_full, d_dec_in, precision=highest).astype(
        jnp.bfloat16
    )
    grads["pb"] = jnp.sum(d_projected.astype(jnp.float32), (0, 1))
    grads["proj"] = jnp.einsum(
        "cvd,cve->de", encoded_low, d_projected, preferred_element_type=jnp.float32
    ).astype(jnp.bfloat16)
    d_encoded = jnp.einsum(
        "cve,de->cvd", d_projected, weights_map["proj"], preferred_element_type=jnp.float32
    )
    final_pull = jax.vjp(layer_norm, patch_rows, final_gain, final_bias)[1]
    d_patch_rows, grads["fg"], grads["fb"] = final_pull(d_encoded)
    d_enc_out = jnp.concatenate([jnp.zeros((chips, 2, DE), jnp.float32), d_patch_rows], 1)
    grads["ev"] = output_gradient(enc_kept, d_enc_out)
    grads["evb"] = jnp.sum(d_enc_out.astype(jnp.bfloat16).astype(jnp.float32), (0, 1))
    if chunked:
        high = pack_part(grads, half_rows, cut, *upper, held)
        d_enc_out, high = tie((d_enc_out, high))
        high = [scatter_wide(part) for part in jnp.split(narrow_sum(high), 2)]
    d_mid, d_hidden, more = mlp_backward(d_enc_out, enc_kept, weights_map, "e")
    grads.update(more)
    grads["eu"] = hidden_gradient(enc_kept, d_hidden)
    if chunked:
        cut = round_up(flat_rows()[0]["eu"][0], 128)
        held = pack_part(grads, cut, padded, 0, padded)
        d_mid, held = tie((d_mid, held))
    attention = scores_backward(d_mid, enc_kept, weights_map, "e", HE)
    d_enc_in, more = stream_backward(d_mid, *attention, enc_kept, weights_map, "e", HE)
    grads.update(more)
    grads["cls"] = jnp.sum(d_enc_in[:, 0, :], 0)
    chips_all = float(chips * lax.axis_size("wide") * lax.axis_size("narrow"))
    if chunked:
        low = pack_part(grads, 0, cut, 0, padded, held)
        d_enc_in, low, high[0] = tie((d_enc_in, low, high[0]))
    patch_grad = jnp.einsum(
        "cvp,cvd->cpd", choose_full, d_enc_in[:, 2:, :], precision=highest
    ).astype(jnp.bfloat16)
    if chunked:
        low, high = staged_scatter(narrow_sum(low), high)
        high = lax.all_gather(jnp.stack(high), "wide")
        low = staged_gather(*low)
        start = low.shape[0]
        held = adam_rows(low, to_owner(high, 0), moment1, moment2, 0, (), chips_all)
        grad_out, update, new_moment1, new_moment2 = adam_rows(
            to_owner(low, 1), high, moment1, moment2, start, held, chips_all
        )
    else:
        every = flat_gradient(grads, half_rows * lax.axis_size("narrow"))
        grad_out = sum_everywhere(every, half_rows).astype(jnp.float32) / chips_all
        update, new_moment1, new_moment2 = adam_step(grad_out, moment1, moment2)
    return (dec_out.astype(jnp.bfloat16), patch_grad, grad_out, update, new_moment1, new_moment2)


def solution(mesh):
    placed = (
        P(("wide", "narrow"), None, None),
        P(("wide", "narrow"), None),
        P(("wide", "narrow"), None),
        P(("wide", "narrow"), None),
        P(("wide", "narrow")),
        P(("wide", "narrow"), None, None),
        P("narrow", None),
        P("narrow", None),
        P("narrow", None),
    )
    return jax.shard_map(
        per_device,
        mesh=mesh,
        in_specs=placed,
        out_specs=(
            P(("wide", "narrow"), None, None),
            P(("wide", "narrow"), None, None),
            P("narrow", None),
            P("narrow", None),
            P("narrow", None),
            P("narrow", None),
        ),
        check_vma=False,
    )
```

```python
import math

import jax
import jax.numpy as jnp
from jax import lax
from jax.experimental import pallas as pl
from jax.experimental.pallas import tpu as pltpu
from jax.sharding import PartitionSpec as P

DE = 768
HE = 12
HD = 64
FE = 3072
DD = 512
HDEC = 4
FD = 2048
PATCH = 256


highest = lax.Precision.HIGHEST
first_bias_fix = 0.9999734386011124
second_bias_fix = 0.994079470779666


def block_segments(prefix, width, inner, hidden):
    names = ("g1", "b1", "qkv", "o", "ob", "g2", "b2", "u", "ub", "v", "vb")
    dims = ((width,), (width,), (width, 3 * inner), (inner, width), (width,), (width,), (width,))
    dims = (*dims, (width, hidden), (hidden,), (hidden, width), (width,))
    return [(prefix + name, size) for name, size in zip(names, dims)]


def segment_list():
    ends = (("fg", (DE,)), ("fb", (DE,)), ("proj", (DE, DD)), ("pb", (DD,)), ("mask", (DD,)))
    return [
        ("cls", (DE,)),
        *block_segments("e", DE, HE * HD, FE),
        *ends,
        *block_segments("d", DD, HDEC * HD, FD),
    ]


MARGIN = 512


def flat_rows():
    table = {}
    offset = 0
    for label, dims_of in segment_list():
        rows = math.prod(dims_of) // 128
        table[label] = (offset, rows)
        offset = offset + rows
    return table, offset


def round_up(value, unit):
    return -(-value // unit) * unit


def group_list():
    firsts = ("cls", "eo", "eu", "ev", "proj", "dqkv", "du", "dv")
    groups = []
    for label, dims in segment_list():
        if label in firsts:
            groups.append([])
        if label == "dg1" or label == "db1" or groups:
            groups[-1].append(label)
    return groups


def unpack(sources, total):
    table, used = flat_rows()
    shapes = dict(segment_list())
    groups = group_list()
    spans = [(table[g[0]][0], sum(table[g[-1]])) for g in groups]
    edges = [0, *[min(round_up(high, 16), total) for low, high in spans]]
    half = total // 2
    copies = []
    for k, (low, high) in enumerate(zip(edges, edges[1:])):
        parts = [(low, high)]
        if len(sources) == 2 and low < half < high:
            parts = [(low, half), (half, high)]
        copies.append(parts)
    slots = [(k, p) for k, parts in enumerate(copies) for p in range(len(parts))]
    labels = [label for label, dims in segment_list()]
    matrices = [label for label, dims in segment_list() if len(dims) == 2]
    deepest = max(round_up(high, 16) - low // 16 * 16 for low, high in spans)

    def kernel(*refs):
        ins, rest = refs[: len(sources)], refs[len(sources) :]
        finals = dict(zip(labels, rest))
        staged, wide_rows, sems, *own, out_sems = rest[len(labels) :]
        outs = {**finals, **dict(zip(matrices, own))}

        def leave(label):
            return pltpu.make_async_copy(
                outs[label], finals[label], out_sems.at[matrices.index(label)]
            )

        def copy(slot, source, shift):
            k, p = slot
            low, high = copies[k][p]
            return pltpu.make_async_copy(
                source.at[pl.ds(low - shift, high - low)],
                staged.at[pl.ds(low, high - low)],
                sems.at[slots.index(slot)],
            )

        if len(sources) == 2:
            mine = lax.axis_index("narrow")
            for slot in slots:
                place = 0 if copies[slot[0]][slot[1]][0] < half else 1

                @pl.when(mine == place)
                def own_part(slot=slot, place=place):
                    copy(slot, ins[0], place * half).start()

                @pl.when(mine != place)
                def other_part(slot=slot, place=place):
                    copy(slot, ins[1], place * half).start()
        else:
            for slot in slots:
                copy(slot, ins[0], 0).start()
        for k, group in enumerate(groups):
            for p in range(len(copies[k])):
                copy((k, p), ins[0], copies[k][p][0]).wait()
            low, high = spans[k]
            origin = low // 16 * 16
            length = round_up(high, 16) - origin

            def widen(i, carry, origin=origin):
                spot = pl.multiple_of(i * 128, 128)
                wide_rows[pl.ds(spot, 128), :] = staged[
                    pl.ds(pl.multiple_of(origin + spot, 16), 128), :
                ].astype(jnp.float32)
                return carry

            lax.fori_loop(0, length // 128, widen, 0)
            done = length // 128 * 128
            if done < length:
                wide_rows[done:length, :] = staged[origin + done : origin + length, :].astype(
                    jnp.float32
                )
            for label in group:
                base = table[label][0] - origin
                dims, ref = shapes[label], outs[label]
                tiles = dims[-1] // 128
                if len(dims) == 1:
                    for c in range(tiles):
                        ref[:, c * 128 : (c + 1) * 128] = wide_rows[base + c : base + c + 1, :]
                    continue

                def step(i, carry, base=base, tiles=tiles, ref=ref):
                    for c in range(tiles):
                        rows = wide_rows[pl.ds(base + i * 16 * tiles + c, 16, stride=tiles), :]
                        ref[pl.ds(pl.multiple_of(i * 16, 16), 16), c * 128 : (c + 1) * 128] = (
                            rows.astype(jnp.bfloat16)
                        )
                    return carry

                lax.fori_loop(0, dims[0] // 16, step, 0)
                leave(label).start()
        for label in matrices:
            leave(label).wait()

    out_shape = [
        jax.ShapeDtypeStruct(dims, jnp.bfloat16)
        if len(dims) == 2
        else jax.ShapeDtypeStruct((1, dims[0]), jnp.float32)
        for label, dims in segment_list()
    ]
    outs = pl.pallas_call(
        kernel,
        out_shape=out_shape,
        in_specs=[pl.BlockSpec(memory_space=pl.ANY)] * len(sources),
        out_specs=[
            pl.BlockSpec(memory_space=pl.ANY if label in matrices else pltpu.VMEM)
            for label in labels
        ],
        scratch_shapes=[
            pltpu.VMEM((total, 128), jnp.bfloat16),
            pltpu.VMEM((deepest, 128), jnp.float32),
            pltpu.SemaphoreType.DMA((len(slots),)),
            *[pltpu.VMEM(shapes[label], jnp.bfloat16) for label in matrices],
            pltpu.SemaphoreType.DMA((len(matrices),)),
        ],
        compiler_params=pltpu.CompilerParams(vmem_limit_bytes=61 << 20),
        name="unpack",
    )(*sources)
    return dict(zip(labels, outs))


def pack_part(pieces, low, high, first, last, held=()):
    table, used = flat_rows()
    labels = [k for k, (off, rows) in table.items() if off < high and off + rows > low]
    arrays, places = [], []
    for k in labels:
        value = pieces[k] if pieces[k].ndim == 2 else pieces[k].reshape(1, -1)
        off, rows = table[k]
        tiles = value.shape[1] // 128
        begin, end = 0, 1
        if value.shape[0] > 1:
            begin = max(0, low - off) // (16 * tiles)
            end = -(-min(rows, high - off) // (16 * tiles))
            if 3 * (end - begin) * 16 < value.shape[0]:
                value = value[begin * 16 : end * 16]
                off, end, begin = off + begin * 16 * tiles, end - begin, 0
        arrays.append(value)
        places.append((off, begin, end))
    length = high - low
    middle = (first + last) // 2
    runs = [
        (max(low, start), min(high, end), place, start)
        for place, (start, end) in enumerate(((first, middle), (middle, last)))
        if max(low, start) < min(high, end)
    ]

    def kernel(*refs):
        ins, rest = refs[: len(labels)], refs[len(labels) + len(held) :]
        kept, sent, flat, out, sems = rest
        if used < high:
            start = max(used, low) - low + MARGIN
            flat[start : MARGIN + length, :] = jnp.zeros((MARGIN + length - start, 128), jnp.float32)
        for (off, begin, end), ref in zip(places, ins):
            tiles = ref.shape[1] // 128
            base = off - low + MARGIN
            if ref.shape[0] == 1:
                for c in range(tiles):
                    spot = base + c
                    if 0 <= spot < length + 2 * MARGIN:
                        flat[spot : spot + 1, :] = ref[:, c * 128 : (c + 1) * 128]
                continue
            block = 16 * tiles

            def step(i, carry, ref=ref, tiles=tiles, base=base, block=block):
                for c in range(tiles):
                    rows = ref[pl.ds(pl.multiple_of(i * 16, 16), 16), c * 128 : (c + 1) * 128]
                    flat[pl.ds(base + i * block + c, 16, stride=tiles), :] = rows.astype(jnp.float32)
                return carry

            lax.fori_loop(begin, end, step, 0)

        def narrow_down(i, carry):
            spot = pl.multiple_of(i * 128, 128)
            out[pl.ds(spot, 128), :] = flat[pl.ds(MARGIN + spot, 128), :].astype(jnp.bfloat16)
            return carry

        lax.fori_loop(0, length // 128, narrow_down, 0)
        mine = lax.axis_index("narrow")

        def copy(n, target):
            start, end, place, origin = runs[n]
            return pltpu.make_async_copy(
                out.at[pl.ds(start - low, end - start)],
                target.at[pl.ds(start - origin, end - start)],
                sems.at[n],
            )

        for n, (start, end, place, origin) in enumerate(runs):

            @pl.when(mine == place)
            def keep(n=n):
                copy(n, kept).start()

            @pl.when(mine != place)
            def send(n=n):
                copy(n, sent).start()

        for n in range(len(runs)):
            copy(n, kept).wait()

    anywhere = pl.BlockSpec(memory_space=pl.ANY)
    whole = pl.BlockSpec(memory_space=pltpu.VMEM)
    return pl.pallas_call(
        kernel,
        out_shape=[jax.ShapeDtypeStruct((middle - first, 128), jnp.bfloat16)] * 2,
        in_specs=[whole] * len(arrays) + [anywhere] * len(held),
        out_specs=[anywhere] * 2,
        input_output_aliases={len(arrays) + n: n for n in range(len(held))},
        scratch_shapes=[
            pltpu.VMEM((length + 2 * MARGIN, 128), jnp.float32),
            pltpu.VMEM((length, 128), jnp.bfloat16),
            pltpu.SemaphoreType.DMA((len(runs),)),
        ],
        compiler_params=pltpu.CompilerParams(vmem_limit_bytes=61 << 20),
        name=f"pack{low}",
    )(*arrays, *held)


def flat_gradient(grads, unit):
    table, used = flat_rows()
    flat = jnp.concatenate([grads[k].astype(jnp.bfloat16).reshape(-1) for k, dims in segment_list()])
    padding = (round_up(used, unit) - used) * 128
    flat = jnp.concatenate([flat, jnp.zeros((padding,), jnp.bfloat16)])
    return flat.reshape(-1, 128)


def added(first, second):
    return (first.astype(jnp.float32) + second.astype(jnp.float32)).astype(jnp.bfloat16)


def piece(value, index, rows):
    return lax.dynamic_slice_in_dim(value, index * rows, rows, 0)


class Line:
    def __init__(self, stride, size):
        self.stride, self.size, self.wide = stride, size, lax.axis_size("wide")
        self.me = (lax.axis_index("wide") // stride) % size
        self.groups = [
            [i + k * stride for k in range(size)]
            for i in range(self.wide)
            if (i // stride) % size == 0
        ]

    def swap(self, value):
        pairs = [pair for a, b in self.groups for pair in ((a, b), (b, a))]
        return lax.ppermute(value, "wide", pairs)

    def exchange(self, value):
        return lax.all_to_all(value, "wide", 0, 0, axis_index_groups=self.groups)

    def scatter(self, value):
        rows = value.shape[0] // self.size
        if self.size == 2:
            got = self.swap(piece(value, 1 - self.me, rows))
            return added(piece(value, self.me, rows), got)
        got = self.exchange(value.reshape(self.size, -1, 128)).astype(jnp.float32)
        return jnp.sum(got, 0).astype(jnp.bfloat16).reshape(rows, -1, 128)

    def gather(self, value):
        if self.size == 2:
            got = self.swap(value)
            low = self.me == 0
            return jnp.concatenate([jnp.where(low, value, got), jnp.where(low, got, value)], 0)
        copies = jnp.broadcast_to(value[None], (self.size, *value.shape))
        return self.exchange(copies).reshape(-1, *value.shape[1:])


def narrow_swap(value, step):
    count = lax.axis_size("narrow")
    return lax.ppermute(value, "narrow", [(i, (i + step) % count) for i in range(count)])


def flat3(value, places):
    return value.reshape(places, -1, 128)


def wide_lines():
    return Line(1, 2), Line(2, 2), Line(4, lax.axis_size("wide") // 4)


def staged_scatter(total):
    x, y, z = wide_lines()
    unit = lax.axis_size("wide") * 8
    most = total.shape[0] // unit * 4 // 11
    first, second = most * unit, 2 * most * unit
    a = total[:first].reshape(2, 2, z.size, -1, 128)
    b = total[first:second].reshape(2, 2, z.size, -1, 128)
    c = total[second:].reshape(z.size, 2, 2, -1, 128)
    c = z.scatter(flat3(c, z.size))
    a = x.scatter(flat3(a, 2))
    b = y.scatter(flat3(b, 2))
    a = y.scatter(flat3(a, 2))
    b = x.scatter(flat3(b, 2))
    a, b, c = lax.optimization_barrier((a, b, c))
    ab = z.scatter(jnp.concatenate([flat3(a, z.size), flat3(b, z.size)], 1))
    c = x.scatter(flat3(c, 2))
    c = y.scatter(flat3(c, 2))
    return lax.optimization_barrier((ab, c))


def staged_gather(ab, c, beside=()):
    x, y, z = wide_lines()
    ab = z.gather(flat3(ab, 1))
    c = x.gather(y.gather(flat3(c, 1)))
    ab, c, beside = lax.optimization_barrier((ab, c, beside))
    half = ab.shape[1] // 2
    a, b = ab[:, :half], ab[:, half:]
    c = z.gather(flat3(c, 1))
    a = y.gather(flat3(a, 1)).reshape(-1, 128)
    b = x.gather(flat3(b, 1)).reshape(-1, 128)
    return join_pieces((x, a, x.swap(a)), (y, b, y.swap(b)), c.reshape(-1, 128)), beside


def join_pieces(first, second, third):
    pairs = (first, second)
    sizes = [2 * own.shape[0] for line, own, other in pairs]

    def kernel(own1, other1, own2, other2, last, out, sems):
        copies = []
        start = 0
        for (line, own, other), refs in zip(pairs, ((own1, other1), (own2, other2))):
            rows = own.shape[0]
            me = (lax.axis_index("wide") // line.stride) % 2
            for ref, place in zip(refs, (me, 1 - me)):
                copies.append((ref, pl.multiple_of(start + place * rows, 8), rows))
            start += 2 * rows
        copies.append((last, start, third.shape[0]))
        copies = [
            pltpu.make_async_copy(ref, out.at[pl.ds(spot, rows)], sems.at[n])
            for n, (ref, spot, rows) in enumerate(copies)
        ]
        for copy in copies:
            copy.start()
        for copy in copies:
            copy.wait()

    return pl.pallas_call(
        kernel,
        out_shape=jax.ShapeDtypeStruct((sum(sizes) + third.shape[0], 128), third.dtype),
        in_specs=[pl.BlockSpec(memory_space=pltpu.VMEM)] * 5,
        out_specs=pl.BlockSpec(memory_space=pl.ANY),
        scratch_shapes=[pltpu.SemaphoreType.DMA((5,))],
        name="join",
    )(first[1], first[2], second[1], second[2], third)


def narrow_sum(halves):
    return added(halves[0], narrow_swap(halves[1], 1))


def sum_everywhere(value, rows):
    count = lax.axis_size("narrow")
    mine = lax.axis_index("narrow")
    total = lax.dynamic_slice_in_dim(value, mine * rows, rows, 0)
    for step in range(1, count):
        other = lax.dynamic_slice_in_dim(value, (mine + step) % count * rows, rows, 0)
        total = added(total, narrow_swap(other, step))
    unit = lax.axis_size("wide") * 16
    total = jnp.pad(total, ((0, round_up(rows, unit) - rows), (0, 0)))
    return staged_gather(*staged_scatter(total))[0][:rows]


def scatter_first(value):
    x, y, z = wide_lines()
    a, b = jnp.split(value, 2)
    return x.scatter(flat3(a, 2)), y.scatter(flat3(b, 2))


def scatter_second(pair):
    x, y, z = wide_lines()
    return y.scatter(flat3(pair[0], 2)), x.scatter(flat3(pair[1], 2))


def scatter_last(pair):
    z = wide_lines()[2]
    both = jnp.concatenate([flat3(v, z.size) for v in pair], 1)
    return z.scatter(both).reshape(-1, 128)


BLOCK = 2496


def adam_rows(low, high, moment1, moment2, start, held, chips_all):
    shift = start // BLOCK
    steps = -(-min(low.shape[0], moment1.shape[0] - start) // BLOCK)

    def kernel(core, low_rows, high_rows, first, second, *rest):
        grad_out, update, new_first, new_second = rest[len(held) :]
        grad = jnp.where(core[0] == 0, low_rows[...], high_rows[...].reshape(BLOCK, 128))
        grad = grad.astype(jnp.float32) / chips_all
        grad_out[...] = grad
        update[...], new_first[...], new_second[...] = adam_step(grad, first[...], second[...])

    def spec(index_map):
        return pl.BlockSpec((BLOCK, 128), index_map)

    here = spec(lambda i, core: (i + shift, 0))
    high = high.reshape(-1, 4, 2, BLOCK // 4, 128)

    def high_place(i, core):
        turn = jnp.where(core[0] == 1, i, 0)
        part, spot = turn // 4, turn % 4
        return 0, jnp.where(part == 0, spot % 2 * 2 + spot // 2, spot), part, 0, 0

    parts = (
        spec(lambda i, core: (jnp.where(core[0] == 0, i, 0), 0)),
        pl.BlockSpec((4, 1, 1, BLOCK // 4, 128), high_place),
    )
    core = lax.axis_index("narrow").astype(jnp.int32).reshape(1)
    return pl.pallas_call(
        kernel,
        out_shape=[jax.ShapeDtypeStruct(moment1.shape, jnp.float32)] * 4,
        grid_spec=pltpu.PrefetchScalarGridSpec(
            num_scalar_prefetch=1,
            grid=(steps,),
            in_specs=[*parts, here, here] + [pl.BlockSpec(memory_space=pl.ANY)] * len(held),
            out_specs=[here] * 4,
        ),
        input_output_aliases={5 + n: n for n in range(len(held))},
        compiler_params=pltpu.CompilerParams(vmem_limit_bytes=40 << 20),
        name=f"adam{start}",
    )(core, low, high, moment1, moment2, *held)


def to_owner(value, source):
    return lax.ppermute(value, "narrow", [(source, 1 - source)])


def whole_params(params):
    low_params = params.astype(jnp.bfloat16)
    if lax.axis_size("narrow") == 2:
        return (low_params, narrow_swap(low_params, 1))
    return (lax.all_gather(low_params, "narrow", axis=0, tiled=True),)


def position_table():
    half_width = DD // 2
    places = jnp.arange(PATCH, dtype=jnp.float32)[:, None]
    rates = jnp.exp(jnp.arange(half_width, dtype=jnp.float32) * (-math.log(10000.0) / half_width))
    angles = places * rates[None, :]
    return jnp.concatenate([jnp.sin(angles), jnp.cos(angles)], 1)


def layer_norm(stream, gain_vec, bias_vec):
    average = jnp.mean(stream, -1, keepdims=True)
    centred = stream - average
    spread = jnp.mean(centred * centred, -1, keepdims=True)
    return centred * lax.rsqrt(spread + 1e-05) * gain_vec + bias_vec


def vector(weights_map, label):
    return weights_map[label].reshape(-1)


def adam_step(grads, moment1, moment2):
    new_first = 0.9 * moment1 + (1.0 - 0.9) * grads
    new_second = 0.95 * moment2 + (1.0 - 0.95) * grads * grads
    update = new_first / first_bias_fix / (jnp.sqrt(new_second / second_bias_fix) + 1e-08)
    return (update, new_first, new_second)


tail_terms = (
    0.05025708328,
    -0.1828833063,
    0.1690591746,
    -0.005588040603,
    0.141423544,
    0.1685436795,
    0.2078425222,
    0.2256696051,
    0.2256758619,
)


def gelu_and_slope(u):
    t = 1.0 / (1.0 + (0.4 * math.sqrt(0.5)) * jnp.abs(u))
    bell = jnp.exp(-0.5 * u * u)
    tail = 0.5 * tail_terms[0]
    for term in tail_terms[1:]:
        tail = tail * t + 0.5 * term
    tail = tail * t * bell
    below = jnp.where(u < 0, tail, 1.0 - tail)
    slope = below + u * bell * (1.0 / math.sqrt(2.0 * math.pi))
    return (u * below).astype(jnp.bfloat16), slope.astype(jnp.bfloat16)


def block_forward(stream, weights_map, prefix, heads):
    chips, tokens, width = stream.shape
    inner = heads * HD
    normed1 = layer_norm(
        stream,
        vector(weights_map, prefix + "g1"),
        vector(weights_map, prefix + "b1"),
    )
    first_in = normed1.astype(jnp.bfloat16)
    triple = jnp.einsum(
        "ctd,de->cte", first_in, weights_map[prefix + "qkv"], preferred_element_type=jnp.float32
    ).astype(jnp.bfloat16)
    query_rows = triple[:, :, :inner].reshape(chips, tokens, heads, HD)
    key_rows = triple[:, :, inner : 2 * inner].reshape(chips, tokens, heads, HD)
    value_rows = triple[:, :, 2 * inner :].reshape(chips, tokens, heads, HD)
    scores = jnp.einsum(
        "cqhe,ckhe->chqk", query_rows, key_rows, preferred_element_type=jnp.float32
    ) * HD ** (-0.5)
    topmost = jnp.max(scores, -1, keepdims=True)
    expos = jnp.exp(scores - topmost)
    totals = jnp.sum(expos, -1, keepdims=True)
    logsum = topmost + jnp.log(totals)
    probs = (expos / totals).astype(jnp.bfloat16)
    mixed = jnp.einsum("chqk,ckhe->cqhe", probs, value_rows, preferred_element_type=jnp.float32)
    mixed = mixed.reshape(chips, tokens, inner).astype(jnp.bfloat16)
    middle = (
        stream
        + jnp.einsum(
            "cti,id->ctd", mixed, weights_map[prefix + "o"], preferred_element_type=jnp.float32
        )
        + vector(weights_map, prefix + "ob")
    )
    normed2 = layer_norm(
        middle,
        vector(weights_map, prefix + "g2"),
        vector(weights_map, prefix + "b2"),
    )
    second_in = normed2.astype(jnp.bfloat16)
    hidden_pre = jnp.einsum(
        "ctd,df->ctf", second_in, weights_map[prefix + "u"], preferred_element_type=jnp.float32
    ) + vector(weights_map, prefix + "ub")
    activ, slope = lax.optimization_barrier(gelu_and_slope(hidden_pre))
    result = (
        middle
        + jnp.einsum(
            "ctf,fd->ctd", activ, weights_map[prefix + "v"], preferred_element_type=jnp.float32
        )
        + vector(weights_map, prefix + "vb")
    )
    kept = (
        stream,
        middle,
        first_in,
        query_rows,
        key_rows,
        value_rows,
        logsum,
        mixed,
        second_in,
        slope,
        activ,
    )
    return (result, kept)


def norm_backward(stream, weights_map, gain_label, bias_label, upstream):
    pull = jax.vjp(
        layer_norm, stream, vector(weights_map, gain_label), vector(weights_map, bias_label)
    )[1]
    return pull(upstream)


def mlp_backward(upstream, kept, weights_map, prefix):
    middle, second_in, slope = kept[1], kept[8], kept[9]
    grads = {}
    branch_two = upstream.astype(jnp.bfloat16)
    grads[prefix + "vb"] = jnp.sum(branch_two.astype(jnp.float32), (0, 1))
    d_activ = jnp.einsum(
        "ctd,fd->ctf", branch_two, weights_map[prefix + "v"], preferred_element_type=jnp.float32
    )
    d_hidden = (d_activ * slope.astype(jnp.float32)).astype(jnp.bfloat16)
    grads[prefix + "ub"] = jnp.sum(d_hidden.astype(jnp.float32), (0, 1))
    d_second = jnp.einsum(
        "ctf,df->ctd", d_hidden, weights_map[prefix + "u"], preferred_element_type=jnp.float32
    )
    d_middle_part, grads[prefix + "g2"], grads[prefix + "b2"] = norm_backward(
        middle, weights_map, prefix + "g2", prefix + "b2", d_second
    )
    return upstream + d_middle_part, d_hidden, grads


def hidden_gradient(kept, d_hidden):
    return jnp.einsum(
        "ctd,ctf->df", kept[8], d_hidden, preferred_element_type=jnp.float32
    ).astype(jnp.bfloat16)


def output_gradient(kept, upstream):
    return jnp.einsum(
        "ctf,ctd->fd", kept[10], upstream.astype(jnp.bfloat16), preferred_element_type=jnp.float32
    ).astype(jnp.bfloat16)


def scores_backward(d_middle, kept, weights_map, prefix, heads):
    query_rows, key_rows, value_rows, logsum = kept[3:7]
    chips, tokens, width = d_middle.shape
    branch_one = d_middle.astype(jnp.bfloat16)
    d_mixed = jnp.einsum(
        "ctd,id->cti", branch_one, weights_map[prefix + "o"], preferred_element_type=jnp.float32
    )
    d_mixed = d_mixed.astype(jnp.bfloat16).reshape(chips, tokens, heads, HD)
    scores = jnp.einsum(
        "cqhe,ckhe->chqk", query_rows, key_rows, preferred_element_type=jnp.float32
    ) * HD ** (-0.5)
    probs_full = jnp.exp(scores - logsum)
    probs_low = probs_full.astype(jnp.bfloat16)
    d_value = jnp.einsum("chqk,cqhe->ckhe", probs_low, d_mixed, preferred_element_type=jnp.float32)
    d_probs = jnp.einsum("cqhe,ckhe->chqk", d_mixed, value_rows, preferred_element_type=jnp.float32)
    row_shift = jnp.sum(d_probs * probs_full, -1, keepdims=True)
    d_scores = (probs_full * (d_probs - row_shift)).astype(jnp.bfloat16)
    return d_scores, d_value.astype(jnp.bfloat16)


def stream_backward(d_middle, d_scores, d_value, kept, weights_map, prefix, heads):
    stream, first_in, query_rows, key_rows, mixed = kept[0], kept[2], kept[3], kept[4], kept[7]
    chips, tokens, width = stream.shape
    inner = heads * HD
    grads = {}
    branch_one = d_middle.astype(jnp.bfloat16)
    grads[prefix + "ob"] = jnp.sum(branch_one.astype(jnp.float32), (0, 1))
    grads[prefix + "o"] = jnp.einsum(
        "cti,ctd->id", mixed, branch_one, preferred_element_type=jnp.float32
    ).astype(jnp.bfloat16)
    d_query = jnp.einsum(
        "chqk,ckhe->cqhe", d_scores, key_rows, preferred_element_type=jnp.float32
    ) * HD ** (-0.5)
    d_key = jnp.einsum(
        "chqk,cqhe->ckhe", d_scores, query_rows, preferred_element_type=jnp.float32
    ) * HD ** (-0.5)
    d_triple = jnp.concatenate(
        [
            d_query.reshape(chips, tokens, inner).astype(jnp.bfloat16),
            d_key.reshape(chips, tokens, inner).astype(jnp.bfloat16),
            d_value.reshape(chips, tokens, inner),
        ],
        -1,
    )
    grads[prefix + "qkv"] = jnp.einsum(
        "ctd,cte->de", first_in, d_triple, preferred_element_type=jnp.float32
    ).astype(jnp.bfloat16)
    d_first = jnp.einsum(
        "cte,de->ctd", d_triple, weights_map[prefix + "qkv"], preferred_element_type=jnp.float32
    )
    d_stream_part, grads[prefix + "g1"], grads[prefix + "b1"] = norm_backward(
        stream, weights_map, prefix + "g1", prefix + "b1", d_first
    )
    return (d_middle + d_stream_part, grads)


def per_device(patches, timeloc, visible, masked, flags, cotangent, params, moment1, moment2):
    total_rows = params.shape[0] * lax.axis_size("narrow")
    weights_map = unpack(whole_params(params), total_rows)
    chips = patches.shape[0]
    patch_ids = jnp.arange(PATCH, dtype=jnp.int32)
    chooser = visible[:, :, None] == patch_ids[None, None, :]
    choose_low = chooser.astype(jnp.bfloat16)
    choose_full = chooser.astype(jnp.float32)
    picked = jnp.einsum("cvp,cpd->cvd", choose_low, patches, preferred_element_type=jnp.float32)
    keep_meta = (1 - flags).astype(jnp.float32)
    meta_row = timeloc.astype(jnp.float32) * keep_meta[:, None]
    class_row = jnp.broadcast_to(vector(weights_map, "cls")[None, None, :], (chips, 1, DE))
    enc_in = jnp.concatenate([class_row, meta_row[:, None, :], picked], 1)
    enc_out, enc_kept = block_forward(enc_in, weights_map, "e", HE)
    patch_rows = enc_out[:, 2:, :]
    final_gain = vector(weights_map, "fg")
    final_bias = vector(weights_map, "fb")
    encoded_low = layer_norm(patch_rows, final_gain, final_bias).astype(jnp.bfloat16)
    projected = jnp.einsum(
        "cvd,de->cve", encoded_low, weights_map["proj"], preferred_element_type=jnp.float32
    ) + vector(weights_map, "pb")
    filled = jnp.einsum("cvp,cve->cpe", choose_full, projected, precision=highest)
    mask_rows = 1.0 - jnp.sum(choose_full, 1)
    dec_in = (
        filled
        + mask_rows[:, :, None] * vector(weights_map, "mask")[None, None, :]
        + position_table()[None]
    )
    dec_out, dec_kept = block_forward(dec_in, weights_map, "d", HDEC)
    tie = lax.optimization_barrier
    chunked = lax.axis_size("narrow") == 2 and lax.axis_size("wide") == 16
    half_rows = params.shape[0]
    padded = round_up(half_rows, 512)
    upper = (half_rows, half_rows + padded)
    upstream = cotangent.astype(jnp.float32)
    d_mid, d_hidden, grads = mlp_backward(upstream, dec_kept, weights_map, "d")
    grads["du"] = hidden_gradient(dec_kept, d_hidden)
    grads["dv"] = output_gradient(dec_kept, upstream)
    if chunked:
        cut = round_up(flat_rows()[0]["du"][0], 128)
        held = pack_part(grads, cut, upper[1], *upper)
        d_mid, held = tie((d_mid, held))
    attention = scores_backward(d_mid, dec_kept, weights_map, "d", HDEC)
    d_dec_in, more = stream_backward(d_mid, *attention, dec_kept, weights_map, "d", HDEC)
    grads.update(more)
    grads["mask"] = jnp.sum(mask_rows[:, :, None] * d_dec_in, (0, 1))
    d_projected = jnp.einsum("cvp,cpe->cve", choose_full, d_dec_in, precision=highest).astype(
        jnp.bfloat16
    )
    grads["pb"] = jnp.sum(d_projected.astype(jnp.float32), (0, 1))
    grads["proj"] = jnp.einsum(
        "cvd,cve->de", encoded_low, d_projected, preferred_element_type=jnp.float32
    ).astype(jnp.bfloat16)
    d_encoded = jnp.einsum(
        "cve,de->cvd", d_projected, weights_map["proj"], preferred_element_type=jnp.float32
    )
    final_pull = jax.vjp(layer_norm, patch_rows, final_gain, final_bias)[1]
    d_patch_rows, grads["fg"], grads["fb"] = final_pull(d_encoded)
    d_enc_out = jnp.concatenate([jnp.zeros((chips, 2, DE), jnp.float32), d_patch_rows], 1)
    grads["ev"] = output_gradient(enc_kept, d_enc_out)
    grads["evb"] = jnp.sum(d_enc_out.astype(jnp.bfloat16).astype(jnp.float32), (0, 1))
    if chunked:
        high = pack_part(grads, half_rows, cut, *upper, held)
        d_enc_out, high = tie((d_enc_out, high))
        high = scatter_first(narrow_sum(high))
    d_mid, d_hidden, more = mlp_backward(d_enc_out, enc_kept, weights_map, "e")
    grads.update(more)
    grads["eu"] = hidden_gradient(enc_kept, d_hidden)
    if chunked:
        cut = round_up(flat_rows()[0]["eu"][0], 128)
        held = pack_part(grads, cut, padded, 0, padded)
        d_mid, held, high = tie((d_mid, held, high))
        high = scatter_second(high)
    attention = scores_backward(d_mid, enc_kept, weights_map, "e", HE)
    if chunked:
        attention, d_mid, high = tie((attention, d_mid, high))
        high = scatter_last(high)
    d_enc_in, more = stream_backward(d_mid, *attention, enc_kept, weights_map, "e", HE)
    grads.update(more)
    grads["cls"] = jnp.sum(d_enc_in[:, 0, :], 0)
    chips_all = float(chips * lax.axis_size("wide") * lax.axis_size("narrow"))
    if chunked:
        low = pack_part(grads, 0, cut, 0, padded, held)
        d_enc_in, low, high = tie((d_enc_in, low, high))
        high = lax.all_gather(high, "wide")
    patch_grad = jnp.einsum(
        "cvp,cvd->cpd", choose_full, d_enc_in[:, 2:, :], precision=highest
    ).astype(jnp.bfloat16)
    if chunked:
        low, high = staged_gather(*staged_scatter(narrow_sum(low)), high)
        start = low.shape[0]
        held = adam_rows(low, to_owner(high, 0), moment1, moment2, 0, (), chips_all)
        grad_out, update, new_moment1, new_moment2 = adam_rows(
            to_owner(low, 1), high, moment1, moment2, start, held, chips_all
        )
    else:
        every = flat_gradient(grads, half_rows * lax.axis_size("narrow"))
        grad_out = sum_everywhere(every, half_rows).astype(jnp.float32) / chips_all
        update, new_moment1, new_moment2 = adam_step(grad_out, moment1, moment2)
    return (dec_out.astype(jnp.bfloat16), patch_grad, grad_out, update, new_moment1, new_moment2)


def solution(mesh):
    placed = (
        P(("wide", "narrow"), None, None),
        P(("wide", "narrow"), None),
        P(("wide", "narrow"), None),
        P(("wide", "narrow"), None),
        P(("wide", "narrow")),
        P(("wide", "narrow"), None, None),
        P("narrow", None),
        P("narrow", None),
        P("narrow", None),
    )
    return jax.shard_map(
        per_device,
        mesh=mesh,
        in_specs=placed,
        out_specs=(
            P(("wide", "narrow"), None, None),
            P(("wide", "narrow"), None, None),
            P("narrow", None),
            P("narrow", None),
            P("narrow", None),
            P("narrow", None),
        ),
        check_vma=False,
    )
```

```python
import math

import jax
import jax.numpy as jnp
from jax import lax
from jax.experimental import pallas as pl
from jax.experimental.pallas import tpu as pltpu
from jax.sharding import PartitionSpec as P

DE = 768
HE = 12
HD = 64
FE = 3072
DD = 512
HDEC = 4
FD = 2048
PATCH = 256


highest = lax.Precision.HIGHEST
first_bias_fix = 0.9999734386011124
second_bias_fix = 0.994079470779666


def block_segments(prefix, width, inner, hidden):
    names = ("g1", "b1", "qkv", "o", "ob", "g2", "b2", "u", "ub", "v", "vb")
    dims = ((width,), (width,), (width, 3 * inner), (inner, width), (width,), (width,), (width,))
    dims = (*dims, (width, hidden), (hidden,), (hidden, width), (width,))
    return [(prefix + name, size) for name, size in zip(names, dims)]


def segment_list():
    ends = (("fg", (DE,)), ("fb", (DE,)), ("proj", (DE, DD)), ("pb", (DD,)), ("mask", (DD,)))
    return [
        ("cls", (DE,)),
        *block_segments("e", DE, HE * HD, FE),
        *ends,
        *block_segments("d", DD, HDEC * HD, FD),
    ]


MARGIN = 512


def flat_rows():
    table = {}
    offset = 0
    for label, dims_of in segment_list():
        rows = math.prod(dims_of) // 128
        table[label] = (offset, rows)
        offset = offset + rows
    return table, offset


def round_up(value, unit):
    return -(-value // unit) * unit


def group_list():
    firsts = ("cls", "eo", "eu", "ev", "proj", "dqkv", "du", "dv")
    groups = []
    for label, dims in segment_list():
        if label in firsts:
            groups.append([])
        if label == "dg1" or label == "db1" or groups:
            groups[-1].append(label)
    return groups


def unpack(sources, total):
    table, used = flat_rows()
    shapes = dict(segment_list())
    groups = group_list()
    spans = [(table[g[0]][0], sum(table[g[-1]])) for g in groups]
    edges = [0, *[min(round_up(high, 16), total) for low, high in spans]]
    half = total // 2
    copies = []
    for k, (low, high) in enumerate(zip(edges, edges[1:])):
        parts = [(low, high)]
        if len(sources) == 2 and low < half < high:
            parts = [(low, half), (half, high)]
        copies.append(parts)
    slots = [(k, p) for k, parts in enumerate(copies) for p in range(len(parts))]
    labels = [label for label, dims in segment_list()]
    matrices = [label for label, dims in segment_list() if len(dims) == 2]
    deepest = max(round_up(high, 16) - low // 16 * 16 for low, high in spans)

    def kernel(*refs):
        ins, rest = refs[: len(sources)], refs[len(sources) :]
        finals = dict(zip(labels, rest))
        staged, wide_rows, sems, *own, out_sems = rest[len(labels) :]
        outs = {**finals, **dict(zip(matrices, own))}

        def leave(label):
            return pltpu.make_async_copy(
                outs[label], finals[label], out_sems.at[matrices.index(label)]
            )

        def copy(slot, source, shift):
            k, p = slot
            low, high = copies[k][p]
            return pltpu.make_async_copy(
                source.at[pl.ds(low - shift, high - low)],
                staged.at[pl.ds(low, high - low)],
                sems.at[slots.index(slot)],
            )

        if len(sources) == 2:
            mine = lax.axis_index("narrow")
            for slot in slots:
                place = 0 if copies[slot[0]][slot[1]][0] < half else 1

                @pl.when(mine == place)
                def own_part(slot=slot, place=place):
                    copy(slot, ins[0], place * half).start()

                @pl.when(mine != place)
                def other_part(slot=slot, place=place):
                    copy(slot, ins[1], place * half).start()
        else:
            for slot in slots:
                copy(slot, ins[0], 0).start()
        for k, group in enumerate(groups):
            for p in range(len(copies[k])):
                copy((k, p), ins[0], copies[k][p][0]).wait()
            low, high = spans[k]
            origin = low // 16 * 16
            length = round_up(high, 16) - origin

            def widen(i, carry, origin=origin):
                spot = pl.multiple_of(i * 128, 128)
                wide_rows[pl.ds(spot, 128), :] = staged[
                    pl.ds(pl.multiple_of(origin + spot, 16), 128), :
                ].astype(jnp.float32)
                return carry

            lax.fori_loop(0, length // 128, widen, 0)
            done = length // 128 * 128
            if done < length:
                wide_rows[done:length, :] = staged[origin + done : origin + length, :].astype(
                    jnp.float32
                )
            for label in group:
                base = table[label][0] - origin
                dims, ref = shapes[label], outs[label]
                tiles = dims[-1] // 128
                if len(dims) == 1:
                    for c in range(tiles):
                        ref[:, c * 128 : (c + 1) * 128] = wide_rows[base + c : base + c + 1, :]
                    continue

                def step(i, carry, base=base, tiles=tiles, ref=ref):
                    for c in range(tiles):
                        rows = wide_rows[pl.ds(base + i * 16 * tiles + c, 16, stride=tiles), :]
                        ref[pl.ds(pl.multiple_of(i * 16, 16), 16), c * 128 : (c + 1) * 128] = (
                            rows.astype(jnp.bfloat16)
                        )
                    return carry

                lax.fori_loop(0, dims[0] // 16, step, 0)
                leave(label).start()
        for label in matrices:
            leave(label).wait()

    out_shape = [
        jax.ShapeDtypeStruct(dims, jnp.bfloat16)
        if len(dims) == 2
        else jax.ShapeDtypeStruct((1, dims[0]), jnp.float32)
        for label, dims in segment_list()
    ]
    outs = pl.pallas_call(
        kernel,
        out_shape=out_shape,
        in_specs=[pl.BlockSpec(memory_space=pl.ANY)] * len(sources),
        out_specs=[
            pl.BlockSpec(memory_space=pl.ANY if label in matrices else pltpu.VMEM)
            for label in labels
        ],
        scratch_shapes=[
            pltpu.VMEM((total, 128), jnp.bfloat16),
            pltpu.VMEM((deepest, 128), jnp.float32),
            pltpu.SemaphoreType.DMA((len(slots),)),
            *[pltpu.VMEM(shapes[label], jnp.bfloat16) for label in matrices],
            pltpu.SemaphoreType.DMA((len(matrices),)),
        ],
        compiler_params=pltpu.CompilerParams(vmem_limit_bytes=61 << 20),
        name="unpack",
    )(*sources)
    return dict(zip(labels, outs))


def pack_part(pieces, low, high, first, last, held=()):
    table, used = flat_rows()
    labels = [k for k, (off, rows) in table.items() if off < high and off + rows > low]
    arrays, places = [], []
    for k in labels:
        value = pieces[k] if pieces[k].ndim == 2 else pieces[k].reshape(1, -1)
        off, rows = table[k]
        tiles = value.shape[1] // 128
        begin, end = 0, 1
        if value.shape[0] > 1:
            begin = max(0, low - off) // (16 * tiles)
            end = -(-min(rows, high - off) // (16 * tiles))
            if 3 * (end - begin) * 16 < value.shape[0]:
                value = value[begin * 16 : end * 16]
                off, end, begin = off + begin * 16 * tiles, end - begin, 0
        arrays.append(value)
        places.append((off, begin, end))
    length = high - low
    middle = (first + last) // 2
    runs = [
        (max(low, start), min(high, end), place, start)
        for place, (start, end) in enumerate(((first, middle), (middle, last)))
        if max(low, start) < min(high, end)
    ]

    def kernel(*refs):
        ins, rest = refs[: len(labels)], refs[len(labels) + len(held) :]
        kept, sent, flat, out, sems = rest
        if used < high:
            start = max(used, low) - low + MARGIN
            flat[start : MARGIN + length, :] = jnp.zeros((MARGIN + length - start, 128), jnp.float32)
        for (off, begin, end), ref in zip(places, ins):
            tiles = ref.shape[1] // 128
            base = off - low + MARGIN
            if ref.shape[0] == 1:
                for c in range(tiles):
                    spot = base + c
                    if 0 <= spot < length + 2 * MARGIN:
                        flat[spot : spot + 1, :] = ref[:, c * 128 : (c + 1) * 128]
                continue
            block = 16 * tiles

            def step(i, carry, ref=ref, tiles=tiles, base=base, block=block):
                for c in range(tiles):
                    rows = ref[pl.ds(pl.multiple_of(i * 16, 16), 16), c * 128 : (c + 1) * 128]
                    flat[pl.ds(base + i * block + c, 16, stride=tiles), :] = rows.astype(jnp.float32)
                return carry

            lax.fori_loop(begin, end, step, 0)

        def narrow_down(i, carry):
            spot = pl.multiple_of(i * 128, 128)
            out[pl.ds(spot, 128), :] = flat[pl.ds(MARGIN + spot, 128), :].astype(jnp.bfloat16)
            return carry

        lax.fori_loop(0, length // 128, narrow_down, 0)
        mine = lax.axis_index("narrow")

        def copy(n, target):
            start, end, place, origin = runs[n]
            return pltpu.make_async_copy(
                out.at[pl.ds(start - low, end - start)],
                target.at[pl.ds(start - origin, end - start)],
                sems.at[n],
            )

        for n, (start, end, place, origin) in enumerate(runs):

            @pl.when(mine == place)
            def keep(n=n):
                copy(n, kept).start()

            @pl.when(mine != place)
            def send(n=n):
                copy(n, sent).start()

        for n in range(len(runs)):
            copy(n, kept).wait()

    anywhere = pl.BlockSpec(memory_space=pl.ANY)
    whole = pl.BlockSpec(memory_space=pltpu.VMEM)
    return pl.pallas_call(
        kernel,
        out_shape=[jax.ShapeDtypeStruct((middle - first, 128), jnp.bfloat16)] * 2,
        in_specs=[whole] * len(arrays) + [anywhere] * len(held),
        out_specs=[anywhere] * 2,
        input_output_aliases={len(arrays) + n: n for n in range(len(held))},
        scratch_shapes=[
            pltpu.VMEM((length + 2 * MARGIN, 128), jnp.float32),
            pltpu.VMEM((length, 128), jnp.bfloat16),
            pltpu.SemaphoreType.DMA((len(runs),)),
        ],
        compiler_params=pltpu.CompilerParams(vmem_limit_bytes=61 << 20),
        name=f"pack{low}",
    )(*arrays, *held)


def flat_gradient(grads, unit):
    table, used = flat_rows()
    flat = jnp.concatenate([grads[k].astype(jnp.bfloat16).reshape(-1) for k, dims in segment_list()])
    padding = (round_up(used, unit) - used) * 128
    flat = jnp.concatenate([flat, jnp.zeros((padding,), jnp.bfloat16)])
    return flat.reshape(-1, 128)


def added(first, second):
    return (first.astype(jnp.float32) + second.astype(jnp.float32)).astype(jnp.bfloat16)


def piece(value, index, rows):
    return lax.dynamic_slice_in_dim(value, index * rows, rows, 0)


class Line:
    def __init__(self, stride, size):
        self.stride, self.size, self.wide = stride, size, lax.axis_size("wide")
        self.me = (lax.axis_index("wide") // stride) % size
        self.groups = [
            [i + k * stride for k in range(size)]
            for i in range(self.wide)
            if (i // stride) % size == 0
        ]

    def swap(self, value):
        pairs = [pair for a, b in self.groups for pair in ((a, b), (b, a))]
        return lax.ppermute(value, "wide", pairs)

    def exchange(self, value):
        return lax.all_to_all(value, "wide", 0, 0, axis_index_groups=self.groups)

    def scatter(self, value):
        rows = value.shape[0] // self.size
        if self.size == 2:
            got = self.swap(piece(value, 1 - self.me, rows))
            return added(piece(value, self.me, rows), got)
        got = self.exchange(value.reshape(self.size, -1, 128)).astype(jnp.float32)
        return jnp.sum(got, 0).astype(jnp.bfloat16).reshape(rows, -1, 128)

    def gather(self, value):
        if self.size == 2:
            got = self.swap(value)
            low = self.me == 0
            return jnp.concatenate([jnp.where(low, value, got), jnp.where(low, got, value)], 0)
        copies = jnp.broadcast_to(value[None], (self.size, *value.shape))
        return self.exchange(copies).reshape(-1, *value.shape[1:])


def narrow_swap(value, step):
    count = lax.axis_size("narrow")
    return lax.ppermute(value, "narrow", [(i, (i + step) % count) for i in range(count)])


def flat3(value, places):
    return value.reshape(places, -1, 128)


def wide_lines():
    return Line(1, 2), Line(2, 2), Line(4, lax.axis_size("wide") // 4)


def staged_scatter(total):
    x, y, z = wide_lines()
    unit = lax.axis_size("wide") * 8
    most = total.shape[0] // unit * 4 // 11
    first, second = most * unit, 2 * most * unit
    a = total[:first].reshape(2, 2, z.size, -1, 128)
    b = total[first:second].reshape(2, 2, z.size, -1, 128)
    c = total[second:].reshape(z.size, 2, 2, -1, 128)
    c = z.scatter(flat3(c, z.size))
    a = x.scatter(flat3(a, 2))
    b = y.scatter(flat3(b, 2))
    a = y.scatter(flat3(a, 2))
    b = x.scatter(flat3(b, 2))
    a, b, c = lax.optimization_barrier((a, b, c))
    ab = z.scatter(jnp.concatenate([flat3(a, z.size), flat3(b, z.size)], 1))
    c = x.scatter(flat3(c, 2))
    c = y.scatter(flat3(c, 2))
    return lax.optimization_barrier((ab, c))


def staged_gather(ab, c):
    x, y, z = wide_lines()
    ab = z.gather(flat3(ab, 1))
    c = x.gather(y.gather(flat3(c, 1)))
    ab, c = lax.optimization_barrier((ab, c))
    half = ab.shape[1] // 2
    a, b = ab[:, :half], ab[:, half:]
    c = z.gather(flat3(c, 1))
    a = y.gather(flat3(a, 1)).reshape(-1, 128)
    b = x.gather(flat3(b, 1)).reshape(-1, 128)
    pieces = [x.gather(flat3(a, 1)), y.gather(flat3(b, 1)), c]
    return jnp.concatenate([v.reshape(-1, 128) for v in pieces], 0)


def join_pieces(first, second, after):
    pairs = (first, second)
    total = sum(2 * own.shape[0] for line, own, other in pairs)

    def kernel(own1, other1, own2, other2, *rest):
        out, sems = rest[len(after) :]
        copies = []
        start = 0
        for (line, own, other), refs in zip(pairs, ((own1, other1), (own2, other2))):
            rows = own.shape[0]
            me = (lax.axis_index("wide") // line.stride) % 2
            for ref, place in zip(refs, (me, 1 - me)):
                spot = pl.multiple_of(start + place * rows, 8)
                target = out.at[pl.ds(spot, rows)]
                copies.append(pltpu.make_async_copy(ref, target, sems.at[len(copies)]))
            start += 2 * rows
        for copy in copies:
            copy.start()
        for copy in copies:
            copy.wait()

    return pl.pallas_call(
        kernel,
        out_shape=jax.ShapeDtypeStruct((total, 128), first[1].dtype),
        in_specs=[pl.BlockSpec(memory_space=pltpu.VMEM)] * 4
        + [pl.BlockSpec(memory_space=pl.ANY)] * len(after),
        out_specs=pl.BlockSpec(memory_space=pl.ANY),
        scratch_shapes=[pltpu.SemaphoreType.DMA((4,))],
        name="join",
    )(first[1], first[2], second[1], second[2], *after)


def narrow_sum(halves):
    return added(halves[0], narrow_swap(halves[1], 1))


def sum_everywhere(value, rows):
    count = lax.axis_size("narrow")
    mine = lax.axis_index("narrow")
    total = lax.dynamic_slice_in_dim(value, mine * rows, rows, 0)
    for step in range(1, count):
        other = lax.dynamic_slice_in_dim(value, (mine + step) % count * rows, rows, 0)
        total = added(total, narrow_swap(other, step))
    unit = lax.axis_size("wide") * 16
    total = jnp.pad(total, ((0, round_up(rows, unit) - rows), (0, 0)))
    return staged_gather(*staged_scatter(total))[:rows]


def scatter_first(value):
    x, y, z = wide_lines()
    a, b = jnp.split(value, 2)
    return x.scatter(flat3(a, 2)), y.scatter(flat3(b, 2))


def scatter_second(pair):
    x, y, z = wide_lines()
    return y.scatter(flat3(pair[0], 2)), x.scatter(flat3(pair[1], 2))


def scatter_last(pair):
    z = wide_lines()[2]
    both = jnp.concatenate([flat3(v, z.size) for v in pair], 1)
    return z.scatter(both).reshape(-1, 128)


def gather_first(value):
    z = wide_lines()[2]
    value = z.gather(flat3(value, 1))
    half = value.shape[1] // 2
    return flat3(value[:, :half], 1), flat3(value[:, half:], 1)


def gather_second(pair):
    x, y, z = wide_lines()
    return y.gather(pair[0]).reshape(-1, 128), x.gather(pair[1]).reshape(-1, 128)


def gather_last(pair):
    x, y, z = wide_lines()
    a, b = pair
    return (a, x.swap(a)), (b, y.swap(b))


def joined(pairs, after=()):
    x, y, z = wide_lines()
    return join_pieces((x, *pairs[0]), (y, *pairs[1]), after)


BLOCK = 2368


def adam_rows(low, high, moment1, moment2, start, stop, held, chips_all):
    shift = start // BLOCK
    steps = -(-min(stop - start, moment1.shape[0] - start) // BLOCK)
    plans = []
    for place, pieces in enumerate((low, high)):
        for origin, piece_rows in pieces:
            first, last = max(start, origin), min(stop, origin + piece_rows.shape[0])
            if first < last:
                plans.append((place, piece_rows, first - origin, first - start, last - first))

    def kernel(*refs):
        sources, rest = refs[: len(plans)], refs[len(plans) :]
        first, second, *rest = rest
        grad_out, update, new_first, new_second, token, fetched, sems = rest[len(held) :]
        mine = lax.axis_index("narrow")
        step = pl.program_id(0)

        def copy(n):
            place, piece_rows, source_row, row, count = plans[n]
            return pltpu.make_async_copy(
                sources[n].at[pl.ds(source_row, count)], fetched.at[pl.ds(row, count)], sems.at[n]
            )

        for place in range(2):

            @pl.when(jnp.logical_and(step == 0, mine == place))
            def fetch(place=place):
                own = [n for n, plan in enumerate(plans) if plan[0] == place]
                for n in own:
                    copy(n).start()
                for n in own:
                    copy(n).wait()

        token[...] = jnp.zeros((8, 128), jnp.float32)
        spot = pl.multiple_of(step * BLOCK, 16)
        grad = fetched[pl.ds(spot, BLOCK), :].astype(jnp.float32) / chips_all
        grad_out[...] = grad
        update[...], new_first[...], new_second[...] = adam_step(grad, first[...], second[...])

    here = pl.BlockSpec((BLOCK, 128), lambda i: (i + shift, 0))
    anywhere = pl.BlockSpec(memory_space=pl.ANY)
    base = len(plans) + 2
    return pl.pallas_call(
        kernel,
        out_shape=[jax.ShapeDtypeStruct(moment1.shape, jnp.float32)] * 4
        + [jax.ShapeDtypeStruct((8, 128), jnp.float32)],
        grid=(steps,),
        in_specs=[anywhere] * len(plans) + [here, here] + [anywhere] * len(held),
        out_specs=[here] * 4 + [pl.BlockSpec((8, 128), lambda i: (0, 0))],
        scratch_shapes=[
            pltpu.VMEM((max(steps * BLOCK, stop - start), 128), jnp.bfloat16),
            pltpu.SemaphoreType.DMA((len(plans),)),
        ],
        input_output_aliases={base + n: n for n in range(len(held))},
        compiler_params=pltpu.CompilerParams(vmem_limit_bytes=40 << 20),
        cost_estimate=pl.CostEstimate(
            flops=(stop - start) * 128 * 16,
            transcendentals=(stop - start) * 128 * 2,
            bytes_accessed=(stop - start) * 128 * 26,
        ),
        name=f"adam{start}",
    )(*[plan[1] for plan in plans], moment1, moment2, *held)


def to_owner(value, source):
    return lax.ppermute(value, "narrow", [(source, 1 - source)])


def whole_params(params):
    low_params = params.astype(jnp.bfloat16)
    if lax.axis_size("narrow") == 2:
        return (low_params, narrow_swap(low_params, 1))
    return (lax.all_gather(low_params, "narrow", axis=0, tiled=True),)


def position_table():
    half_width = DD // 2
    places = jnp.arange(PATCH, dtype=jnp.float32)[:, None]
    rates = jnp.exp(jnp.arange(half_width, dtype=jnp.float32) * (-math.log(10000.0) / half_width))
    angles = places * rates[None, :]
    return jnp.concatenate([jnp.sin(angles), jnp.cos(angles)], 1)


def layer_norm(stream, gain_vec, bias_vec):
    average = jnp.mean(stream, -1, keepdims=True)
    centred = stream - average
    spread = jnp.mean(centred * centred, -1, keepdims=True)
    return centred * lax.rsqrt(spread + 1e-05) * gain_vec + bias_vec


def vector(weights_map, label):
    return weights_map[label].reshape(-1)


def adam_step(grads, moment1, moment2):
    new_first = 0.9 * moment1 + (1.0 - 0.9) * grads
    new_second = 0.95 * moment2 + (1.0 - 0.95) * grads * grads
    update = new_first / first_bias_fix / (jnp.sqrt(new_second / second_bias_fix) + 1e-08)
    return (update, new_first, new_second)


tail_terms = (
    0.05025708328,
    -0.1828833063,
    0.1690591746,
    -0.005588040603,
    0.141423544,
    0.1685436795,
    0.2078425222,
    0.2256696051,
    0.2256758619,
)


def gelu_and_slope(u):
    t = 1.0 / (1.0 + (0.4 * math.sqrt(0.5)) * jnp.abs(u))
    bell = jnp.exp(-0.5 * u * u)
    tail = 0.5 * tail_terms[0]
    for term in tail_terms[1:]:
        tail = tail * t + 0.5 * term
    tail = tail * t * bell
    below = jnp.where(u < 0, tail, 1.0 - tail)
    slope = below + u * bell * (1.0 / math.sqrt(2.0 * math.pi))
    return (u * below).astype(jnp.bfloat16), slope.astype(jnp.bfloat16)


def block_forward(stream, weights_map, prefix, heads):
    chips, tokens, width = stream.shape
    inner = heads * HD
    normed1 = layer_norm(
        stream,
        vector(weights_map, prefix + "g1"),
        vector(weights_map, prefix + "b1"),
    )
    first_in = normed1.astype(jnp.bfloat16)
    triple = jnp.einsum(
        "ctd,de->cte", first_in, weights_map[prefix + "qkv"], preferred_element_type=jnp.float32
    ).astype(jnp.bfloat16)
    query_rows = triple[:, :, :inner].reshape(chips, tokens, heads, HD)
    key_rows = triple[:, :, inner : 2 * inner].reshape(chips, tokens, heads, HD)
    value_rows = triple[:, :, 2 * inner :].reshape(chips, tokens, heads, HD)
    scores = jnp.einsum(
        "cqhe,ckhe->chqk", query_rows, key_rows, preferred_element_type=jnp.float32
    ) * HD ** (-0.5)
    topmost = jnp.max(scores, -1, keepdims=True)
    expos = jnp.exp(scores - topmost)
    totals = jnp.sum(expos, -1, keepdims=True)
    logsum = topmost + jnp.log(totals)
    probs = (expos / totals).astype(jnp.bfloat16)
    mixed = jnp.einsum("chqk,ckhe->cqhe", probs, value_rows, preferred_element_type=jnp.float32)
    mixed = mixed.reshape(chips, tokens, inner).astype(jnp.bfloat16)
    middle = (
        stream
        + jnp.einsum(
            "cti,id->ctd", mixed, weights_map[prefix + "o"], preferred_element_type=jnp.float32
        )
        + vector(weights_map, prefix + "ob")
    )
    normed2 = layer_norm(
        middle,
        vector(weights_map, prefix + "g2"),
        vector(weights_map, prefix + "b2"),
    )
    second_in = normed2.astype(jnp.bfloat16)
    hidden_pre = jnp.einsum(
        "ctd,df->ctf", second_in, weights_map[prefix + "u"], preferred_element_type=jnp.float32
    ) + vector(weights_map, prefix + "ub")
    activ, slope = lax.optimization_barrier(gelu_and_slope(hidden_pre))
    result = (
        middle
        + jnp.einsum(
            "ctf,fd->ctd", activ, weights_map[prefix + "v"], preferred_element_type=jnp.float32
        )
        + vector(weights_map, prefix + "vb")
    )
    kept = (
        stream,
        middle,
        first_in,
        query_rows,
        key_rows,
        value_rows,
        logsum,
        mixed,
        second_in,
        slope,
        activ,
    )
    return (result, kept)


def norm_backward(stream, weights_map, gain_label, bias_label, upstream):
    pull = jax.vjp(
        layer_norm, stream, vector(weights_map, gain_label), vector(weights_map, bias_label)
    )[1]
    return pull(upstream)


def mlp_backward(upstream, kept, weights_map, prefix):
    middle, second_in, slope = kept[1], kept[8], kept[9]
    grads = {}
    branch_two = upstream.astype(jnp.bfloat16)
    grads[prefix + "vb"] = jnp.sum(branch_two.astype(jnp.float32), (0, 1))
    d_activ = jnp.einsum(
        "ctd,fd->ctf", branch_two, weights_map[prefix + "v"], preferred_element_type=jnp.float32
    )
    d_hidden = (d_activ * slope.astype(jnp.float32)).astype(jnp.bfloat16)
    grads[prefix + "ub"] = jnp.sum(d_hidden.astype(jnp.float32), (0, 1))
    d_second = jnp.einsum(
        "ctf,df->ctd", d_hidden, weights_map[prefix + "u"], preferred_element_type=jnp.float32
    )
    d_middle_part, grads[prefix + "g2"], grads[prefix + "b2"] = norm_backward(
        middle, weights_map, prefix + "g2", prefix + "b2", d_second
    )
    return upstream + d_middle_part, d_hidden, grads


def hidden_gradient(kept, d_hidden):
    return jnp.einsum(
        "ctd,ctf->df", kept[8], d_hidden, preferred_element_type=jnp.float32
    ).astype(jnp.bfloat16)


def output_gradient(kept, upstream):
    return jnp.einsum(
        "ctf,ctd->fd", kept[10], upstream.astype(jnp.bfloat16), preferred_element_type=jnp.float32
    ).astype(jnp.bfloat16)


def scores_backward(d_middle, kept, weights_map, prefix, heads):
    query_rows, key_rows, value_rows, logsum = kept[3:7]
    chips, tokens, width = d_middle.shape
    branch_one = d_middle.astype(jnp.bfloat16)
    d_mixed = jnp.einsum(
        "ctd,id->cti", branch_one, weights_map[prefix + "o"], preferred_element_type=jnp.float32
    )
    d_mixed = d_mixed.astype(jnp.bfloat16).reshape(chips, tokens, heads, HD)
    scores = jnp.einsum(
        "cqhe,ckhe->chqk", query_rows, key_rows, preferred_element_type=jnp.float32
    ) * HD ** (-0.5)
    probs_full = jnp.exp(scores - logsum)
    probs_low = probs_full.astype(jnp.bfloat16)
    d_value = jnp.einsum("chqk,cqhe->ckhe", probs_low, d_mixed, preferred_element_type=jnp.float32)
    d_probs = jnp.einsum("cqhe,ckhe->chqk", d_mixed, value_rows, preferred_element_type=jnp.float32)
    row_shift = jnp.sum(d_probs * probs_full, -1, keepdims=True)
    d_scores = (probs_full * (d_probs - row_shift)).astype(jnp.bfloat16)
    return d_scores, d_value.astype(jnp.bfloat16)


def stream_backward(d_middle, d_scores, d_value, kept, weights_map, prefix, heads):
    stream, first_in, query_rows, key_rows, mixed = kept[0], kept[2], kept[3], kept[4], kept[7]
    chips, tokens, width = stream.shape
    inner = heads * HD
    grads = {}
    branch_one = d_middle.astype(jnp.bfloat16)
    grads[prefix + "ob"] = jnp.sum(branch_one.astype(jnp.float32), (0, 1))
    grads[prefix + "o"] = jnp.einsum(
        "cti,ctd->id", mixed, branch_one, preferred_element_type=jnp.float32
    ).astype(jnp.bfloat16)
    d_query = jnp.einsum(
        "chqk,ckhe->cqhe", d_scores, key_rows, preferred_element_type=jnp.float32
    ) * HD ** (-0.5)
    d_key = jnp.einsum(
        "chqk,cqhe->ckhe", d_scores, query_rows, preferred_element_type=jnp.float32
    ) * HD ** (-0.5)
    d_triple = jnp.concatenate(
        [
            d_query.reshape(chips, tokens, inner).astype(jnp.bfloat16),
            d_key.reshape(chips, tokens, inner).astype(jnp.bfloat16),
            d_value.reshape(chips, tokens, inner),
        ],
        -1,
    )
    grads[prefix + "qkv"] = jnp.einsum(
        "ctd,cte->de", first_in, d_triple, preferred_element_type=jnp.float32
    ).astype(jnp.bfloat16)
    d_first = jnp.einsum(
        "cte,de->ctd", d_triple, weights_map[prefix + "qkv"], preferred_element_type=jnp.float32
    )
    d_stream_part, grads[prefix + "g1"], grads[prefix + "b1"] = norm_backward(
        stream, weights_map, prefix + "g1", prefix + "b1", d_first
    )
    return (d_middle + d_stream_part, grads)


def per_device(patches, timeloc, visible, masked, flags, cotangent, params, moment1, moment2):
    total_rows = params.shape[0] * lax.axis_size("narrow")
    weights_map = unpack(whole_params(params), total_rows)
    chips = patches.shape[0]
    patch_ids = jnp.arange(PATCH, dtype=jnp.int32)
    chooser = visible[:, :, None] == patch_ids[None, None, :]
    choose_low = chooser.astype(jnp.bfloat16)
    choose_full = chooser.astype(jnp.float32)
    picked = jnp.einsum("cvp,cpd->cvd", choose_low, patches, preferred_element_type=jnp.float32)
    keep_meta = (1 - flags).astype(jnp.float32)
    meta_row = timeloc.astype(jnp.float32) * keep_meta[:, None]
    class_row = jnp.broadcast_to(vector(weights_map, "cls")[None, None, :], (chips, 1, DE))
    enc_in = jnp.concatenate([class_row, meta_row[:, None, :], picked], 1)
    enc_out, enc_kept = block_forward(enc_in, weights_map, "e", HE)
    patch_rows = enc_out[:, 2:, :]
    final_gain = vector(weights_map, "fg")
    final_bias = vector(weights_map, "fb")
    encoded_low = layer_norm(patch_rows, final_gain, final_bias).astype(jnp.bfloat16)
    projected = jnp.einsum(
        "cvd,de->cve", encoded_low, weights_map["proj"], preferred_element_type=jnp.float32
    ) + vector(weights_map, "pb")
    filled = jnp.einsum("cvp,cve->cpe", choose_full, projected, precision=highest)
    mask_rows = 1.0 - jnp.sum(choose_full, 1)
    dec_in = (
        filled
        + mask_rows[:, :, None] * vector(weights_map, "mask")[None, None, :]
        + position_table()[None]
    )
    dec_out, dec_kept = block_forward(dec_in, weights_map, "d", HDEC)
    tie = lax.optimization_barrier
    chunked = lax.axis_size("narrow") == 2 and lax.axis_size("wide") == 16
    half_rows = params.shape[0]
    padded = round_up(half_rows, 512)
    upper = (half_rows, half_rows + padded)
    upstream = cotangent.astype(jnp.float32)
    d_mid, d_hidden, grads = mlp_backward(upstream, dec_kept, weights_map, "d")
    grads["du"] = hidden_gradient(dec_kept, d_hidden)
    grads["dv"] = output_gradient(dec_kept, upstream)
    if chunked:
        cut = round_up(flat_rows()[0]["du"][0], 128)
        held = pack_part(grads, cut, upper[1], *upper)
        d_mid, held = tie((d_mid, held))
    attention = scores_backward(d_mid, dec_kept, weights_map, "d", HDEC)
    d_dec_in, more = stream_backward(d_mid, *attention, dec_kept, weights_map, "d", HDEC)
    grads.update(more)
    grads["mask"] = jnp.sum(mask_rows[:, :, None] * d_dec_in, (0, 1))
    d_projected = jnp.einsum("cvp,cpe->cve", choose_full, d_dec_in, precision=highest).astype(
        jnp.bfloat16
    )
    grads["pb"] = jnp.sum(d_projected.astype(jnp.float32), (0, 1))
    grads["proj"] = jnp.einsum(
        "cvd,cve->de", encoded_low, d_projected, preferred_element_type=jnp.float32
    ).astype(jnp.bfloat16)
    d_encoded = jnp.einsum(
        "cve,de->cvd", d_projected, weights_map["proj"], preferred_element_type=jnp.float32
    )
    final_pull = jax.vjp(layer_norm, patch_rows, final_gain, final_bias)[1]
    d_patch_rows, grads["fg"], grads["fb"] = final_pull(d_encoded)
    d_enc_out = jnp.concatenate([jnp.zeros((chips, 2, DE), jnp.float32), d_patch_rows], 1)
    grads["ev"] = output_gradient(enc_kept, d_enc_out)
    grads["evb"] = jnp.sum(d_enc_out.astype(jnp.bfloat16).astype(jnp.float32), (0, 1))
    if chunked:
        high = pack_part(grads, half_rows, cut, *upper, held)
        d_enc_out, high = tie((d_enc_out, high))
        high = scatter_first(narrow_sum(high))
    d_mid, d_hidden, more = mlp_backward(d_enc_out, enc_kept, weights_map, "e")
    grads.update(more)
    grads["eu"] = hidden_gradient(enc_kept, d_hidden)
    if chunked:
        cut = round_up(flat_rows()[0]["eu"][0], 512)
        late = pack_part(grads, cut, padded, cut, padded)
        d_mid, late, high = tie((d_mid, late, high))
        high = scatter_second(high)
        late = scatter_first(narrow_sum(late))
    attention = scores_backward(d_mid, enc_kept, weights_map, "e", HE)
    if chunked:
        attention, d_mid, high, late = tie((attention, d_mid, high, late))
        high = scatter_last(high)
        late = scatter_second(late)
    d_enc_in, more = stream_backward(d_mid, *attention, enc_kept, weights_map, "e", HE)
    grads.update(more)
    grads["cls"] = jnp.sum(d_enc_in[:, 0, :], 0)
    chips_all = float(chips * lax.axis_size("wide") * lax.axis_size("narrow"))
    if chunked:
        low = pack_part(grads, 0, cut, 0, cut)
        d_enc_in, low, high, late = tie((d_enc_in, low, high, late))
        high = gather_first(high)
        late = scatter_last(late)
        low = scatter_second(scatter_first(narrow_sum(low)))
    patch_grad = jnp.einsum(
        "cvp,cvd->cpd", choose_full, d_enc_in[:, 2:, :], precision=highest
    ).astype(jnp.bfloat16)
    if chunked:
        patch_grad, low, high, late = tie((patch_grad, low, high, late))
        high = gather_last(gather_second(high))
        late = gather_first(late)
        low = scatter_last(low)
        low, high, late = tie((low, high, late))
        high = joined(high)
        late = gather_last(gather_second(late))
        low = gather_first(low)
        other_high = to_owner(high, 0)
        low, high, other_high, late = tie((low, high, other_high, late))
        late = joined(late)
        other_late = to_owner(late, 1)
        low = gather_second(low)
        low, late, other_late = tie((low, late, other_late))
        pieces = ((cut, late), (cut + late.shape[0], other_late))
        uppers = ((0, other_high), (other_high.shape[0], high))
        *held, token = adam_rows(pieces, uppers, moment1, moment2, cut, padded, (), chips_all)
        low = joined(gather_last(low), (token,))
        pieces = ((0, low), (low.shape[0], to_owner(low, 1)))
        grad_out, update, new_moment1, new_moment2, token = adam_rows(
            pieces, uppers, moment1, moment2, 0, cut, held, chips_all
        )
    else:
        every = flat_gradient(grads, half_rows * lax.axis_size("narrow"))
        grad_out = sum_everywhere(every, half_rows).astype(jnp.float32) / chips_all
        update, new_moment1, new_moment2 = adam_step(grad_out, moment1, moment2)
    return (dec_out.astype(jnp.bfloat16), patch_grad, grad_out, update, new_moment1, new_moment2)


def solution(mesh):
    placed = (
        P(("wide", "narrow"), None, None),
        P(("wide", "narrow"), None),
        P(("wide", "narrow"), None),
        P(("wide", "narrow"), None),
        P(("wide", "narrow")),
        P(("wide", "narrow"), None, None),
        P("narrow", None),
        P("narrow", None),
        P("narrow", None),
    )
    return jax.shard_map(
        per_device,
        mesh=mesh,
        in_specs=placed,
        out_specs=(
            P(("wide", "narrow"), None, None),
            P(("wide", "narrow"), None, None),
            P("narrow", None),
            P("narrow", None),
            P("narrow", None),
            P("narrow", None),
        ),
        check_vma=False,
    )
```

```python
import math

import jax
import jax.numpy as jnp
from jax import lax
from jax.experimental import pallas as pl
from jax.experimental.pallas import tpu as pltpu
from jax.sharding import PartitionSpec as P

DE = 768
HE = 12
HD = 64
FE = 3072
DD = 512
HDEC = 4
FD = 2048
PATCH = 256


highest = lax.Precision.HIGHEST
first_bias_fix = 0.9999734386011124
second_bias_fix = 0.994079470779666


def block_segments(prefix, width, inner, hidden):
    names = ("g1", "b1", "qkv", "o", "ob", "g2", "b2", "u", "ub", "v", "vb")
    dims = ((width,), (width,), (width, 3 * inner), (inner, width), (width,), (width,), (width,))
    dims = (*dims, (width, hidden), (hidden,), (hidden, width), (width,))
    return [(prefix + name, size) for name, size in zip(names, dims)]


def segment_list():
    ends = (("fg", (DE,)), ("fb", (DE,)), ("proj", (DE, DD)), ("pb", (DD,)), ("mask", (DD,)))
    return [
        ("cls", (DE,)),
        *block_segments("e", DE, HE * HD, FE),
        *ends,
        *block_segments("d", DD, HDEC * HD, FD),
    ]


MARGIN = 512


def flat_rows():
    table = {}
    offset = 0
    for label, dims_of in segment_list():
        rows = math.prod(dims_of) // 128
        table[label] = (offset, rows)
        offset = offset + rows
    return table, offset


def round_up(value, unit):
    return -(-value // unit) * unit


def group_list():
    firsts = ("cls", "eo", "eu", "ev", "proj", "dqkv", "du", "dv")
    groups = []
    for label, dims in segment_list():
        if label in firsts:
            groups.append([])
        if label == "dg1" or label == "db1" or groups:
            groups[-1].append(label)
    return groups


def unpack(sources, total):
    table, used = flat_rows()
    shapes = dict(segment_list())
    groups = group_list()
    spans = [(table[g[0]][0], sum(table[g[-1]])) for g in groups]
    edges = [0, *[min(round_up(high, 16), total) for low, high in spans]]
    half = total // 2
    copies = []
    for k, (low, high) in enumerate(zip(edges, edges[1:])):
        parts = [(low, high)]
        if len(sources) == 2 and low < half < high:
            parts = [(low, half), (half, high)]
        copies.append(parts)
    slots = [(k, p) for k, parts in enumerate(copies) for p in range(len(parts))]
    labels = [label for label, dims in segment_list()]
    matrices = [label for label, dims in segment_list() if len(dims) == 2]
    deepest = max(round_up(high, 16) - low // 16 * 16 for low, high in spans)

    def kernel(*refs):
        ins, rest = refs[: len(sources)], refs[len(sources) :]
        finals = dict(zip(labels, rest))
        staged, wide_rows, sems, *own, out_sems = rest[len(labels) :]
        outs = {**finals, **dict(zip(matrices, own))}

        def leave(label):
            return pltpu.make_async_copy(
                outs[label], finals[label], out_sems.at[matrices.index(label)]
            )

        def copy(slot, source, shift):
            k, p = slot
            low, high = copies[k][p]
            return pltpu.make_async_copy(
                source.at[pl.ds(low - shift, high - low)],
                staged.at[pl.ds(low, high - low)],
                sems.at[slots.index(slot)],
            )

        if len(sources) == 2:
            mine = lax.axis_index("narrow")
            for slot in slots:
                place = 0 if copies[slot[0]][slot[1]][0] < half else 1

                @pl.when(mine == place)
                def own_part(slot=slot, place=place):
                    copy(slot, ins[0], place * half).start()

                @pl.when(mine != place)
                def other_part(slot=slot, place=place):
                    copy(slot, ins[1], place * half).start()
        else:
            for slot in slots:
                copy(slot, ins[0], 0).start()
        for k, group in enumerate(groups):
            for p in range(len(copies[k])):
                copy((k, p), ins[0], copies[k][p][0]).wait()
            low, high = spans[k]
            origin = low // 16 * 16
            length = round_up(high, 16) - origin

            def widen(i, carry, origin=origin):
                spot = pl.multiple_of(i * 128, 128)
                wide_rows[pl.ds(spot, 128), :] = staged[
                    pl.ds(pl.multiple_of(origin + spot, 16), 128), :
                ].astype(jnp.float32)
                return carry

            lax.fori_loop(0, length // 128, widen, 0)
            done = length // 128 * 128
            if done < length:
                wide_rows[done:length, :] = staged[origin + done : origin + length, :].astype(
                    jnp.float32
                )
            for label in group:
                base = table[label][0] - origin
                dims, ref = shapes[label], outs[label]
                tiles = dims[-1] // 128
                if len(dims) == 1:
                    for c in range(tiles):
                        ref[:, c * 128 : (c + 1) * 128] = wide_rows[base + c : base + c + 1, :]
                    continue

                def step(i, carry, base=base, tiles=tiles, ref=ref):
                    for c in range(tiles):
                        rows = wide_rows[pl.ds(base + i * 16 * tiles + c, 16, stride=tiles), :]
                        ref[pl.ds(pl.multiple_of(i * 16, 16), 16), c * 128 : (c + 1) * 128] = (
                            rows.astype(jnp.bfloat16)
                        )
                    return carry

                lax.fori_loop(0, dims[0] // 16, step, 0)
                leave(label).start()
        for label in matrices:
            leave(label).wait()

    out_shape = [
        jax.ShapeDtypeStruct(dims, jnp.bfloat16)
        if len(dims) == 2
        else jax.ShapeDtypeStruct((1, dims[0]), jnp.float32)
        for label, dims in segment_list()
    ]
    outs = pl.pallas_call(
        kernel,
        out_shape=out_shape,
        in_specs=[pl.BlockSpec(memory_space=pl.ANY)] * len(sources),
        out_specs=[
            pl.BlockSpec(memory_space=pl.ANY if label in matrices else pltpu.VMEM)
            for label in labels
        ],
        scratch_shapes=[
            pltpu.VMEM((total, 128), jnp.bfloat16),
            pltpu.VMEM((deepest, 128), jnp.float32),
            pltpu.SemaphoreType.DMA((len(slots),)),
            *[pltpu.VMEM(shapes[label], jnp.bfloat16) for label in matrices],
            pltpu.SemaphoreType.DMA((len(matrices),)),
        ],
        compiler_params=pltpu.CompilerParams(vmem_limit_bytes=61 << 20),
        name="unpack",
    )(*sources)
    return dict(zip(labels, outs))


def pack_part(pieces, low, high, first, last, held=()):
    table, used = flat_rows()
    labels = [k for k, (off, rows) in table.items() if off < high and off + rows > low]
    arrays, places = [], []
    for k in labels:
        value = pieces[k] if pieces[k].ndim == 2 else pieces[k].reshape(1, -1)
        off, rows = table[k]
        tiles = value.shape[1] // 128
        begin, end = 0, 1
        if value.shape[0] > 1:
            begin = max(0, low - off) // (16 * tiles)
            end = -(-min(rows, high - off) // (16 * tiles))
            if 3 * (end - begin) * 16 < value.shape[0]:
                value = value[begin * 16 : end * 16]
                off, end, begin = off + begin * 16 * tiles, end - begin, 0
        arrays.append(value)
        places.append((off, begin, end))
    length = high - low
    middle = (first + last) // 2
    runs = [
        (max(low, start), min(high, end), place, start)
        for place, (start, end) in enumerate(((first, middle), (middle, last)))
        if max(low, start) < min(high, end)
    ]

    def kernel(*refs):
        ins, rest = refs[: len(labels)], refs[len(labels) + len(held) :]
        kept, sent, flat, out, sems = rest
        if used < high:
            start = max(used, low) - low + MARGIN
            flat[start : MARGIN + length, :] = jnp.zeros((MARGIN + length - start, 128), jnp.float32)
        for (off, begin, end), ref in zip(places, ins):
            tiles = ref.shape[1] // 128
            base = off - low + MARGIN
            if ref.shape[0] == 1:
                for c in range(tiles):
                    spot = base + c
                    if 0 <= spot < length + 2 * MARGIN:
                        flat[spot : spot + 1, :] = ref[:, c * 128 : (c + 1) * 128]
                continue
            block = 16 * tiles

            def step(i, carry, ref=ref, tiles=tiles, base=base, block=block):
                for c in range(tiles):
                    rows = ref[pl.ds(pl.multiple_of(i * 16, 16), 16), c * 128 : (c + 1) * 128]
                    flat[pl.ds(base + i * block + c, 16, stride=tiles), :] = rows.astype(jnp.float32)
                return carry

            lax.fori_loop(begin, end, step, 0)

        def narrow_down(i, carry):
            spot = pl.multiple_of(i * 128, 128)
            out[pl.ds(spot, 128), :] = flat[pl.ds(MARGIN + spot, 128), :].astype(jnp.bfloat16)
            return carry

        lax.fori_loop(0, length // 128, narrow_down, 0)
        mine = lax.axis_index("narrow")

        def copy(n, target):
            start, end, place, origin = runs[n]
            return pltpu.make_async_copy(
                out.at[pl.ds(start - low, end - start)],
                target.at[pl.ds(start - origin, end - start)],
                sems.at[n],
            )

        for n, (start, end, place, origin) in enumerate(runs):

            @pl.when(mine == place)
            def keep(n=n):
                copy(n, kept).start()

            @pl.when(mine != place)
            def send(n=n):
                copy(n, sent).start()

        for n in range(len(runs)):
            copy(n, kept).wait()

    anywhere = pl.BlockSpec(memory_space=pl.ANY)
    whole = pl.BlockSpec(memory_space=pltpu.VMEM)
    return pl.pallas_call(
        kernel,
        out_shape=[jax.ShapeDtypeStruct((middle - first, 128), jnp.bfloat16)] * 2,
        in_specs=[whole] * len(arrays) + [anywhere] * len(held),
        out_specs=[anywhere] * 2,
        input_output_aliases={len(arrays) + n: n for n in range(len(held))},
        scratch_shapes=[
            pltpu.VMEM((length + 2 * MARGIN, 128), jnp.float32),
            pltpu.VMEM((length, 128), jnp.bfloat16),
            pltpu.SemaphoreType.DMA((len(runs),)),
        ],
        compiler_params=pltpu.CompilerParams(vmem_limit_bytes=61 << 20),
        name=f"pack{low}",
    )(*arrays, *held)


def flat_gradient(grads, unit):
    table, used = flat_rows()
    flat = jnp.concatenate([grads[k].astype(jnp.bfloat16).reshape(-1) for k, dims in segment_list()])
    padding = (round_up(used, unit) - used) * 128
    flat = jnp.concatenate([flat, jnp.zeros((padding,), jnp.bfloat16)])
    return flat.reshape(-1, 128)


def added(first, second):
    return (first.astype(jnp.float32) + second.astype(jnp.float32)).astype(jnp.bfloat16)


def piece(value, index, rows):
    return lax.dynamic_slice_in_dim(value, index * rows, rows, 0)


class Line:
    def __init__(self, stride, size):
        self.stride, self.size, self.wide = stride, size, lax.axis_size("wide")
        self.me = (lax.axis_index("wide") // stride) % size
        self.groups = [
            [i + k * stride for k in range(size)]
            for i in range(self.wide)
            if (i // stride) % size == 0
        ]

    def swap(self, value):
        pairs = [pair for a, b in self.groups for pair in ((a, b), (b, a))]
        return lax.ppermute(value, "wide", pairs)

    def exchange(self, value):
        return lax.all_to_all(value, "wide", 0, 0, axis_index_groups=self.groups)

    def scatter(self, value):
        rows = value.shape[0] // self.size
        if self.size == 2:
            got = self.swap(piece(value, 1 - self.me, rows))
            return added(piece(value, self.me, rows), got)
        got = self.exchange(value.reshape(self.size, -1, 128)).astype(jnp.float32)
        return jnp.sum(got, 0).astype(jnp.bfloat16).reshape(rows, -1, 128)

    def gather(self, value):
        if self.size == 2:
            got = self.swap(value)
            low = self.me == 0
            return jnp.concatenate([jnp.where(low, value, got), jnp.where(low, got, value)], 0)
        copies = jnp.broadcast_to(value[None], (self.size, *value.shape))
        return self.exchange(copies).reshape(-1, *value.shape[1:])


def narrow_swap(value, step):
    count = lax.axis_size("narrow")
    return lax.ppermute(value, "narrow", [(i, (i + step) % count) for i in range(count)])


def flat3(value, places):
    return value.reshape(places, -1, 128)


def wide_lines():
    return Line(1, 2), Line(2, 2), Line(4, lax.axis_size("wide") // 4)


def staged_scatter(total):
    x, y, z = wide_lines()
    unit = lax.axis_size("wide") * 8
    most = total.shape[0] // unit * 4 // 11
    first, second = most * unit, 2 * most * unit
    a = total[:first].reshape(2, 2, z.size, -1, 128)
    b = total[first:second].reshape(2, 2, z.size, -1, 128)
    c = total[second:].reshape(z.size, 2, 2, -1, 128)
    c = z.scatter(flat3(c, z.size))
    a = x.scatter(flat3(a, 2))
    b = y.scatter(flat3(b, 2))
    a = y.scatter(flat3(a, 2))
    b = x.scatter(flat3(b, 2))
    a, b, c = lax.optimization_barrier((a, b, c))
    ab = z.scatter(jnp.concatenate([flat3(a, z.size), flat3(b, z.size)], 1))
    c = x.scatter(flat3(c, 2))
    c = y.scatter(flat3(c, 2))
    return lax.optimization_barrier((ab, c))


def staged_gather(ab, c):
    x, y, z = wide_lines()
    ab = z.gather(flat3(ab, 1))
    c = x.gather(y.gather(flat3(c, 1)))
    ab, c = lax.optimization_barrier((ab, c))
    half = ab.shape[1] // 2
    a, b = ab[:, :half], ab[:, half:]
    c = z.gather(flat3(c, 1))
    a = y.gather(flat3(a, 1)).reshape(-1, 128)
    b = x.gather(flat3(b, 1)).reshape(-1, 128)
    pieces = [x.gather(flat3(a, 1)), y.gather(flat3(b, 1)), c]
    return jnp.concatenate([v.reshape(-1, 128) for v in pieces], 0)


def join_pieces(first, second):
    pairs = (first, second)
    total = sum(2 * own.shape[0] for line, own, other in pairs)

    def kernel(own1, other1, own2, other2, out, sems):
        copies = []
        start = 0
        for (line, own, other), refs in zip(pairs, ((own1, other1), (own2, other2))):
            rows = own.shape[0]
            me = (lax.axis_index("wide") // line.stride) % 2
            for ref, place in zip(refs, (me, 1 - me)):
                spot = pl.multiple_of(start + place * rows, 8)
                target = out.at[pl.ds(spot, rows)]
                copies.append(pltpu.make_async_copy(ref, target, sems.at[len(copies)]))
            start += 2 * rows
        for copy in copies:
            copy.start()
        for copy in copies:
            copy.wait()

    return pl.pallas_call(
        kernel,
        out_shape=jax.ShapeDtypeStruct((total, 128), first[1].dtype),
        in_specs=[pl.BlockSpec(memory_space=pltpu.VMEM)] * 4,
        out_specs=pl.BlockSpec(memory_space=pl.ANY),
        scratch_shapes=[pltpu.SemaphoreType.DMA((4,))],
        name="join",
    )(first[1], first[2], second[1], second[2])


def narrow_sum(halves):
    return added(halves[0], narrow_swap(halves[1], 1))


def sum_everywhere(value, rows):
    count = lax.axis_size("narrow")
    mine = lax.axis_index("narrow")
    total = lax.dynamic_slice_in_dim(value, mine * rows, rows, 0)
    for step in range(1, count):
        other = lax.dynamic_slice_in_dim(value, (mine + step) % count * rows, rows, 0)
        total = added(total, narrow_swap(other, step))
    unit = lax.axis_size("wide") * 16
    total = jnp.pad(total, ((0, round_up(rows, unit) - rows), (0, 0)))
    return staged_gather(*staged_scatter(total))[:rows]


def scatter_first(value):
    x, y, z = wide_lines()
    a, b = jnp.split(value, 2)
    return x.scatter(flat3(a, 2)), y.scatter(flat3(b, 2))


def scatter_second(pair):
    x, y, z = wide_lines()
    return y.scatter(flat3(pair[0], 2)), x.scatter(flat3(pair[1], 2))


def scatter_last(pair):
    z = wide_lines()[2]
    both = jnp.concatenate([flat3(v, z.size) for v in pair], 1)
    return z.scatter(both).reshape(-1, 128)


def gather_first(value):
    z = wide_lines()[2]
    value = z.gather(flat3(value, 1))
    half = value.shape[1] // 2
    return flat3(value[:, :half], 1), flat3(value[:, half:], 1)


def gather_second(pair):
    x, y, z = wide_lines()
    return y.gather(pair[0]).reshape(-1, 128), x.gather(pair[1]).reshape(-1, 128)


def gather_last(pair):
    x, y, z = wide_lines()
    a, b = pair
    return (a, x.swap(a)), (b, y.swap(b))


def joined(pairs):
    x, y, z = wide_lines()
    return join_pieces((x, *pairs[0]), (y, *pairs[1]))


def adam_rows(low, high, moment1, moment2, flip, held, chips_all):
    block = low[0].shape[0] // 2
    x, y, z = wide_lines()

    def kernel(places, low0, low1, low2, low3, high0, high1, first, second, *rest):
        grad_out, update, new_first, new_second, token = rest[len(held) :]
        i = pl.program_id(0)
        early = jnp.where(i < 2, low0[...], low1[...])
        lower = jnp.where(i < 4, early, jnp.where(i < 6, low2[...], low3[...]))
        upper = jnp.where(i < 4, high0[...], high1[...])
        grad = jnp.where(places[0] == 0, lower, upper).astype(jnp.float32) / chips_all
        grad_out[...] = grad
        update[...], new_first[...], new_second[...] = adam_step(grad, first[...], second[...])
        token[...] = jnp.zeros((8, 128), jnp.float32)

    def spot(i, places):
        part = i // 2 % 2
        return part * 4 + jnp.where(part == 0, places[1], places[2]) * 2 + i % 2

    def low_spec(n):
        return pl.BlockSpec(
            (block, 128),
            lambda i, places: (jnp.where(places[0] == 0, jnp.clip(i - 2 * n, 0, 1), 0), 0),
        )

    def high_spec(n):
        def place(i, places):
            wanted = jnp.logical_and(places[0] == 1, i // 4 == n)
            return jnp.where(wanted, spot(i, places), 0), 0

        return pl.BlockSpec((block, 128), place)

    here = pl.BlockSpec((block, 128), lambda i, places: (i // 4 * 8 + spot(i, places), 0))
    mark = pl.BlockSpec((8, 128), lambda i, places: (0, 0))
    rows = 8 * block
    places = [lax.axis_index("narrow"), x.me ^ flip, y.me ^ flip]
    places = jnp.stack([place.astype(jnp.int32) for place in places])
    in_specs = [low_spec(n) for n in range(4)] + [high_spec(n) for n in range(2)] + [here, here]
    return pl.pallas_call(
        kernel,
        out_shape=[jax.ShapeDtypeStruct(moment1.shape, jnp.float32)] * 4
        + [jax.ShapeDtypeStruct((8, 128), jnp.float32)],
        grid_spec=pltpu.PrefetchScalarGridSpec(
            num_scalar_prefetch=1,
            grid=(8,),
            in_specs=in_specs + [pl.BlockSpec(memory_space=pl.ANY)] * len(held),
            out_specs=[here] * 4 + [mark],
        ),
        input_output_aliases={9 + n: n for n in range(min(4, len(held)))},
        compiler_params=pltpu.CompilerParams(vmem_limit_bytes=40 << 20),
        cost_estimate=pl.CostEstimate(
            flops=rows * 128 * 16, transcendentals=rows * 128 * 2, bytes_accessed=rows * 128 * 26
        ),
        name=f"adam{flip}",
    )(places, *low, *high, moment1, moment2, *held)


def to_owner(value, source):
    return lax.ppermute(value, "narrow", [(source, 1 - source)])


def whole_params(params):
    low_params = params.astype(jnp.bfloat16)
    if lax.axis_size("narrow") == 2:
        return (low_params, narrow_swap(low_params, 1))
    return (lax.all_gather(low_params, "narrow", axis=0, tiled=True),)


def position_table():
    half_width = DD // 2
    places = jnp.arange(PATCH, dtype=jnp.float32)[:, None]
    rates = jnp.exp(jnp.arange(half_width, dtype=jnp.float32) * (-math.log(10000.0) / half_width))
    angles = places * rates[None, :]
    return jnp.concatenate([jnp.sin(angles), jnp.cos(angles)], 1)


def layer_norm(stream, gain_vec, bias_vec):
    average = jnp.mean(stream, -1, keepdims=True)
    centred = stream - average
    spread = jnp.mean(centred * centred, -1, keepdims=True)
    return centred * lax.rsqrt(spread + 1e-05) * gain_vec + bias_vec


def vector(weights_map, label):
    return weights_map[label].reshape(-1)


def adam_step(grads, moment1, moment2):
    new_first = 0.9 * moment1 + (1.0 - 0.9) * grads
    new_second = 0.95 * moment2 + (1.0 - 0.95) * grads * grads
    update = new_first / first_bias_fix / (jnp.sqrt(new_second / second_bias_fix) + 1e-08)
    return (update, new_first, new_second)


tail_terms = (
    0.05025708328,
    -0.1828833063,
    0.1690591746,
    -0.005588040603,
    0.141423544,
    0.1685436795,
    0.2078425222,
    0.2256696051,
    0.2256758619,
)


def gelu_and_slope(u):
    t = 1.0 / (1.0 + (0.4 * math.sqrt(0.5)) * jnp.abs(u))
    bell = jnp.exp(-0.5 * u * u)
    tail = 0.5 * tail_terms[0]
    for term in tail_terms[1:]:
        tail = tail * t + 0.5 * term
    tail = tail * t * bell
    below = jnp.where(u < 0, tail, 1.0 - tail)
    slope = below + u * bell * (1.0 / math.sqrt(2.0 * math.pi))
    return (u * below).astype(jnp.bfloat16), slope.astype(jnp.bfloat16)


def block_forward(stream, weights_map, prefix, heads):
    chips, tokens, width = stream.shape
    inner = heads * HD
    normed1 = layer_norm(
        stream,
        vector(weights_map, prefix + "g1"),
        vector(weights_map, prefix + "b1"),
    )
    first_in = normed1.astype(jnp.bfloat16)
    triple = jnp.einsum(
        "ctd,de->cte", first_in, weights_map[prefix + "qkv"], preferred_element_type=jnp.float32
    ).astype(jnp.bfloat16)
    query_rows = triple[:, :, :inner].reshape(chips, tokens, heads, HD)
    key_rows = triple[:, :, inner : 2 * inner].reshape(chips, tokens, heads, HD)
    value_rows = triple[:, :, 2 * inner :].reshape(chips, tokens, heads, HD)
    scores = jnp.einsum(
        "cqhe,ckhe->chqk", query_rows, key_rows, preferred_element_type=jnp.float32
    ) * HD ** (-0.5)
    topmost = jnp.max(scores, -1, keepdims=True)
    expos = jnp.exp(scores - topmost)
    totals = jnp.sum(expos, -1, keepdims=True)
    logsum = topmost + jnp.log(totals)
    probs = (expos / totals).astype(jnp.bfloat16)
    mixed = jnp.einsum("chqk,ckhe->cqhe", probs, value_rows, preferred_element_type=jnp.float32)
    mixed = mixed.reshape(chips, tokens, inner).astype(jnp.bfloat16)
    middle = (
        stream
        + jnp.einsum(
            "cti,id->ctd", mixed, weights_map[prefix + "o"], preferred_element_type=jnp.float32
        )
        + vector(weights_map, prefix + "ob")
    )
    normed2 = layer_norm(
        middle,
        vector(weights_map, prefix + "g2"),
        vector(weights_map, prefix + "b2"),
    )
    second_in = normed2.astype(jnp.bfloat16)
    hidden_pre = jnp.einsum(
        "ctd,df->ctf", second_in, weights_map[prefix + "u"], preferred_element_type=jnp.float32
    ) + vector(weights_map, prefix + "ub")
    activ, slope = lax.optimization_barrier(gelu_and_slope(hidden_pre))
    result = (
        middle
        + jnp.einsum(
            "ctf,fd->ctd", activ, weights_map[prefix + "v"], preferred_element_type=jnp.float32
        )
        + vector(weights_map, prefix + "vb")
    )
    kept = (
        stream,
        middle,
        first_in,
        query_rows,
        key_rows,
        value_rows,
        logsum,
        mixed,
        second_in,
        slope,
        activ,
    )
    return (result, kept)


def norm_backward(stream, weights_map, gain_label, bias_label, upstream):
    pull = jax.vjp(
        layer_norm, stream, vector(weights_map, gain_label), vector(weights_map, bias_label)
    )[1]
    return pull(upstream)


def mlp_backward(upstream, kept, weights_map, prefix):
    middle, second_in, slope = kept[1], kept[8], kept[9]
    grads = {}
    branch_two = upstream.astype(jnp.bfloat16)
    grads[prefix + "vb"] = jnp.sum(branch_two.astype(jnp.float32), (0, 1))
    d_activ = jnp.einsum(
        "ctd,fd->ctf", branch_two, weights_map[prefix + "v"], preferred_element_type=jnp.float32
    )
    d_hidden = (d_activ * slope.astype(jnp.float32)).astype(jnp.bfloat16)
    grads[prefix + "ub"] = jnp.sum(d_hidden.astype(jnp.float32), (0, 1))
    d_second = jnp.einsum(
        "ctf,df->ctd", d_hidden, weights_map[prefix + "u"], preferred_element_type=jnp.float32
    )
    d_middle_part, grads[prefix + "g2"], grads[prefix + "b2"] = norm_backward(
        middle, weights_map, prefix + "g2", prefix + "b2", d_second
    )
    return upstream + d_middle_part, d_hidden, grads


def hidden_gradient(kept, d_hidden):
    return jnp.einsum(
        "ctd,ctf->df", kept[8], d_hidden, preferred_element_type=jnp.float32
    ).astype(jnp.bfloat16)


def output_gradient(kept, upstream):
    return jnp.einsum(
        "ctf,ctd->fd", kept[10], upstream.astype(jnp.bfloat16), preferred_element_type=jnp.float32
    ).astype(jnp.bfloat16)


def scores_backward(d_middle, kept, weights_map, prefix, heads):
    query_rows, key_rows, value_rows, logsum = kept[3:7]
    chips, tokens, width = d_middle.shape
    branch_one = d_middle.astype(jnp.bfloat16)
    d_mixed = jnp.einsum(
        "ctd,id->cti", branch_one, weights_map[prefix + "o"], preferred_element_type=jnp.float32
    )
    d_mixed = d_mixed.astype(jnp.bfloat16).reshape(chips, tokens, heads, HD)
    scores = jnp.einsum(
        "cqhe,ckhe->chqk", query_rows, key_rows, preferred_element_type=jnp.float32
    ) * HD ** (-0.5)
    probs_full = jnp.exp(scores - logsum)
    probs_low = probs_full.astype(jnp.bfloat16)
    d_value = jnp.einsum("chqk,cqhe->ckhe", probs_low, d_mixed, preferred_element_type=jnp.float32)
    d_probs = jnp.einsum("cqhe,ckhe->chqk", d_mixed, value_rows, preferred_element_type=jnp.float32)
    row_shift = jnp.sum(d_probs * probs_full, -1, keepdims=True)
    d_scores = (probs_full * (d_probs - row_shift)).astype(jnp.bfloat16)
    return d_scores, d_value.astype(jnp.bfloat16)


def stream_backward(d_middle, d_scores, d_value, kept, weights_map, prefix, heads):
    stream, first_in, query_rows, key_rows, mixed = kept[0], kept[2], kept[3], kept[4], kept[7]
    chips, tokens, width = stream.shape
    inner = heads * HD
    grads = {}
    branch_one = d_middle.astype(jnp.bfloat16)
    grads[prefix + "ob"] = jnp.sum(branch_one.astype(jnp.float32), (0, 1))
    grads[prefix + "o"] = jnp.einsum(
        "cti,ctd->id", mixed, branch_one, preferred_element_type=jnp.float32
    ).astype(jnp.bfloat16)
    d_query = jnp.einsum(
        "chqk,ckhe->cqhe", d_scores, key_rows, preferred_element_type=jnp.float32
    ) * HD ** (-0.5)
    d_key = jnp.einsum(
        "chqk,cqhe->ckhe", d_scores, query_rows, preferred_element_type=jnp.float32
    ) * HD ** (-0.5)
    d_triple = jnp.concatenate(
        [
            d_query.reshape(chips, tokens, inner).astype(jnp.bfloat16),
            d_key.reshape(chips, tokens, inner).astype(jnp.bfloat16),
            d_value.reshape(chips, tokens, inner),
        ],
        -1,
    )
    grads[prefix + "qkv"] = jnp.einsum(
        "ctd,cte->de", first_in, d_triple, preferred_element_type=jnp.float32
    ).astype(jnp.bfloat16)
    d_first = jnp.einsum(
        "cte,de->ctd", d_triple, weights_map[prefix + "qkv"], preferred_element_type=jnp.float32
    )
    d_stream_part, grads[prefix + "g1"], grads[prefix + "b1"] = norm_backward(
        stream, weights_map, prefix + "g1", prefix + "b1", d_first
    )
    return (d_middle + d_stream_part, grads)


def per_device(patches, timeloc, visible, masked, flags, cotangent, params, moment1, moment2):
    total_rows = params.shape[0] * lax.axis_size("narrow")
    weights_map = unpack(whole_params(params), total_rows)
    chips = patches.shape[0]
    patch_ids = jnp.arange(PATCH, dtype=jnp.int32)
    chooser = visible[:, :, None] == patch_ids[None, None, :]
    choose_low = chooser.astype(jnp.bfloat16)
    choose_full = chooser.astype(jnp.float32)
    picked = jnp.einsum("cvp,cpd->cvd", choose_low, patches, preferred_element_type=jnp.float32)
    keep_meta = (1 - flags).astype(jnp.float32)
    meta_row = timeloc.astype(jnp.float32) * keep_meta[:, None]
    class_row = jnp.broadcast_to(vector(weights_map, "cls")[None, None, :], (chips, 1, DE))
    enc_in = jnp.concatenate([class_row, meta_row[:, None, :], picked], 1)
    enc_out, enc_kept = block_forward(enc_in, weights_map, "e", HE)
    patch_rows = enc_out[:, 2:, :]
    final_gain = vector(weights_map, "fg")
    final_bias = vector(weights_map, "fb")
    encoded_low = layer_norm(patch_rows, final_gain, final_bias).astype(jnp.bfloat16)
    projected = jnp.einsum(
        "cvd,de->cve", encoded_low, weights_map["proj"], preferred_element_type=jnp.float32
    ) + vector(weights_map, "pb")
    filled = jnp.einsum("cvp,cve->cpe", choose_full, projected, precision=highest)
    mask_rows = 1.0 - jnp.sum(choose_full, 1)
    dec_in = (
        filled
        + mask_rows[:, :, None] * vector(weights_map, "mask")[None, None, :]
        + position_table()[None]
    )
    dec_out, dec_kept = block_forward(dec_in, weights_map, "d", HDEC)
    tie = lax.optimization_barrier
    chunked = lax.axis_size("narrow") == 2 and lax.axis_size("wide") == 16
    half_rows = params.shape[0]
    padded = round_up(half_rows, 512)
    upper = (half_rows, half_rows + padded)
    upstream = cotangent.astype(jnp.float32)
    d_mid, d_hidden, grads = mlp_backward(upstream, dec_kept, weights_map, "d")
    grads["du"] = hidden_gradient(dec_kept, d_hidden)
    grads["dv"] = output_gradient(dec_kept, upstream)
    if chunked:
        cut = round_up(flat_rows()[0]["du"][0], 128)
        held = pack_part(grads, cut, upper[1], *upper)
        d_mid, held = tie((d_mid, held))
    attention = scores_backward(d_mid, dec_kept, weights_map, "d", HDEC)
    d_dec_in, more = stream_backward(d_mid, *attention, dec_kept, weights_map, "d", HDEC)
    grads.update(more)
    grads["mask"] = jnp.sum(mask_rows[:, :, None] * d_dec_in, (0, 1))
    d_projected = jnp.einsum("cvp,cpe->cve", choose_full, d_dec_in, precision=highest).astype(
        jnp.bfloat16
    )
    grads["pb"] = jnp.sum(d_projected.astype(jnp.float32), (0, 1))
    grads["proj"] = jnp.einsum(
        "cvd,cve->de", encoded_low, d_projected, preferred_element_type=jnp.float32
    ).astype(jnp.bfloat16)
    d_encoded = jnp.einsum(
        "cve,de->cvd", d_projected, weights_map["proj"], preferred_element_type=jnp.float32
    )
    final_pull = jax.vjp(layer_norm, patch_rows, final_gain, final_bias)[1]
    d_patch_rows, grads["fg"], grads["fb"] = final_pull(d_encoded)
    d_enc_out = jnp.concatenate([jnp.zeros((chips, 2, DE), jnp.float32), d_patch_rows], 1)
    grads["ev"] = output_gradient(enc_kept, d_enc_out)
    grads["evb"] = jnp.sum(d_enc_out.astype(jnp.bfloat16).astype(jnp.float32), (0, 1))
    if chunked:
        high = pack_part(grads, half_rows, cut, *upper, held)
        d_enc_out, high = tie((d_enc_out, high))
        high = scatter_first(narrow_sum(high))
    d_mid, d_hidden, more = mlp_backward(d_enc_out, enc_kept, weights_map, "e")
    grads.update(more)
    grads["eu"] = hidden_gradient(enc_kept, d_hidden)
    if chunked:
        cut = round_up(flat_rows()[0]["eu"][0], 128)
        held = pack_part(grads, cut, padded, 0, padded)
        d_mid, held, high = tie((d_mid, held, high))
        high = scatter_second(high)
    attention = scores_backward(d_mid, enc_kept, weights_map, "e", HE)
    if chunked:
        attention, d_mid, high = tie((attention, d_mid, high))
        high = scatter_last(high)
    d_enc_in, more = stream_backward(d_mid, *attention, enc_kept, weights_map, "e", HE)
    grads.update(more)
    grads["cls"] = jnp.sum(d_enc_in[:, 0, :], 0)
    chips_all = float(chips * lax.axis_size("wide") * lax.axis_size("narrow"))
    if chunked:
        low = pack_part(grads, 0, cut, 0, padded, held)
        d_enc_in, low, high = tie((d_enc_in, low, high))
        high = gather_first(high)
        low = scatter_first(narrow_sum(low))
    patch_grad = jnp.einsum(
        "cvp,cvd->cpd", choose_full, d_enc_in[:, 2:, :], precision=highest
    ).astype(jnp.bfloat16)
    if chunked:
        patch_grad, low, high = tie((patch_grad, low, high))
        high = gather_second(high)
        low = scatter_second(low)
        low, high = tie((low, high))
        high = gather_last(high)
        low = scatter_last(low)
        low, high = tie((low, high))
        high = joined(high)
        high = (to_owner(high, 0), high)
        low = gather_first(low)
        low, high = tie((low, high))
        low = gather_second(low)
        early = (*low, *[to_owner(v, 1) for v in low])
        *held, token = adam_rows(early, high, moment1, moment2, 0, (), chips_all)
        late = [pair[1] for pair in gather_last(low)]
        late, token = tie((late, token))
        late = (*late, *[to_owner(v, 1) for v in late])
        grad_out, update, new_moment1, new_moment2, token = adam_rows(
            late, high, moment1, moment2, 1, (*held, token), chips_all
        )
    else:
        every = flat_gradient(grads, half_rows * lax.axis_size("narrow"))
        grad_out = sum_everywhere(every, half_rows).astype(jnp.float32) / chips_all
        update, new_moment1, new_moment2 = adam_step(grad_out, moment1, moment2)
    return (dec_out.astype(jnp.bfloat16), patch_grad, grad_out, update, new_moment1, new_moment2)


def solution(mesh):
    placed = (
        P(("wide", "narrow"), None, None),
        P(("wide", "narrow"), None),
        P(("wide", "narrow"), None),
        P(("wide", "narrow"), None),
        P(("wide", "narrow")),
        P(("wide", "narrow"), None, None),
        P("narrow", None),
        P("narrow", None),
        P("narrow", None),
    )
    return jax.shard_map(
        per_device,
        mesh=mesh,
        in_specs=placed,
        out_specs=(
            P(("wide", "narrow"), None, None),
            P(("wide", "narrow"), None, None),
            P("narrow", None),
            P("narrow", None),
            P("narrow", None),
            P("narrow", None),
        ),
        check_vma=False,
    )
```

```python
import math

import jax
import jax.numpy as jnp
from jax import lax
from jax.experimental import pallas as pl
from jax.experimental.pallas import tpu as pltpu
from jax.sharding import PartitionSpec as P

DE = 768
HE = 12
HD = 64
FE = 3072
DD = 512
HDEC = 4
FD = 2048
PATCH = 256


highest = lax.Precision.HIGHEST
first_bias_fix = 0.9999734386011124
second_bias_fix = 0.994079470779666


def block_segments(prefix, width, inner, hidden):
    names = ("g1", "b1", "qkv", "o", "ob", "g2", "b2", "u", "ub", "v", "vb")
    dims = ((width,), (width,), (width, 3 * inner), (inner, width), (width,), (width,), (width,))
    dims = (*dims, (width, hidden), (hidden,), (hidden, width), (width,))
    return [(prefix + name, size) for name, size in zip(names, dims)]


def segment_list():
    ends = (("fg", (DE,)), ("fb", (DE,)), ("proj", (DE, DD)), ("pb", (DD,)), ("mask", (DD,)))
    return [
        ("cls", (DE,)),
        *block_segments("e", DE, HE * HD, FE),
        *ends,
        *block_segments("d", DD, HDEC * HD, FD),
    ]


MARGIN = 512


def flat_rows():
    table = {}
    offset = 0
    for label, dims_of in segment_list():
        rows = math.prod(dims_of) // 128
        table[label] = (offset, rows)
        offset = offset + rows
    return table, offset


def round_up(value, unit):
    return -(-value // unit) * unit


def group_list():
    firsts = ("cls", "eo", "eu", "ev", "proj", "dqkv", "du", "dv")
    groups = []
    for label, dims in segment_list():
        if label in firsts:
            groups.append([])
        if label == "dg1" or label == "db1" or groups:
            groups[-1].append(label)
    return groups


def unpack(sources, total):
    table, used = flat_rows()
    shapes = dict(segment_list())
    groups = group_list()
    spans = [(table[g[0]][0], sum(table[g[-1]])) for g in groups]
    edges = [0, *[min(round_up(high, 16), total) for low, high in spans]]
    half = total // 2
    copies = []
    for k, (low, high) in enumerate(zip(edges, edges[1:])):
        parts = [(low, high)]
        if len(sources) == 2 and low < half < high:
            parts = [(low, half), (half, high)]
        copies.append(parts)
    slots = [(k, p) for k, parts in enumerate(copies) for p in range(len(parts))]
    labels = [label for label, dims in segment_list()]
    matrices = [label for label, dims in segment_list() if len(dims) == 2]
    deepest = max(round_up(high, 16) - low // 16 * 16 for low, high in spans)

    def kernel(*refs):
        ins, rest = refs[: len(sources)], refs[len(sources) :]
        finals = dict(zip(labels, rest))
        staged, wide_rows, sems, *own, out_sems = rest[len(labels) :]
        outs = {**finals, **dict(zip(matrices, own))}

        def leave(label):
            return pltpu.make_async_copy(
                outs[label], finals[label], out_sems.at[matrices.index(label)]
            )

        def copy(slot, source, shift):
            k, p = slot
            low, high = copies[k][p]
            return pltpu.make_async_copy(
                source.at[pl.ds(low - shift, high - low)],
                staged.at[pl.ds(low, high - low)],
                sems.at[slots.index(slot)],
            )

        if len(sources) == 2:
            mine = lax.axis_index("narrow")
            for slot in slots:
                place = 0 if copies[slot[0]][slot[1]][0] < half else 1

                @pl.when(mine == place)
                def own_part(slot=slot, place=place):
                    copy(slot, ins[0], place * half).start()

                @pl.when(mine != place)
                def other_part(slot=slot, place=place):
                    copy(slot, ins[1], place * half).start()
        else:
            for slot in slots:
                copy(slot, ins[0], 0).start()
        for k, group in enumerate(groups):
            for p in range(len(copies[k])):
                copy((k, p), ins[0], copies[k][p][0]).wait()
            low, high = spans[k]
            origin = low // 16 * 16
            length = round_up(high, 16) - origin

            def widen(i, carry, origin=origin):
                spot = pl.multiple_of(i * 128, 128)
                wide_rows[pl.ds(spot, 128), :] = staged[
                    pl.ds(pl.multiple_of(origin + spot, 16), 128), :
                ].astype(jnp.float32)
                return carry

            lax.fori_loop(0, length // 128, widen, 0)
            done = length // 128 * 128
            if done < length:
                wide_rows[done:length, :] = staged[origin + done : origin + length, :].astype(
                    jnp.float32
                )
            for label in group:
                base = table[label][0] - origin
                dims, ref = shapes[label], outs[label]
                tiles = dims[-1] // 128
                if len(dims) == 1:
                    for c in range(tiles):
                        ref[:, c * 128 : (c + 1) * 128] = wide_rows[base + c : base + c + 1, :]
                    continue

                def step(i, carry, base=base, tiles=tiles, ref=ref):
                    for c in range(tiles):
                        rows = wide_rows[pl.ds(base + i * 16 * tiles + c, 16, stride=tiles), :]
                        ref[pl.ds(pl.multiple_of(i * 16, 16), 16), c * 128 : (c + 1) * 128] = (
                            rows.astype(jnp.bfloat16)
                        )
                    return carry

                lax.fori_loop(0, dims[0] // 16, step, 0)
                leave(label).start()
        for label in matrices:
            leave(label).wait()

    out_shape = [
        jax.ShapeDtypeStruct(dims, jnp.bfloat16)
        if len(dims) == 2
        else jax.ShapeDtypeStruct((1, dims[0]), jnp.float32)
        for label, dims in segment_list()
    ]
    outs = pl.pallas_call(
        kernel,
        out_shape=out_shape,
        in_specs=[pl.BlockSpec(memory_space=pl.ANY)] * len(sources),
        out_specs=[
            pl.BlockSpec(memory_space=pl.ANY if label in matrices else pltpu.VMEM)
            for label in labels
        ],
        scratch_shapes=[
            pltpu.VMEM((total, 128), jnp.bfloat16),
            pltpu.VMEM((deepest, 128), jnp.float32),
            pltpu.SemaphoreType.DMA((len(slots),)),
            *[pltpu.VMEM(shapes[label], jnp.bfloat16) for label in matrices],
            pltpu.SemaphoreType.DMA((len(matrices),)),
        ],
        compiler_params=pltpu.CompilerParams(vmem_limit_bytes=61 << 20),
        name="unpack",
    )(*sources)
    return dict(zip(labels, outs))


def pack_part(pieces, low, high, first, last, held=()):
    table, used = flat_rows()
    labels = [k for k, (off, rows) in table.items() if off < high and off + rows > low]
    arrays, places = [], []
    for k in labels:
        value = pieces[k] if pieces[k].ndim == 2 else pieces[k].reshape(1, -1)
        off, rows = table[k]
        tiles = value.shape[1] // 128
        begin, end = 0, 1
        if value.shape[0] > 1:
            begin = max(0, low - off) // (16 * tiles)
            end = -(-min(rows, high - off) // (16 * tiles))
            if 3 * (end - begin) * 16 < value.shape[0]:
                value = value[begin * 16 : end * 16]
                off, end, begin = off + begin * 16 * tiles, end - begin, 0
        arrays.append(value)
        places.append((off, begin, end))
    length = high - low
    middle = (first + last) // 2
    runs = [
        (max(low, start), min(high, end), place, start)
        for place, (start, end) in enumerate(((first, middle), (middle, last)))
        if max(low, start) < min(high, end)
    ]

    def kernel(*refs):
        ins, rest = refs[: len(labels)], refs[len(labels) + len(held) :]
        kept, sent, flat, out, sems = rest
        if used < high:
            start = max(used, low) - low + MARGIN
            flat[start : MARGIN + length, :] = jnp.zeros((MARGIN + length - start, 128), jnp.float32)
        for (off, begin, end), ref in zip(places, ins):
            tiles = ref.shape[1] // 128
            base = off - low + MARGIN
            if ref.shape[0] == 1:
                for c in range(tiles):
                    spot = base + c
                    if 0 <= spot < length + 2 * MARGIN:
                        flat[spot : spot + 1, :] = ref[:, c * 128 : (c + 1) * 128]
                continue
            block = 16 * tiles

            def step(i, carry, ref=ref, tiles=tiles, base=base, block=block):
                for c in range(tiles):
                    rows = ref[pl.ds(pl.multiple_of(i * 16, 16), 16), c * 128 : (c + 1) * 128]
                    flat[pl.ds(base + i * block + c, 16, stride=tiles), :] = rows.astype(jnp.float32)
                return carry

            lax.fori_loop(begin, end, step, 0)

        def narrow_down(i, carry):
            spot = pl.multiple_of(i * 128, 128)
            out[pl.ds(spot, 128), :] = flat[pl.ds(MARGIN + spot, 128), :].astype(jnp.bfloat16)
            return carry

        lax.fori_loop(0, length // 128, narrow_down, 0)
        mine = lax.axis_index("narrow")

        def copy(n, target):
            start, end, place, origin = runs[n]
            return pltpu.make_async_copy(
                out.at[pl.ds(start - low, end - start)],
                target.at[pl.ds(start - origin, end - start)],
                sems.at[n],
            )

        for n, (start, end, place, origin) in enumerate(runs):

            @pl.when(mine == place)
            def keep(n=n):
                copy(n, kept).start()

            @pl.when(mine != place)
            def send(n=n):
                copy(n, sent).start()

        for n in range(len(runs)):
            copy(n, kept).wait()

    anywhere = pl.BlockSpec(memory_space=pl.ANY)
    whole = pl.BlockSpec(memory_space=pltpu.VMEM)
    return pl.pallas_call(
        kernel,
        out_shape=[jax.ShapeDtypeStruct((middle - first, 128), jnp.bfloat16)] * 2,
        in_specs=[whole] * len(arrays) + [anywhere] * len(held),
        out_specs=[anywhere] * 2,
        input_output_aliases={len(arrays) + n: n for n in range(len(held))},
        scratch_shapes=[
            pltpu.VMEM((length + 2 * MARGIN, 128), jnp.float32),
            pltpu.VMEM((length, 128), jnp.bfloat16),
            pltpu.SemaphoreType.DMA((len(runs),)),
        ],
        compiler_params=pltpu.CompilerParams(vmem_limit_bytes=61 << 20),
        name=f"pack{low}",
    )(*arrays, *held)


def flat_gradient(grads, unit):
    table, used = flat_rows()
    flat = jnp.concatenate([grads[k].astype(jnp.bfloat16).reshape(-1) for k, dims in segment_list()])
    padding = (round_up(used, unit) - used) * 128
    flat = jnp.concatenate([flat, jnp.zeros((padding,), jnp.bfloat16)])
    return flat.reshape(-1, 128)


def added(first, second):
    return (first.astype(jnp.float32) + second.astype(jnp.float32)).astype(jnp.bfloat16)


def piece(value, index, rows):
    return lax.dynamic_slice_in_dim(value, index * rows, rows, 0)


class Line:
    def __init__(self, stride, size):
        self.stride, self.size, self.wide = stride, size, lax.axis_size("wide")
        self.me = (lax.axis_index("wide") // stride) % size
        self.groups = [
            [i + k * stride for k in range(size)]
            for i in range(self.wide)
            if (i // stride) % size == 0
        ]

    def swap(self, value):
        pairs = [pair for a, b in self.groups for pair in ((a, b), (b, a))]
        return lax.ppermute(value, "wide", pairs)

    def exchange(self, value):
        return lax.all_to_all(value, "wide", 0, 0, axis_index_groups=self.groups)

    def scatter(self, value):
        rows = value.shape[0] // self.size
        if self.size == 2:
            got = self.swap(piece(value, 1 - self.me, rows))
            return added(piece(value, self.me, rows), got)
        got = self.exchange(value.reshape(self.size, -1, 128)).astype(jnp.float32)
        return jnp.sum(got, 0).astype(jnp.bfloat16).reshape(rows, -1, 128)

    def gather(self, value):
        if self.size == 2:
            got = self.swap(value)
            low = self.me == 0
            return jnp.concatenate([jnp.where(low, value, got), jnp.where(low, got, value)], 0)
        copies = jnp.broadcast_to(value[None], (self.size, *value.shape))
        return self.exchange(copies).reshape(-1, *value.shape[1:])


def narrow_swap(value, step):
    count = lax.axis_size("narrow")
    return lax.ppermute(value, "narrow", [(i, (i + step) % count) for i in range(count)])


def flat3(value, places):
    return value.reshape(places, -1, 128)


def wide_lines():
    return Line(1, 2), Line(2, 2), Line(4, lax.axis_size("wide") // 4)


def staged_scatter(total):
    x, y, z = wide_lines()
    unit = lax.axis_size("wide") * 8
    most = total.shape[0] // unit * 4 // 11
    first, second = most * unit, 2 * most * unit
    a = total[:first].reshape(2, 2, z.size, -1, 128)
    b = total[first:second].reshape(2, 2, z.size, -1, 128)
    c = total[second:].reshape(z.size, 2, 2, -1, 128)
    c = z.scatter(flat3(c, z.size))
    a = x.scatter(flat3(a, 2))
    b = y.scatter(flat3(b, 2))
    a = y.scatter(flat3(a, 2))
    b = x.scatter(flat3(b, 2))
    a, b, c = lax.optimization_barrier((a, b, c))
    ab = z.scatter(jnp.concatenate([flat3(a, z.size), flat3(b, z.size)], 1))
    c = x.scatter(flat3(c, 2))
    c = y.scatter(flat3(c, 2))
    return lax.optimization_barrier((ab, c))


def staged_gather(ab, c):
    x, y, z = wide_lines()
    ab = z.gather(flat3(ab, 1))
    c = x.gather(y.gather(flat3(c, 1)))
    ab, c = lax.optimization_barrier((ab, c))
    half = ab.shape[1] // 2
    a, b = ab[:, :half], ab[:, half:]
    c = z.gather(flat3(c, 1))
    a = y.gather(flat3(a, 1)).reshape(-1, 128)
    b = x.gather(flat3(b, 1)).reshape(-1, 128)
    pieces = [x.gather(flat3(a, 1)), y.gather(flat3(b, 1)), c]
    return jnp.concatenate([v.reshape(-1, 128) for v in pieces], 0)


def join_pieces(first, second):
    pairs = (first, second)
    total = sum(2 * own.shape[0] for line, own, other in pairs)

    def kernel(own1, other1, own2, other2, out, sems):
        copies = []
        start = 0
        for (line, own, other), refs in zip(pairs, ((own1, other1), (own2, other2))):
            rows = own.shape[0]
            me = (lax.axis_index("wide") // line.stride) % 2
            for ref, place in zip(refs, (me, 1 - me)):
                spot = pl.multiple_of(start + place * rows, 8)
                target = out.at[pl.ds(spot, rows)]
                copies.append(pltpu.make_async_copy(ref, target, sems.at[len(copies)]))
            start += 2 * rows
        for copy in copies:
            copy.start()
        for copy in copies:
            copy.wait()

    return pl.pallas_call(
        kernel,
        out_shape=jax.ShapeDtypeStruct((total, 128), first[1].dtype),
        in_specs=[pl.BlockSpec(memory_space=pltpu.VMEM)] * 4,
        out_specs=pl.BlockSpec(memory_space=pl.ANY),
        scratch_shapes=[pltpu.SemaphoreType.DMA((4,))],
        cost_estimate=pl.CostEstimate(flops=0, transcendentals=0, bytes_accessed=total * 512),
        name="join",
    )(first[1], first[2], second[1], second[2])


def narrow_sum(halves):
    return added(halves[0], narrow_swap(halves[1], 1))


def sum_everywhere(value, rows):
    count = lax.axis_size("narrow")
    mine = lax.axis_index("narrow")
    total = lax.dynamic_slice_in_dim(value, mine * rows, rows, 0)
    for step in range(1, count):
        other = lax.dynamic_slice_in_dim(value, (mine + step) % count * rows, rows, 0)
        total = added(total, narrow_swap(other, step))
    unit = lax.axis_size("wide") * 16
    total = jnp.pad(total, ((0, round_up(rows, unit) - rows), (0, 0)))
    return staged_gather(*staged_scatter(total))[:rows]


def scatter_first(value):
    x, y, z = wide_lines()
    a, b = jnp.split(value, 2)
    return x.scatter(flat3(a, 2)), y.scatter(flat3(b, 2))


def scatter_second(pair):
    x, y, z = wide_lines()
    return y.scatter(flat3(pair[0], 2)), x.scatter(flat3(pair[1], 2))


def scatter_last(pair):
    z = wide_lines()[2]
    both = jnp.concatenate([flat3(v, z.size) for v in pair], 1)
    return z.scatter(both).reshape(-1, 128)


def gather_first(value):
    z = wide_lines()[2]
    value = z.gather(flat3(value, 1))
    half = value.shape[1] // 2
    return flat3(value[:, :half], 1), flat3(value[:, half:], 1)


def gather_second(pair):
    x, y, z = wide_lines()
    return y.gather(pair[0]).reshape(-1, 128), x.gather(pair[1]).reshape(-1, 128)


def gather_last(pair):
    x, y, z = wide_lines()
    a, b = pair
    return (a, x.swap(a)), (b, y.swap(b))


def joined(pairs):
    x, y, z = wide_lines()
    return join_pieces((x, *pairs[0]), (y, *pairs[1]))


def adam_rows(low, high, moment1, moment2, flip, held, chips_all):
    block = low[0].shape[0] // 2
    x, y, z = wide_lines()

    def kernel(places, low0, low1, low2, low3, high0, high1, first, second, *rest):
        grad_out, update, new_first, new_second, token = rest[len(held) :]
        i = pl.program_id(0)
        early = jnp.where(i < 2, low0[...], low1[...])
        lower = jnp.where(i < 4, early, jnp.where(i < 6, low2[...], low3[...]))
        upper = jnp.where(i < 4, high0[...], high1[...])
        grad = jnp.where(places[0] == 0, lower, upper).astype(jnp.float32) / chips_all
        grad_out[...] = grad
        update[...], new_first[...], new_second[...] = adam_step(grad, first[...], second[...])
        token[...] = jnp.zeros((8, 128), jnp.float32)

    def spot(i, places):
        part = i // 2 % 2
        return part * 4 + jnp.where(part == 0, places[1], places[2]) * 2 + i % 2

    def low_spec(n):
        return pl.BlockSpec(
            (block, 128),
            lambda i, places: (jnp.where(places[0] == 0, jnp.clip(i - 2 * n, 0, 1), 0), 0),
        )

    def high_spec(n):
        def place(i, places):
            wanted = jnp.logical_and(places[0] == 1, i // 4 == n)
            return jnp.where(wanted, spot(i, places), 0), 0

        return pl.BlockSpec((block, 128), place)

    here = pl.BlockSpec((block, 128), lambda i, places: (i // 4 * 8 + spot(i, places), 0))
    mark = pl.BlockSpec((8, 128), lambda i, places: (0, 0))
    rows = 8 * block
    places = [lax.axis_index("narrow"), x.me ^ flip, y.me ^ flip]
    places = jnp.stack([place.astype(jnp.int32) for place in places])
    in_specs = [low_spec(n) for n in range(4)] + [high_spec(n) for n in range(2)] + [here, here]
    return pl.pallas_call(
        kernel,
        out_shape=[jax.ShapeDtypeStruct(moment1.shape, jnp.float32)] * 4
        + [jax.ShapeDtypeStruct((8, 128), jnp.float32)],
        grid_spec=pltpu.PrefetchScalarGridSpec(
            num_scalar_prefetch=1,
            grid=(8,),
            in_specs=in_specs + [pl.BlockSpec(memory_space=pl.ANY)] * len(held),
            out_specs=[here] * 4 + [mark],
        ),
        input_output_aliases={9 + n: n for n in range(min(4, len(held)))},
        compiler_params=pltpu.CompilerParams(vmem_limit_bytes=40 << 20),
        cost_estimate=pl.CostEstimate(
            flops=rows * 128 * 16, transcendentals=rows * 128 * 2, bytes_accessed=rows * 128 * 26
        ),
        name=f"adam{flip}",
    )(places, *low, *high, moment1, moment2, *held)


def to_owner(value, source):
    return lax.ppermute(value, "narrow", [(source, 1 - source)])


def whole_params(params):
    low_params = params.astype(jnp.bfloat16)
    if lax.axis_size("narrow") == 2:
        return (low_params, narrow_swap(low_params, 1))
    return (lax.all_gather(low_params, "narrow", axis=0, tiled=True),)


def position_table():
    half_width = DD // 2
    places = jnp.arange(PATCH, dtype=jnp.float32)[:, None]
    rates = jnp.exp(jnp.arange(half_width, dtype=jnp.float32) * (-math.log(10000.0) / half_width))
    angles = places * rates[None, :]
    return jnp.concatenate([jnp.sin(angles), jnp.cos(angles)], 1)


def layer_norm(stream, gain_vec, bias_vec):
    average = jnp.mean(stream, -1, keepdims=True)
    centred = stream - average
    spread = jnp.mean(centred * centred, -1, keepdims=True)
    return centred * lax.rsqrt(spread + 1e-05) * gain_vec + bias_vec


def vector(weights_map, label):
    return weights_map[label].reshape(-1)


def adam_step(grads, moment1, moment2):
    new_first = 0.9 * moment1 + (1.0 - 0.9) * grads
    new_second = 0.95 * moment2 + (1.0 - 0.95) * grads * grads
    update = new_first / first_bias_fix / (jnp.sqrt(new_second / second_bias_fix) + 1e-08)
    return (update, new_first, new_second)


tail_terms = (
    0.05025708328,
    -0.1828833063,
    0.1690591746,
    -0.005588040603,
    0.141423544,
    0.1685436795,
    0.2078425222,
    0.2256696051,
    0.2256758619,
)


def gelu_and_slope(u):
    t = 1.0 / (1.0 + (0.4 * math.sqrt(0.5)) * jnp.abs(u))
    bell = jnp.exp(-0.5 * u * u)
    tail = 0.5 * tail_terms[0]
    for term in tail_terms[1:]:
        tail = tail * t + 0.5 * term
    tail = tail * t * bell
    below = jnp.where(u < 0, tail, 1.0 - tail)
    slope = below + u * bell * (1.0 / math.sqrt(2.0 * math.pi))
    return (u * below).astype(jnp.bfloat16), slope.astype(jnp.bfloat16)


def block_forward(stream, weights_map, prefix, heads):
    chips, tokens, width = stream.shape
    inner = heads * HD
    normed1 = layer_norm(
        stream,
        vector(weights_map, prefix + "g1"),
        vector(weights_map, prefix + "b1"),
    )
    first_in = normed1.astype(jnp.bfloat16)
    triple = jnp.einsum(
        "ctd,de->cte", first_in, weights_map[prefix + "qkv"], preferred_element_type=jnp.float32
    ).astype(jnp.bfloat16)
    query_rows = triple[:, :, :inner].reshape(chips, tokens, heads, HD)
    key_rows = triple[:, :, inner : 2 * inner].reshape(chips, tokens, heads, HD)
    value_rows = triple[:, :, 2 * inner :].reshape(chips, tokens, heads, HD)
    scores = jnp.einsum(
        "cqhe,ckhe->chqk", query_rows, key_rows, preferred_element_type=jnp.float32
    ) * HD ** (-0.5)
    topmost = jnp.max(scores, -1, keepdims=True)
    expos = jnp.exp(scores - topmost)
    totals = jnp.sum(expos, -1, keepdims=True)
    logsum = topmost + jnp.log(totals)
    probs = (expos / totals).astype(jnp.bfloat16)
    mixed = jnp.einsum("chqk,ckhe->cqhe", probs, value_rows, preferred_element_type=jnp.float32)
    mixed = mixed.reshape(chips, tokens, inner).astype(jnp.bfloat16)
    middle = (
        stream
        + jnp.einsum(
            "cti,id->ctd", mixed, weights_map[prefix + "o"], preferred_element_type=jnp.float32
        )
        + vector(weights_map, prefix + "ob")
    )
    normed2 = layer_norm(
        middle,
        vector(weights_map, prefix + "g2"),
        vector(weights_map, prefix + "b2"),
    )
    second_in = normed2.astype(jnp.bfloat16)
    hidden_pre = jnp.einsum(
        "ctd,df->ctf", second_in, weights_map[prefix + "u"], preferred_element_type=jnp.float32
    ) + vector(weights_map, prefix + "ub")
    activ, slope = lax.optimization_barrier(gelu_and_slope(hidden_pre))
    result = (
        middle
        + jnp.einsum(
            "ctf,fd->ctd", activ, weights_map[prefix + "v"], preferred_element_type=jnp.float32
        )
        + vector(weights_map, prefix + "vb")
    )
    kept = (
        stream,
        middle,
        first_in,
        query_rows,
        key_rows,
        value_rows,
        logsum,
        mixed,
        second_in,
        slope,
        activ,
    )
    return (result, kept)


def norm_backward(stream, weights_map, gain_label, bias_label, upstream):
    pull = jax.vjp(
        layer_norm, stream, vector(weights_map, gain_label), vector(weights_map, bias_label)
    )[1]
    return pull(upstream)


def mlp_backward(upstream, kept, weights_map, prefix):
    middle, second_in, slope = kept[1], kept[8], kept[9]
    grads = {}
    branch_two = upstream.astype(jnp.bfloat16)
    grads[prefix + "vb"] = jnp.sum(branch_two.astype(jnp.float32), (0, 1))
    d_activ = jnp.einsum(
        "ctd,fd->ctf", branch_two, weights_map[prefix + "v"], preferred_element_type=jnp.float32
    )
    d_hidden = (d_activ * slope.astype(jnp.float32)).astype(jnp.bfloat16)
    grads[prefix + "ub"] = jnp.sum(d_hidden.astype(jnp.float32), (0, 1))
    d_second = jnp.einsum(
        "ctf,df->ctd", d_hidden, weights_map[prefix + "u"], preferred_element_type=jnp.float32
    )
    d_middle_part, grads[prefix + "g2"], grads[prefix + "b2"] = norm_backward(
        middle, weights_map, prefix + "g2", prefix + "b2", d_second
    )
    return upstream + d_middle_part, d_hidden, grads


def hidden_gradient(kept, d_hidden):
    return jnp.einsum(
        "ctd,ctf->df", kept[8], d_hidden, preferred_element_type=jnp.float32
    ).astype(jnp.bfloat16)


def output_gradient(kept, upstream):
    return jnp.einsum(
        "ctf,ctd->fd", kept[10], upstream.astype(jnp.bfloat16), preferred_element_type=jnp.float32
    ).astype(jnp.bfloat16)


def scores_backward(d_middle, kept, weights_map, prefix, heads):
    query_rows, key_rows, value_rows, logsum = kept[3:7]
    chips, tokens, width = d_middle.shape
    branch_one = d_middle.astype(jnp.bfloat16)
    d_mixed = jnp.einsum(
        "ctd,id->cti", branch_one, weights_map[prefix + "o"], preferred_element_type=jnp.float32
    )
    d_mixed = d_mixed.astype(jnp.bfloat16).reshape(chips, tokens, heads, HD)
    scores = jnp.einsum(
        "cqhe,ckhe->chqk", query_rows, key_rows, preferred_element_type=jnp.float32
    ) * HD ** (-0.5)
    probs_full = jnp.exp(scores - logsum)
    probs_low = probs_full.astype(jnp.bfloat16)
    d_value = jnp.einsum("chqk,cqhe->ckhe", probs_low, d_mixed, preferred_element_type=jnp.float32)
    d_probs = jnp.einsum("cqhe,ckhe->chqk", d_mixed, value_rows, preferred_element_type=jnp.float32)
    row_shift = jnp.sum(d_probs * probs_full, -1, keepdims=True)
    d_scores = (probs_full * (d_probs - row_shift)).astype(jnp.bfloat16)
    return d_scores, d_value.astype(jnp.bfloat16)


def stream_backward(d_middle, d_scores, d_value, kept, weights_map, prefix, heads):
    stream, first_in, query_rows, key_rows, mixed = kept[0], kept[2], kept[3], kept[4], kept[7]
    chips, tokens, width = stream.shape
    inner = heads * HD
    grads = {}
    branch_one = d_middle.astype(jnp.bfloat16)
    grads[prefix + "ob"] = jnp.sum(branch_one.astype(jnp.float32), (0, 1))
    grads[prefix + "o"] = jnp.einsum(
        "cti,ctd->id", mixed, branch_one, preferred_element_type=jnp.float32
    ).astype(jnp.bfloat16)
    d_query = jnp.einsum(
        "chqk,ckhe->cqhe", d_scores, key_rows, preferred_element_type=jnp.float32
    ) * HD ** (-0.5)
    d_key = jnp.einsum(
        "chqk,cqhe->ckhe", d_scores, query_rows, preferred_element_type=jnp.float32
    ) * HD ** (-0.5)
    d_triple = jnp.concatenate(
        [
            d_query.reshape(chips, tokens, inner).astype(jnp.bfloat16),
            d_key.reshape(chips, tokens, inner).astype(jnp.bfloat16),
            d_value.reshape(chips, tokens, inner),
        ],
        -1,
    )
    grads[prefix + "qkv"] = jnp.einsum(
        "ctd,cte->de", first_in, d_triple, preferred_element_type=jnp.float32
    ).astype(jnp.bfloat16)
    d_first = jnp.einsum(
        "cte,de->ctd", d_triple, weights_map[prefix + "qkv"], preferred_element_type=jnp.float32
    )
    d_stream_part, grads[prefix + "g1"], grads[prefix + "b1"] = norm_backward(
        stream, weights_map, prefix + "g1", prefix + "b1", d_first
    )
    return (d_middle + d_stream_part, grads)


def per_device(patches, timeloc, visible, masked, flags, cotangent, params, moment1, moment2):
    total_rows = params.shape[0] * lax.axis_size("narrow")
    weights_map = unpack(whole_params(params), total_rows)
    chips = patches.shape[0]
    patch_ids = jnp.arange(PATCH, dtype=jnp.int32)
    chooser = visible[:, :, None] == patch_ids[None, None, :]
    choose_low = chooser.astype(jnp.bfloat16)
    choose_full = chooser.astype(jnp.float32)
    picked = jnp.einsum("cvp,cpd->cvd", choose_low, patches, preferred_element_type=jnp.float32)
    keep_meta = (1 - flags).astype(jnp.float32)
    meta_row = timeloc.astype(jnp.float32) * keep_meta[:, None]
    class_row = jnp.broadcast_to(vector(weights_map, "cls")[None, None, :], (chips, 1, DE))
    enc_in = jnp.concatenate([class_row, meta_row[:, None, :], picked], 1)
    enc_out, enc_kept = block_forward(enc_in, weights_map, "e", HE)
    patch_rows = enc_out[:, 2:, :]
    final_gain = vector(weights_map, "fg")
    final_bias = vector(weights_map, "fb")
    encoded_low = layer_norm(patch_rows, final_gain, final_bias).astype(jnp.bfloat16)
    projected = jnp.einsum(
        "cvd,de->cve", encoded_low, weights_map["proj"], preferred_element_type=jnp.float32
    ) + vector(weights_map, "pb")
    filled = jnp.einsum("cvp,cve->cpe", choose_full, projected, precision=highest)
    mask_rows = 1.0 - jnp.sum(choose_full, 1)
    dec_in = (
        filled
        + mask_rows[:, :, None] * vector(weights_map, "mask")[None, None, :]
        + position_table()[None]
    )
    dec_out, dec_kept = block_forward(dec_in, weights_map, "d", HDEC)
    tie = lax.optimization_barrier
    chunked = lax.axis_size("narrow") == 2 and lax.axis_size("wide") == 16
    half_rows = params.shape[0]
    padded = round_up(half_rows, 512)
    upper = (half_rows, half_rows + padded)
    upstream = cotangent.astype(jnp.float32)
    d_mid, d_hidden, grads = mlp_backward(upstream, dec_kept, weights_map, "d")
    grads["du"] = hidden_gradient(dec_kept, d_hidden)
    grads["dv"] = output_gradient(dec_kept, upstream)
    if chunked:
        cut = round_up(flat_rows()[0]["du"][0], 128)
        held = pack_part(grads, cut, upper[1], *upper)
        d_mid, held = tie((d_mid, held))
    attention = scores_backward(d_mid, dec_kept, weights_map, "d", HDEC)
    d_dec_in, more = stream_backward(d_mid, *attention, dec_kept, weights_map, "d", HDEC)
    grads.update(more)
    grads["mask"] = jnp.sum(mask_rows[:, :, None] * d_dec_in, (0, 1))
    d_projected = jnp.einsum("cvp,cpe->cve", choose_full, d_dec_in, precision=highest).astype(
        jnp.bfloat16
    )
    grads["pb"] = jnp.sum(d_projected.astype(jnp.float32), (0, 1))
    grads["proj"] = jnp.einsum(
        "cvd,cve->de", encoded_low, d_projected, preferred_element_type=jnp.float32
    ).astype(jnp.bfloat16)
    d_encoded = jnp.einsum(
        "cve,de->cvd", d_projected, weights_map["proj"], preferred_element_type=jnp.float32
    )
    final_pull = jax.vjp(layer_norm, patch_rows, final_gain, final_bias)[1]
    d_patch_rows, grads["fg"], grads["fb"] = final_pull(d_encoded)
    d_enc_out = jnp.concatenate([jnp.zeros((chips, 2, DE), jnp.float32), d_patch_rows], 1)
    grads["ev"] = output_gradient(enc_kept, d_enc_out)
    grads["evb"] = jnp.sum(d_enc_out.astype(jnp.bfloat16).astype(jnp.float32), (0, 1))
    if chunked:
        high = pack_part(grads, half_rows, cut, *upper, held)
        d_enc_out, high = tie((d_enc_out, high))
        high = scatter_first(narrow_sum(high))
    d_mid, d_hidden, more = mlp_backward(d_enc_out, enc_kept, weights_map, "e")
    grads.update(more)
    grads["eu"] = hidden_gradient(enc_kept, d_hidden)
    if chunked:
        cut = round_up(flat_rows()[0]["eu"][0], 128)
        held = pack_part(grads, cut, padded, 0, padded)
        d_mid, held, high = tie((d_mid, held, high))
        high = scatter_second(high)
    attention = scores_backward(d_mid, enc_kept, weights_map, "e", HE)
    if chunked:
        attention, d_mid, high = tie((attention, d_mid, high))
        high = scatter_last(high)
    d_enc_in, more = stream_backward(d_mid, *attention, enc_kept, weights_map, "e", HE)
    grads.update(more)
    grads["cls"] = jnp.sum(d_enc_in[:, 0, :], 0)
    chips_all = float(chips * lax.axis_size("wide") * lax.axis_size("narrow"))
    if chunked:
        low = pack_part(grads, 0, cut, 0, padded, held)
        d_enc_in, low, high = tie((d_enc_in, low, high))
        high = gather_first(high)
        low = scatter_first(narrow_sum(low))
    patch_grad = jnp.einsum(
        "cvp,cvd->cpd", choose_full, d_enc_in[:, 2:, :], precision=highest
    ).astype(jnp.bfloat16)
    if chunked:
        patch_grad, low, high = tie((patch_grad, low, high))
        low = scatter_second(low)
        low, high = tie((low, high))
        high = gather_second(high)
        low = scatter_last(low)
        low, high = tie((low, high))
        high = gather_last(high)
        low = gather_first(low)
        low, high = tie((low, high))
        high = joined(high)
        high = (to_owner(high, 0), high)
        low = gather_second(low)
        early = (*low, *[to_owner(v, 1) for v in low])
        *held, token = adam_rows(early, high, moment1, moment2, 0, (), chips_all)
        late = [pair[1] for pair in gather_last(low)]
        late, token = tie((late, token))
        late = (*late, *[to_owner(v, 1) for v in late])
        grad_out, update, new_moment1, new_moment2, token = adam_rows(
            late, high, moment1, moment2, 1, (*held, token), chips_all
        )
    else:
        every = flat_gradient(grads, half_rows * lax.axis_size("narrow"))
        grad_out = sum_everywhere(every, half_rows).astype(jnp.float32) / chips_all
        update, new_moment1, new_moment2 = adam_step(grad_out, moment1, moment2)
    return (dec_out.astype(jnp.bfloat16), patch_grad, grad_out, update, new_moment1, new_moment2)


def solution(mesh):
    placed = (
        P(("wide", "narrow"), None, None),
        P(("wide", "narrow"), None),
        P(("wide", "narrow"), None),
        P(("wide", "narrow"), None),
        P(("wide", "narrow")),
        P(("wide", "narrow"), None, None),
        P("narrow", None),
        P("narrow", None),
        P("narrow", None),
    )
    return jax.shard_map(
        per_device,
        mesh=mesh,
        in_specs=placed,
        out_specs=(
            P(("wide", "narrow"), None, None),
            P(("wide", "narrow"), None, None),
            P("narrow", None),
            P("narrow", None),
            P("narrow", None),
            P("narrow", None),
        ),
        check_vma=False,
    )
```

```python
import math

import jax
import jax.numpy as jnp
from jax import lax
from jax.experimental import pallas as pl
from jax.experimental.pallas import tpu as pltpu
from jax.sharding import PartitionSpec as P

DE = 768
HE = 12
HD = 64
FE = 3072
DD = 512
HDEC = 4
FD = 2048
PATCH = 256


highest = lax.Precision.HIGHEST
first_bias_fix = 0.9999734386011124
second_bias_fix = 0.994079470779666


def block_segments(prefix, width, inner, hidden):
    names = ("g1", "b1", "qkv", "o", "ob", "g2", "b2", "u", "ub", "v", "vb")
    dims = ((width,), (width,), (width, 3 * inner), (inner, width), (width,), (width,), (width,))
    dims = (*dims, (width, hidden), (hidden,), (hidden, width), (width,))
    return [(prefix + name, size) for name, size in zip(names, dims)]


def segment_list():
    ends = (("fg", (DE,)), ("fb", (DE,)), ("proj", (DE, DD)), ("pb", (DD,)), ("mask", (DD,)))
    return [
        ("cls", (DE,)),
        *block_segments("e", DE, HE * HD, FE),
        *ends,
        *block_segments("d", DD, HDEC * HD, FD),
    ]


MARGIN = 512


def flat_rows():
    table = {}
    offset = 0
    for label, dims_of in segment_list():
        rows = math.prod(dims_of) // 128
        table[label] = (offset, rows)
        offset = offset + rows
    return table, offset


def round_up(value, unit):
    return -(-value // unit) * unit


def group_list():
    firsts = ("cls", "eo", "eu", "ev", "proj", "dqkv", "du", "dv")
    groups = []
    for label, dims in segment_list():
        if label in firsts:
            groups.append([])
        if label == "dg1" or label == "db1" or groups:
            groups[-1].append(label)
    return groups


def unpack(sources, total):
    table, used = flat_rows()
    shapes = dict(segment_list())
    groups = group_list()
    spans = [(table[g[0]][0], sum(table[g[-1]])) for g in groups]
    edges = [0, *[min(round_up(high, 16), total) for low, high in spans]]
    half = total // 2
    copies = []
    for k, (low, high) in enumerate(zip(edges, edges[1:])):
        parts = [(low, high)]
        if len(sources) == 2 and low < half < high:
            parts = [(low, half), (half, high)]
        copies.append(parts)
    slots = [(k, p) for k, parts in enumerate(copies) for p in range(len(parts))]
    labels = [label for label, dims in segment_list()]
    matrices = [label for label, dims in segment_list() if len(dims) == 2]
    deepest = max(round_up(high, 16) - low // 16 * 16 for low, high in spans)

    def kernel(*refs):
        ins, rest = refs[: len(sources)], refs[len(sources) :]
        finals = dict(zip(labels, rest))
        staged, wide_rows, sems, *own, out_sems = rest[len(labels) :]
        outs = {**finals, **dict(zip(matrices, own))}

        def leave(label):
            return pltpu.make_async_copy(
                outs[label], finals[label], out_sems.at[matrices.index(label)]
            )

        def copy(slot, source, shift):
            k, p = slot
            low, high = copies[k][p]
            return pltpu.make_async_copy(
                source.at[pl.ds(low - shift, high - low)],
                staged.at[pl.ds(low, high - low)],
                sems.at[slots.index(slot)],
            )

        if len(sources) == 2:
            mine = lax.axis_index("narrow")
            for slot in slots:
                place = 0 if copies[slot[0]][slot[1]][0] < half else 1

                @pl.when(mine == place)
                def own_part(slot=slot, place=place):
                    copy(slot, ins[0], place * half).start()

                @pl.when(mine != place)
                def other_part(slot=slot, place=place):
                    copy(slot, ins[1], place * half).start()
        else:
            for slot in slots:
                copy(slot, ins[0], 0).start()
        for k, group in enumerate(groups):
            for p in range(len(copies[k])):
                copy((k, p), ins[0], copies[k][p][0]).wait()
            low, high = spans[k]
            origin = low // 16 * 16
            length = round_up(high, 16) - origin

            def widen(i, carry, origin=origin):
                spot = pl.multiple_of(i * 128, 128)
                wide_rows[pl.ds(spot, 128), :] = staged[
                    pl.ds(pl.multiple_of(origin + spot, 16), 128), :
                ].astype(jnp.float32)
                return carry

            lax.fori_loop(0, length // 128, widen, 0)
            done = length // 128 * 128
            if done < length:
                wide_rows[done:length, :] = staged[origin + done : origin + length, :].astype(
                    jnp.float32
                )
            for label in group:
                base = table[label][0] - origin
                dims, ref = shapes[label], outs[label]
                tiles = dims[-1] // 128
                if len(dims) == 1:
                    for c in range(tiles):
                        ref[:, c * 128 : (c + 1) * 128] = wide_rows[base + c : base + c + 1, :]
                    continue

                def step(i, carry, base=base, tiles=tiles, ref=ref):
                    for c in range(tiles):
                        rows = wide_rows[pl.ds(base + i * 16 * tiles + c, 16, stride=tiles), :]
                        ref[pl.ds(pl.multiple_of(i * 16, 16), 16), c * 128 : (c + 1) * 128] = (
                            rows.astype(jnp.bfloat16)
                        )
                    return carry

                lax.fori_loop(0, dims[0] // 16, step, 0)
                leave(label).start()
        for label in matrices:
            leave(label).wait()

    out_shape = [
        jax.ShapeDtypeStruct(dims, jnp.bfloat16)
        if len(dims) == 2
        else jax.ShapeDtypeStruct((1, dims[0]), jnp.float32)
        for label, dims in segment_list()
    ]
    outs = pl.pallas_call(
        kernel,
        out_shape=out_shape,
        in_specs=[pl.BlockSpec(memory_space=pl.ANY)] * len(sources),
        out_specs=[
            pl.BlockSpec(memory_space=pl.ANY if label in matrices else pltpu.VMEM)
            for label in labels
        ],
        scratch_shapes=[
            pltpu.VMEM((total, 128), jnp.bfloat16),
            pltpu.VMEM((deepest, 128), jnp.float32),
            pltpu.SemaphoreType.DMA((len(slots),)),
            *[pltpu.VMEM(shapes[label], jnp.bfloat16) for label in matrices],
            pltpu.SemaphoreType.DMA((len(matrices),)),
        ],
        compiler_params=pltpu.CompilerParams(vmem_limit_bytes=61 << 20),
        name="unpack",
    )(*sources)
    return dict(zip(labels, outs))


def pack_part(pieces, low, high, first, last, held=()):
    table, used = flat_rows()
    labels = [k for k, (off, rows) in table.items() if off < high and off + rows > low]
    arrays, places = [], []
    for k in labels:
        value = pieces[k] if pieces[k].ndim == 2 else pieces[k].reshape(1, -1)
        off, rows = table[k]
        tiles = value.shape[1] // 128
        begin, end = 0, 1
        if value.shape[0] > 1:
            begin = max(0, low - off) // (16 * tiles)
            end = -(-min(rows, high - off) // (16 * tiles))
            if 3 * (end - begin) * 16 < value.shape[0]:
                value = value[begin * 16 : end * 16]
                off, end, begin = off + begin * 16 * tiles, end - begin, 0
        arrays.append(value)
        places.append((off, begin, end))
    length = high - low
    middle = (first + last) // 2
    runs = [
        (max(low, start), min(high, end), place, start)
        for place, (start, end) in enumerate(((first, middle), (middle, last)))
        if max(low, start) < min(high, end)
    ]

    def kernel(*refs):
        ins, rest = refs[: len(labels)], refs[len(labels) + len(held) :]
        kept, sent, flat, out, sems = rest
        if used < high:
            start = max(used, low) - low + MARGIN
            flat[start : MARGIN + length, :] = jnp.zeros((MARGIN + length - start, 128), jnp.float32)
        for (off, begin, end), ref in zip(places, ins):
            tiles = ref.shape[1] // 128
            base = off - low + MARGIN
            if ref.shape[0] == 1:
                for c in range(tiles):
                    spot = base + c
                    if 0 <= spot < length + 2 * MARGIN:
                        flat[spot : spot + 1, :] = ref[:, c * 128 : (c + 1) * 128]
                continue
            block = 16 * tiles

            def step(i, carry, ref=ref, tiles=tiles, base=base, block=block):
                for c in range(tiles):
                    rows = ref[pl.ds(pl.multiple_of(i * 16, 16), 16), c * 128 : (c + 1) * 128]
                    flat[pl.ds(base + i * block + c, 16, stride=tiles), :] = rows.astype(jnp.float32)
                return carry

            lax.fori_loop(begin, end, step, 0)

        def narrow_down(i, carry):
            spot = pl.multiple_of(i * 128, 128)
            out[pl.ds(spot, 128), :] = flat[pl.ds(MARGIN + spot, 128), :].astype(jnp.bfloat16)
            return carry

        lax.fori_loop(0, length // 128, narrow_down, 0)
        mine = lax.axis_index("narrow")

        def copy(n, target):
            start, end, place, origin = runs[n]
            return pltpu.make_async_copy(
                out.at[pl.ds(start - low, end - start)],
                target.at[pl.ds(start - origin, end - start)],
                sems.at[n],
            )

        for n, (start, end, place, origin) in enumerate(runs):

            @pl.when(mine == place)
            def keep(n=n):
                copy(n, kept).start()

            @pl.when(mine != place)
            def send(n=n):
                copy(n, sent).start()

        for n in range(len(runs)):
            copy(n, kept).wait()

    anywhere = pl.BlockSpec(memory_space=pl.ANY)
    whole = pl.BlockSpec(memory_space=pltpu.VMEM)
    return pl.pallas_call(
        kernel,
        out_shape=[jax.ShapeDtypeStruct((middle - first, 128), jnp.bfloat16)] * 2,
        in_specs=[whole] * len(arrays) + [anywhere] * len(held),
        out_specs=[anywhere] * 2,
        input_output_aliases={len(arrays) + n: n for n in range(len(held))},
        scratch_shapes=[
            pltpu.VMEM((length + 2 * MARGIN, 128), jnp.float32),
            pltpu.VMEM((length, 128), jnp.bfloat16),
            pltpu.SemaphoreType.DMA((len(runs),)),
        ],
        compiler_params=pltpu.CompilerParams(vmem_limit_bytes=61 << 20),
        name=f"pack{low}",
    )(*arrays, *held)


def flat_gradient(grads, unit):
    table, used = flat_rows()
    flat = jnp.concatenate([grads[k].astype(jnp.bfloat16).reshape(-1) for k, dims in segment_list()])
    padding = (round_up(used, unit) - used) * 128
    flat = jnp.concatenate([flat, jnp.zeros((padding,), jnp.bfloat16)])
    return flat.reshape(-1, 128)


def added(first, second):
    return (first.astype(jnp.float32) + second.astype(jnp.float32)).astype(jnp.bfloat16)


def piece(value, index, rows):
    return lax.dynamic_slice_in_dim(value, index * rows, rows, 0)


class Line:
    def __init__(self, stride, size):
        self.stride, self.size, self.wide = stride, size, lax.axis_size("wide")
        self.me = (lax.axis_index("wide") // stride) % size
        self.groups = [
            [i + k * stride for k in range(size)]
            for i in range(self.wide)
            if (i // stride) % size == 0
        ]

    def swap(self, value):
        pairs = [pair for a, b in self.groups for pair in ((a, b), (b, a))]
        return lax.ppermute(value, "wide", pairs)

    def exchange(self, value):
        return lax.all_to_all(value, "wide", 0, 0, axis_index_groups=self.groups)

    def scatter(self, value):
        rows = value.shape[0] // self.size
        if self.size == 2:
            got = self.swap(piece(value, 1 - self.me, rows))
            return added(piece(value, self.me, rows), got)
        got = self.exchange(value.reshape(self.size, -1, 128)).astype(jnp.float32)
        return jnp.sum(got, 0).astype(jnp.bfloat16).reshape(rows, -1, 128)

    def gather(self, value):
        if self.size == 2:
            got = self.swap(value)
            low = self.me == 0
            return jnp.concatenate([jnp.where(low, value, got), jnp.where(low, got, value)], 0)
        copies = jnp.broadcast_to(value[None], (self.size, *value.shape))
        return self.exchange(copies).reshape(-1, *value.shape[1:])


def narrow_swap(value, step):
    count = lax.axis_size("narrow")
    return lax.ppermute(value, "narrow", [(i, (i + step) % count) for i in range(count)])


def flat3(value, places):
    return value.reshape(places, -1, 128)


def wide_lines():
    return Line(1, 2), Line(2, 2), Line(4, lax.axis_size("wide") // 4)


def staged_scatter(total):
    x, y, z = wide_lines()
    unit = lax.axis_size("wide") * 8
    most = total.shape[0] // unit * 4 // 11
    first, second = most * unit, 2 * most * unit
    a = total[:first].reshape(2, 2, z.size, -1, 128)
    b = total[first:second].reshape(2, 2, z.size, -1, 128)
    c = total[second:].reshape(z.size, 2, 2, -1, 128)
    c = z.scatter(flat3(c, z.size))
    a = x.scatter(flat3(a, 2))
    b = y.scatter(flat3(b, 2))
    a = y.scatter(flat3(a, 2))
    b = x.scatter(flat3(b, 2))
    a, b, c = lax.optimization_barrier((a, b, c))
    ab = z.scatter(jnp.concatenate([flat3(a, z.size), flat3(b, z.size)], 1))
    c = x.scatter(flat3(c, 2))
    c = y.scatter(flat3(c, 2))
    return lax.optimization_barrier((ab, c))


def staged_gather(ab, c):
    x, y, z = wide_lines()
    ab = z.gather(flat3(ab, 1))
    c = x.gather(y.gather(flat3(c, 1)))
    ab, c = lax.optimization_barrier((ab, c))
    half = ab.shape[1] // 2
    a, b = ab[:, :half], ab[:, half:]
    c = z.gather(flat3(c, 1))
    a = y.gather(flat3(a, 1)).reshape(-1, 128)
    b = x.gather(flat3(b, 1)).reshape(-1, 128)
    pieces = [x.gather(flat3(a, 1)), y.gather(flat3(b, 1)), c]
    return jnp.concatenate([v.reshape(-1, 128) for v in pieces], 0)


def join_pieces(first, second):
    pairs = (first, second)
    total = sum(2 * own.shape[0] for line, own, other in pairs)

    def kernel(own1, other1, own2, other2, out, sems):
        copies = []
        start = 0
        for (line, own, other), refs in zip(pairs, ((own1, other1), (own2, other2))):
            rows = own.shape[0]
            me = (lax.axis_index("wide") // line.stride) % 2
            for ref, place in zip(refs, (me, 1 - me)):
                spot = pl.multiple_of(start + place * rows, 8)
                target = out.at[pl.ds(spot, rows)]
                copies.append(pltpu.make_async_copy(ref, target, sems.at[len(copies)]))
            start += 2 * rows
        for copy in copies:
            copy.start()
        for copy in copies:
            copy.wait()

    return pl.pallas_call(
        kernel,
        out_shape=jax.ShapeDtypeStruct((total, 128), first[1].dtype),
        in_specs=[pl.BlockSpec(memory_space=pltpu.VMEM)] * 4,
        out_specs=pl.BlockSpec(memory_space=pl.ANY),
        scratch_shapes=[pltpu.SemaphoreType.DMA((4,))],
        cost_estimate=pl.CostEstimate(flops=0, transcendentals=0, bytes_accessed=total * 512),
        name="join",
    )(first[1], first[2], second[1], second[2])


def narrow_sum(halves):
    return added(halves[0], narrow_swap(halves[1], 1))


def sum_everywhere(value, rows):
    count = lax.axis_size("narrow")
    mine = lax.axis_index("narrow")
    total = lax.dynamic_slice_in_dim(value, mine * rows, rows, 0)
    for step in range(1, count):
        other = lax.dynamic_slice_in_dim(value, (mine + step) % count * rows, rows, 0)
        total = added(total, narrow_swap(other, step))
    unit = lax.axis_size("wide") * 16
    total = jnp.pad(total, ((0, round_up(rows, unit) - rows), (0, 0)))
    return staged_gather(*staged_scatter(total))[:rows]


def scatter_first(value):
    x, y, z = wide_lines()
    a, b = jnp.split(value, 2)
    return x.scatter(flat3(a, 2)), y.scatter(flat3(b, 2))


def scatter_second(pair):
    x, y, z = wide_lines()
    return y.scatter(flat3(pair[0], 2)), x.scatter(flat3(pair[1], 2))


def scatter_last(pair):
    z = wide_lines()[2]
    both = jnp.concatenate([flat3(v, z.size) for v in pair], 1)
    return z.scatter(both).reshape(-1, 128)


def gather_first(value):
    z = wide_lines()[2]
    value = z.gather(flat3(value, 1))
    half = value.shape[1] // 2
    return flat3(value[:, :half], 1), flat3(value[:, half:], 1)


def gather_second(pair):
    x, y, z = wide_lines()
    return y.gather(pair[0]).reshape(-1, 128), x.gather(pair[1]).reshape(-1, 128)


def gather_last(pair):
    x, y, z = wide_lines()
    a, b = pair
    return (a, x.swap(a)), (b, y.swap(b))


def joined(pairs):
    x, y, z = wide_lines()
    return join_pieces((x, *pairs[0]), (y, *pairs[1]))


def adam_rows(low, high, moment1, moment2, flip, held, chips_all):
    block = low[0].shape[0] // 2
    x, y, z = wide_lines()

    def kernel(places, low0, low1, low2, low3, high0, high1, first, second, *rest):
        grad_out, update, new_first, new_second, token = rest[len(held) :]
        i = pl.program_id(0)
        early = jnp.where(i < 2, low0[...], low1[...])
        lower = jnp.where(i < 4, early, jnp.where(i < 6, low2[...], low3[...]))
        upper = jnp.where(i < 4, high0[...], high1[...])
        grad = jnp.where(places[0] == 0, lower, upper).astype(jnp.float32) / chips_all
        grad_out[...] = grad
        update[...], new_first[...], new_second[...] = adam_step(grad, first[...], second[...])
        token[...] = jnp.zeros((8, 128), jnp.float32)

    def spot(i, places):
        part = i // 2 % 2
        return part * 4 + jnp.where(part == 0, places[1], places[2]) * 2 + i % 2

    def low_spec(n):
        return pl.BlockSpec(
            (block, 128),
            lambda i, places: (jnp.where(places[0] == 0, jnp.clip(i - 2 * n, 0, 1), 0), 0),
        )

    def high_spec(n):
        def place(i, places):
            wanted = jnp.logical_and(places[0] == 1, i // 4 == n)
            return jnp.where(wanted, spot(i, places), 0), 0

        return pl.BlockSpec((block, 128), place)

    here = pl.BlockSpec((block, 128), lambda i, places: (i // 4 * 8 + spot(i, places), 0))
    mark = pl.BlockSpec((8, 128), lambda i, places: (0, 0))
    rows = 8 * block
    places = [lax.axis_index("narrow"), x.me ^ flip, y.me ^ flip]
    places = jnp.stack([place.astype(jnp.int32) for place in places])
    in_specs = [low_spec(n) for n in range(4)] + [high_spec(n) for n in range(2)] + [here, here]
    return pl.pallas_call(
        kernel,
        out_shape=[jax.ShapeDtypeStruct(moment1.shape, jnp.float32)] * 4
        + [jax.ShapeDtypeStruct((8, 128), jnp.float32)],
        grid_spec=pltpu.PrefetchScalarGridSpec(
            num_scalar_prefetch=1,
            grid=(8,),
            in_specs=in_specs + [pl.BlockSpec(memory_space=pl.ANY)] * len(held),
            out_specs=[here] * 4 + [mark],
        ),
        input_output_aliases={9 + n: n for n in range(min(4, len(held)))},
        compiler_params=pltpu.CompilerParams(vmem_limit_bytes=40 << 20),
        cost_estimate=pl.CostEstimate(
            flops=rows * 128 * 16, transcendentals=rows * 128 * 2, bytes_accessed=rows * 128 * 26
        ),
        name=f"adam{flip}",
    )(places, *low, *high, moment1, moment2, *held)


def to_owner(value, source):
    return lax.ppermute(value, "narrow", [(source, 1 - source)])


def whole_params(params):
    low_params = params.astype(jnp.bfloat16)
    if lax.axis_size("narrow") == 2:
        return (low_params, narrow_swap(low_params, 1))
    return (lax.all_gather(low_params, "narrow", axis=0, tiled=True),)


def position_table():
    half_width = DD // 2
    places = jnp.arange(PATCH, dtype=jnp.float32)[:, None]
    rates = jnp.exp(jnp.arange(half_width, dtype=jnp.float32) * (-math.log(10000.0) / half_width))
    angles = places * rates[None, :]
    return jnp.concatenate([jnp.sin(angles), jnp.cos(angles)], 1)


def layer_norm(stream, gain_vec, bias_vec):
    average = jnp.mean(stream, -1, keepdims=True)
    centred = stream - average
    spread = jnp.mean(centred * centred, -1, keepdims=True)
    return centred * lax.rsqrt(spread + 1e-05) * gain_vec + bias_vec


def vector(weights_map, label):
    return weights_map[label].reshape(-1)


def adam_step(grads, moment1, moment2):
    new_first = 0.9 * moment1 + (1.0 - 0.9) * grads
    new_second = 0.95 * moment2 + (1.0 - 0.95) * grads * grads
    update = new_first / first_bias_fix / (jnp.sqrt(new_second / second_bias_fix) + 1e-08)
    return (update, new_first, new_second)


tail_terms = (
    0.05025708328,
    -0.1828833063,
    0.1690591746,
    -0.005588040603,
    0.141423544,
    0.1685436795,
    0.2078425222,
    0.2256696051,
    0.2256758619,
)


def gelu_and_slope(u):
    t = 1.0 / (1.0 + (0.4 * math.sqrt(0.5)) * jnp.abs(u))
    bell = jnp.exp(-0.5 * u * u)
    tail = 0.5 * tail_terms[0]
    for term in tail_terms[1:]:
        tail = tail * t + 0.5 * term
    tail = tail * t * bell
    below = jnp.where(u < 0, tail, 1.0 - tail)
    slope = below + u * bell * (1.0 / math.sqrt(2.0 * math.pi))
    return (u * below).astype(jnp.bfloat16), slope.astype(jnp.bfloat16)


def block_forward(stream, weights_map, prefix, heads):
    chips, tokens, width = stream.shape
    inner = heads * HD
    normed1 = layer_norm(
        stream,
        vector(weights_map, prefix + "g1"),
        vector(weights_map, prefix + "b1"),
    )
    first_in = normed1.astype(jnp.bfloat16)
    triple = jnp.einsum(
        "ctd,de->cte", first_in, weights_map[prefix + "qkv"], preferred_element_type=jnp.float32
    ).astype(jnp.bfloat16)
    query_rows = triple[:, :, :inner].reshape(chips, tokens, heads, HD)
    key_rows = triple[:, :, inner : 2 * inner].reshape(chips, tokens, heads, HD)
    value_rows = triple[:, :, 2 * inner :].reshape(chips, tokens, heads, HD)
    scores = jnp.einsum(
        "cqhe,ckhe->chqk", query_rows, key_rows, preferred_element_type=jnp.float32
    ) * HD ** (-0.5)
    topmost = jnp.max(scores, -1, keepdims=True)
    expos = jnp.exp(scores - topmost)
    totals = jnp.sum(expos, -1, keepdims=True)
    logsum = topmost + jnp.log(totals)
    probs = (expos / totals).astype(jnp.bfloat16)
    mixed = jnp.einsum("chqk,ckhe->cqhe", probs, value_rows, preferred_element_type=jnp.float32)
    mixed = mixed.reshape(chips, tokens, inner).astype(jnp.bfloat16)
    middle = (
        stream
        + jnp.einsum(
            "cti,id->ctd", mixed, weights_map[prefix + "o"], preferred_element_type=jnp.float32
        )
        + vector(weights_map, prefix + "ob")
    )
    normed2 = layer_norm(
        middle,
        vector(weights_map, prefix + "g2"),
        vector(weights_map, prefix + "b2"),
    )
    second_in = normed2.astype(jnp.bfloat16)
    hidden_pre = jnp.einsum(
        "ctd,df->ctf", second_in, weights_map[prefix + "u"], preferred_element_type=jnp.float32
    ) + vector(weights_map, prefix + "ub")
    activ, slope = lax.optimization_barrier(gelu_and_slope(hidden_pre))
    result = (
        middle
        + jnp.einsum(
            "ctf,fd->ctd", activ, weights_map[prefix + "v"], preferred_element_type=jnp.float32
        )
        + vector(weights_map, prefix + "vb")
    )
    kept = (
        stream,
        middle,
        first_in,
        query_rows,
        key_rows,
        value_rows,
        logsum,
        mixed,
        second_in,
        slope,
        activ,
    )
    return (result, kept)


def norm_backward(stream, weights_map, gain_label, bias_label, upstream):
    pull = jax.vjp(
        layer_norm, stream, vector(weights_map, gain_label), vector(weights_map, bias_label)
    )[1]
    return pull(upstream)


def mlp_backward(upstream, kept, weights_map, prefix):
    middle, second_in, slope = kept[1], kept[8], kept[9]
    grads = {}
    branch_two = upstream.astype(jnp.bfloat16)
    grads[prefix + "vb"] = jnp.sum(branch_two.astype(jnp.float32), (0, 1))
    d_activ = jnp.einsum(
        "ctd,fd->ctf", branch_two, weights_map[prefix + "v"], preferred_element_type=jnp.float32
    )
    d_hidden = (d_activ * slope.astype(jnp.float32)).astype(jnp.bfloat16)
    grads[prefix + "ub"] = jnp.sum(d_hidden.astype(jnp.float32), (0, 1))
    d_second = jnp.einsum(
        "ctf,df->ctd", d_hidden, weights_map[prefix + "u"], preferred_element_type=jnp.float32
    )
    d_middle_part, grads[prefix + "g2"], grads[prefix + "b2"] = norm_backward(
        middle, weights_map, prefix + "g2", prefix + "b2", d_second
    )
    return upstream + d_middle_part, d_hidden, grads


def hidden_gradient(kept, d_hidden):
    return jnp.einsum(
        "ctd,ctf->df", kept[8], d_hidden, preferred_element_type=jnp.float32
    ).astype(jnp.bfloat16)


def output_gradient(kept, upstream):
    return jnp.einsum(
        "ctf,ctd->fd", kept[10], upstream.astype(jnp.bfloat16), preferred_element_type=jnp.float32
    ).astype(jnp.bfloat16)


def scores_backward(d_middle, kept, weights_map, prefix, heads):
    query_rows, key_rows, value_rows, logsum = kept[3:7]
    chips, tokens, width = d_middle.shape
    branch_one = d_middle.astype(jnp.bfloat16)
    d_mixed = jnp.einsum(
        "ctd,id->cti", branch_one, weights_map[prefix + "o"], preferred_element_type=jnp.float32
    )
    d_mixed = d_mixed.astype(jnp.bfloat16).reshape(chips, tokens, heads, HD)
    scores = jnp.einsum(
        "cqhe,ckhe->chqk", query_rows, key_rows, preferred_element_type=jnp.float32
    ) * HD ** (-0.5)
    probs_full = jnp.exp(scores - logsum)
    probs_low = probs_full.astype(jnp.bfloat16)
    d_value = jnp.einsum("chqk,cqhe->ckhe", probs_low, d_mixed, preferred_element_type=jnp.float32)
    d_probs = jnp.einsum("cqhe,ckhe->chqk", d_mixed, value_rows, preferred_element_type=jnp.float32)
    row_shift = jnp.sum(d_probs * probs_full, -1, keepdims=True)
    d_scores = (probs_full * (d_probs - row_shift)).astype(jnp.bfloat16)
    return d_scores, d_value.astype(jnp.bfloat16)


def stream_backward(d_middle, d_scores, d_value, kept, weights_map, prefix, heads):
    stream, first_in, query_rows, key_rows, mixed = kept[0], kept[2], kept[3], kept[4], kept[7]
    chips, tokens, width = stream.shape
    inner = heads * HD
    grads = {}
    branch_one = d_middle.astype(jnp.bfloat16)
    grads[prefix + "ob"] = jnp.sum(branch_one.astype(jnp.float32), (0, 1))
    grads[prefix + "o"] = jnp.einsum(
        "cti,ctd->id", mixed, branch_one, preferred_element_type=jnp.float32
    ).astype(jnp.bfloat16)
    d_query = jnp.einsum(
        "chqk,ckhe->cqhe", d_scores, key_rows, preferred_element_type=jnp.float32
    ) * HD ** (-0.5)
    d_key = jnp.einsum(
        "chqk,cqhe->ckhe", d_scores, query_rows, preferred_element_type=jnp.float32
    ) * HD ** (-0.5)
    d_triple = jnp.concatenate(
        [
            d_query.reshape(chips, tokens, inner).astype(jnp.bfloat16),
            d_key.reshape(chips, tokens, inner).astype(jnp.bfloat16),
            d_value.reshape(chips, tokens, inner),
        ],
        -1,
    )
    grads[prefix + "qkv"] = jnp.einsum(
        "ctd,cte->de", first_in, d_triple, preferred_element_type=jnp.float32
    ).astype(jnp.bfloat16)
    d_first = jnp.einsum(
        "cte,de->ctd", d_triple, weights_map[prefix + "qkv"], preferred_element_type=jnp.float32
    )
    d_stream_part, grads[prefix + "g1"], grads[prefix + "b1"] = norm_backward(
        stream, weights_map, prefix + "g1", prefix + "b1", d_first
    )
    return (d_middle + d_stream_part, grads)


def per_device(patches, timeloc, visible, masked, flags, cotangent, params, moment1, moment2):
    total_rows = params.shape[0] * lax.axis_size("narrow")
    weights_map = unpack(whole_params(params), total_rows)
    chips = patches.shape[0]
    patch_ids = jnp.arange(PATCH, dtype=jnp.int32)
    chooser = visible[:, :, None] == patch_ids[None, None, :]
    choose_low = chooser.astype(jnp.bfloat16)
    choose_full = chooser.astype(jnp.float32)
    picked = jnp.einsum("cvp,cpd->cvd", choose_low, patches, preferred_element_type=jnp.float32)
    keep_meta = (1 - flags).astype(jnp.float32)
    meta_row = timeloc.astype(jnp.float32) * keep_meta[:, None]
    class_row = jnp.broadcast_to(vector(weights_map, "cls")[None, None, :], (chips, 1, DE))
    enc_in = jnp.concatenate([class_row, meta_row[:, None, :], picked], 1)
    enc_out, enc_kept = block_forward(enc_in, weights_map, "e", HE)
    patch_rows = enc_out[:, 2:, :]
    final_gain = vector(weights_map, "fg")
    final_bias = vector(weights_map, "fb")
    encoded_low = layer_norm(patch_rows, final_gain, final_bias).astype(jnp.bfloat16)
    projected = jnp.einsum(
        "cvd,de->cve", encoded_low, weights_map["proj"], preferred_element_type=jnp.float32
    ) + vector(weights_map, "pb")
    filled = jnp.einsum("cvp,cve->cpe", choose_full, projected, precision=highest)
    mask_rows = 1.0 - jnp.sum(choose_full, 1)
    dec_in = (
        filled
        + mask_rows[:, :, None] * vector(weights_map, "mask")[None, None, :]
        + position_table()[None]
    )
    dec_out, dec_kept = block_forward(dec_in, weights_map, "d", HDEC)
    tie = lax.optimization_barrier
    chunked = lax.axis_size("narrow") == 2 and lax.axis_size("wide") == 16
    half_rows = params.shape[0]
    padded = round_up(half_rows, 512)
    upper = (half_rows, half_rows + padded)
    upstream = cotangent.astype(jnp.float32)
    d_mid, d_hidden, grads = mlp_backward(upstream, dec_kept, weights_map, "d")
    grads["du"] = hidden_gradient(dec_kept, d_hidden)
    grads["dv"] = output_gradient(dec_kept, upstream)
    if chunked:
        cut = round_up(flat_rows()[0]["du"][0], 128)
        held = pack_part(grads, cut, upper[1], *upper)
        d_mid, held = tie((d_mid, held))
    attention = scores_backward(d_mid, dec_kept, weights_map, "d", HDEC)
    d_dec_in, more = stream_backward(d_mid, *attention, dec_kept, weights_map, "d", HDEC)
    grads.update(more)
    grads["mask"] = jnp.sum(mask_rows[:, :, None] * d_dec_in, (0, 1))
    d_projected = jnp.einsum("cvp,cpe->cve", choose_full, d_dec_in, precision=highest).astype(
        jnp.bfloat16
    )
    grads["pb"] = jnp.sum(d_projected.astype(jnp.float32), (0, 1))
    grads["proj"] = jnp.einsum(
        "cvd,cve->de", encoded_low, d_projected, preferred_element_type=jnp.float32
    ).astype(jnp.bfloat16)
    d_encoded = jnp.einsum(
        "cve,de->cvd", d_projected, weights_map["proj"], preferred_element_type=jnp.float32
    )
    final_pull = jax.vjp(layer_norm, patch_rows, final_gain, final_bias)[1]
    d_patch_rows, grads["fg"], grads["fb"] = final_pull(d_encoded)
    d_enc_out = jnp.concatenate([jnp.zeros((chips, 2, DE), jnp.float32), d_patch_rows], 1)
    grads["ev"] = output_gradient(enc_kept, d_enc_out)
    grads["evb"] = jnp.sum(d_enc_out.astype(jnp.bfloat16).astype(jnp.float32), (0, 1))
    if chunked:
        high = pack_part(grads, half_rows, cut, *upper, held)
        d_enc_out, high = tie((d_enc_out, high))
        high = scatter_first(narrow_sum(high))
    d_mid, d_hidden, more = mlp_backward(d_enc_out, enc_kept, weights_map, "e")
    grads.update(more)
    grads["eu"] = hidden_gradient(enc_kept, d_hidden)
    if chunked:
        cut = round_up(flat_rows()[0]["eu"][0], 128)
        held = pack_part(grads, cut, padded, 0, padded)
        d_mid, held, high = tie((d_mid, held, high))
        high = scatter_second(high)
    attention = scores_backward(d_mid, enc_kept, weights_map, "e", HE)
    if chunked:
        attention, d_mid, high = tie((attention, d_mid, high))
        high = scatter_last(high)
    d_enc_in, more = stream_backward(d_mid, *attention, enc_kept, weights_map, "e", HE)
    grads.update(more)
    grads["cls"] = jnp.sum(d_enc_in[:, 0, :], 0)
    chips_all = float(chips * lax.axis_size("wide") * lax.axis_size("narrow"))
    if chunked:
        low = pack_part(grads, 0, cut, 0, padded, held)
        d_enc_in, low, high = tie((d_enc_in, low, high))
        high = gather_first(high)
        low = scatter_first(narrow_sum(low))
    patch_grad = jnp.einsum(
        "cvp,cvd->cpd", choose_full, d_enc_in[:, 2:, :], precision=highest
    ).astype(jnp.bfloat16)
    if chunked:
        patch_grad, low, high = tie((patch_grad, low, high))
        low = scatter_second(low)
        low, high = tie((low, high))
        high = gather_second(high)
        low = scatter_last(low)
        low, high = tie((low, high))
        high = joined(gather_last(high))
        low = gather_first(low)
        low, high = tie((low, high))
        high = (to_owner(high, 0), high)
        low = gather_second(low)
        early = (*low, *[to_owner(v, 1) for v in low])
        *held, token = adam_rows(early, high, moment1, moment2, 0, (), chips_all)
        late = [pair[1] for pair in gather_last(low)]
        late, token = tie((late, token))
        late = (*late, *[to_owner(v, 1) for v in late])
        grad_out, update, new_moment1, new_moment2, token = adam_rows(
            late, high, moment1, moment2, 1, (*held, token), chips_all
        )
    else:
        every = flat_gradient(grads, half_rows * lax.axis_size("narrow"))
        grad_out = sum_everywhere(every, half_rows).astype(jnp.float32) / chips_all
        update, new_moment1, new_moment2 = adam_step(grad_out, moment1, moment2)
    return (dec_out.astype(jnp.bfloat16), patch_grad, grad_out, update, new_moment1, new_moment2)


def solution(mesh):
    placed = (
        P(("wide", "narrow"), None, None),
        P(("wide", "narrow"), None),
        P(("wide", "narrow"), None),
        P(("wide", "narrow"), None),
        P(("wide", "narrow")),
        P(("wide", "narrow"), None, None),
        P("narrow", None),
        P("narrow", None),
        P("narrow", None),
    )
    return jax.shard_map(
        per_device,
        mesh=mesh,
        in_specs=placed,
        out_specs=(
            P(("wide", "narrow"), None, None),
            P(("wide", "narrow"), None, None),
            P("narrow", None),
            P("narrow", None),
            P("narrow", None),
            P("narrow", None),
        ),
        check_vma=False,
    )
```
